32 devices in a mesh: region: 4 (over y, x), tile: 8 (over z, core).
Axes of the slice: x: 2, y: 2, z: 4, core: 2. Of those that a mesh axis runs over, the one named last changes fastest.
Arguments:
- right_side: float32 [16, 32, 32, 256], P('region', 'tile'), may hold values from -20 to 20
- coords: float32 [16, 32, 2, 256], P('region', 'tile'), may hold values from 0 to 1
- pair_list: int32 [8, 16, 32], P(None, 'region', 'tile'), may hold values from 0 to 1, as said below
Outputs:
- solution: float32 [16, 32, 32, 256], P('region', 'tile')
- residual: float32 [16, 32, 32, 256], P('region', 'tile')
The draws below stay inside these ranges and needn't reach their ends.
Inputs may be any that keep to these rules, and one draw needn't show every extreme that they name: pair_list[k + 4] at a block equals pair_list[k] at its neighbour in direction k + 4, for k < 4; a direction that leaves the grid of 16 x 32 blocks is 0.
All inputs are finite; a program needn't handle non-finite values.
Results may differ from the reference program's by a relative error of at most 0.0003.
Values sent between devices are 32-bit elements; how exact they have to be, the bound alone decides.
No kernel may reach another device: no remote copies, remote signals or barrier semaphores. Data moves between devices by JAX's collectives and lax.ppermute only.
A program may use at most 64 MiB of HBM per device.

```python
import jax
import jax.numpy as jnp
from jax import lax

BS = 256
NRHS = 32
ITERS = 2
NXC = 16
NYC = 32


FORWARD_OFFSETS = ((0, 1), (1, 0), (1, 1), (1, -1))


def draw_right_side(key, part):
    key_one = jax.random.fold_in(key, 0)
    rise_x = jnp.arange(NXC, dtype=jnp.float32) / NXC
    rise_y = jnp.arange(NYC, dtype=jnp.float32) / NYC
    growth = jnp.exp(0.5 * jnp.log(3.0) * (rise_x[:, None] + rise_y[None, :]))[:, :, None, None]
    values = jax.random.normal(key_one, (NXC, NYC, NRHS, BS), jnp.float32) * growth
    return jnp.clip(values, -20.0, 20.0)


def draw_coords(key, part):
    sampled = jax.random.uniform(jax.random.fold_in(key, 29), (NXC, NYC, 2, BS), jnp.float32, -1.0, 1.0)
    pushed = jnp.sign(sampled) * jnp.abs(sampled) ** 0.25
    return jnp.clip(0.5 + 0.5 * pushed, 0.0, 1.0)


def draw_pair_list(key, part):
    hot_key, pick_key = jax.random.split(jax.random.fold_in(key, 17))
    coarse = jax.random.randint(hot_key, (NXC // 4 + 1, NYC // 4 + 1), 0, 8)
    hot_mask = jnp.repeat(jnp.repeat(coarse, 4, axis=0), 4, axis=1)[:NXC, :NYC] == 0
    cut_level = jnp.where(hot_mask, 16, 3)
    rolled = jax.random.randint(pick_key, (4, NXC, NYC), 0, 16)
    row_ids = jnp.arange(NXC, dtype=jnp.int32)[:, None]
    col_ids = jnp.arange(NYC, dtype=jnp.int32)[None, :]
    forward = []
    backward = []
    for direction_at in range(4):
        shift_a, shift_b = FORWARD_OFFSETS[direction_at]
        inside = (row_ids + shift_a < NXC) & (col_ids + shift_b >= 0) & (col_ids + shift_b < NYC)
        listed = ((rolled[direction_at] < cut_level) & inside).astype(jnp.int32)
        forward.append(listed)
        padded = jnp.pad(listed, ((1, 1), (1, 1)))
        backward.append(padded[1 - shift_a:1 - shift_a + NXC, 1 - shift_b:1 - shift_b + NYC])
    return jnp.stack(forward + backward).astype(jnp.int32)


def setup_inputs(seed: int = 0) -> dict:
    key_list = jax.random.split(jax.random.key(seed), 4)
    return {
        "right_side": draw_right_side(jax.random.fold_in(key_list[3], 71), 0),
        "coords": draw_coords(jax.random.fold_in(key_list[3], 71), 0),
        "pair_list": draw_pair_list(jax.random.fold_in(key_list[3], 71), 0),
    }


LENGTH_SCALE = 0.2
TAPER_RANGE = 0.5
NUGGET = 3.0
OFFSETS = ((0, 1), (1, 0), (1, 1), (1, -1), (0, -1), (-1, 0), (-1, -1), (-1, 1))

def kernel_tile(own_pts, other_pts, shift_a, shift_b):
    gap_x = other_pts[..., 0, None, :] + shift_a - own_pts[..., 0, :, None]
    gap_y = other_pts[..., 1, None, :] + shift_b - own_pts[..., 1, :, None]
    distance = jnp.sqrt(gap_x * gap_x + gap_y * gap_y)
    scaled = jnp.minimum(distance / TAPER_RANGE, 1.0)
    tapered = (1.0 - scaled) ** 4 * (4.0 * scaled + 1.0)
    return jnp.exp(-distance / LENGTH_SCALE) * tapered

def operate(vector, coords, pair_list):
    row_count, col_count = (vector.shape[0], vector.shape[1])
    padded = jnp.pad(vector, ((1, 1), (1, 1), (0, 0), (0, 0)))
    padded_pts = jnp.pad(coords, ((1, 1), (1, 1), (0, 0), (0, 0)))
    zero_idx = jnp.zeros((), jnp.int32)

    def one_block(position):
        position = position.astype(jnp.int32)
        row_at = (position // col_count).astype(jnp.int32)
        col_at = (position % col_count).astype(jnp.int32)
        own_row = (row_at + 1).astype(jnp.int32)
        own_col = (col_at + 1).astype(jnp.int32)
        own_pts = lax.dynamic_slice(padded_pts, (own_row, own_col, zero_idx, zero_idx), (1, 1, 2, BS))[0, 0]
        own_values = lax.dynamic_slice(padded, (own_row, own_col, zero_idx, zero_idx), (1, 1, NRHS, BS))[0, 0]
        self_tile = kernel_tile(own_pts, own_pts, 0.0, 0.0)
        summed = NUGGET * own_values + jnp.dot(own_values, self_tile.T, precision=lax.Precision.HIGHEST)
        for direction_at in range(8):
            shift_a, shift_b = OFFSETS[direction_at]
            is_listed = pair_list[direction_at, row_at, col_at]
            other_row = (own_row + shift_a).astype(jnp.int32)
            other_col = (own_col + shift_b).astype(jnp.int32)
            other_pts = lax.dynamic_slice(padded_pts, (other_row, other_col, zero_idx, zero_idx), (1, 1, 2, BS))[0, 0]
            values = lax.dynamic_slice(padded, (other_row, other_col, zero_idx, zero_idx), (1, 1, NRHS, BS))[0, 0]

            def listed_term(other_pts=other_pts, values=values, shift_a=shift_a, shift_b=shift_b):
                cov_tile = kernel_tile(own_pts, other_pts, float(shift_a), float(shift_b))
                return jnp.dot(values, cov_tile.T, precision=lax.Precision.HIGHEST)

            def no_term(own_values=own_values):
                return jnp.zeros_like(own_values)
            summed = summed + lax.cond(is_listed > 0, listed_term, no_term)
        return summed
    result = lax.map(one_block, jnp.arange(row_count * col_count, dtype=jnp.int32))
    return result.reshape(row_count, col_count, NRHS, BS)

def inner_sum(left, right):
    return lax.optimization_barrier(jnp.sum(left * right, axis=(0, 1, 3)))

def per_rhs(values):
    return values[None, None, :, None]

def reference(right_side, coords, pair_list):
    solution = jnp.zeros_like(right_side)
    residual = right_side
    direction = right_side
    norm_now = inner_sum(residual, residual)
    for iteration in range(ITERS):
        image_field = operate(direction, coords, pair_list)
        step_len = norm_now / inner_sum(direction, image_field)
        solution = solution + per_rhs(step_len) * direction
        residual = residual - per_rhs(step_len) * image_field
        if iteration + 1 < ITERS:
            norm_next = inner_sum(residual, residual)
            direction = residual + per_rhs(norm_next / norm_now) * direction
            norm_now = norm_next
    return (solution, residual)
```

```python
import functools

import jax
import jax.numpy as jnp
from jax import lax
from jax.experimental import pallas as pl
from jax.experimental.pallas import tpu as pltpu
from jax.sharding import PartitionSpec as P

LENGTH_SCALE = 0.2
TAPER_RANGE = 0.5
NUGGET = 3.0
OFFSETS = ((0, 1), (1, 0), (1, 1), (1, -1), (0, -1), (-1, 0), (-1, -1), (-1, 1))
FACTOR = 4.0**0.2
UNIT = FACTOR / TAPER_RANGE
DECAY = -1.4426950408889634 / (LENGTH_SCALE * UNIT)
STRIP = 64
VMEM_LIMIT = 48 * 1024 * 1024


def dot_nn(a, b):
    return lax.dot_general(a, b, (((1,), (0,)), ((), ())), preferred_element_type=jnp.float32)


def dot_nt(a, b):
    return lax.dot_general(a, b, (((1,), (1,)), ((), ())), preferred_element_type=jnp.float32)


def split_hi_lo(values):
    hi = values.astype(jnp.bfloat16)
    lo = (values - hi.astype(jnp.float32)).astype(jnp.bfloat16)
    return hi, lo


def across_lanes(row, lanes):
    return jnp.transpose(jnp.broadcast_to(row, (lanes, row.shape[1])))


def make_tile(tile_ref, spread_ref, other, points_ref, own, shift_a, shift_b):
    points = tile_ref.shape[1]
    lanes = spread_ref.shape[3]
    own_x = points_ref[own, 0:1] - shift_a
    own_y = points_ref[own, 1:2] - shift_b
    for start in range(0, points, STRIP):
        rows = slice(start, start + STRIP)
        for left in range(0, points, lanes):
            cols = slice(left, left + lanes)
            gap_x = spread_ref[other, 0, rows] - own_x[:, cols]
            gap_y = spread_ref[other, 1, rows] - own_y[:, cols]
            square = jnp.maximum(gap_x * gap_x + gap_y * gap_y, 1e-30)
            dist = square * lax.rsqrt(square)
            rest = jnp.maximum(FACTOR - dist, 0.0)
            rest2 = rest * rest
            cov = (jnp.exp2(dist * DECAY) * (rest2 * rest2)) * (1.25 * FACTOR - rest)
            hi, lo = split_hi_lo(cov)
            tile_ref[0, rows, cols] = hi
            tile_ref[1, rows, cols] = lo


def product(dot, parts_ref, at, tile_ref):
    rhs = parts_ref.shape[1] // 2
    both = dot(parts_ref[at], tile_ref[0])
    cross = dot(parts_ref[at, 0:rhs], tile_ref[1])
    return both[:rhs] + both[rhs:] + cross


def store_parts(parts_ref, at, values):
    rhs = values.shape[0]
    hi, lo = split_hi_lo(values)
    parts_ref[at, 0:rhs] = hi
    parts_ref[at, rhs : 2 * rhs] = lo


def run_items(items_ref, count, tile_a, tile_b, make, use):
    tile_b[...] = jnp.zeros_like(tile_b)

    def one_turn(turn, carry):
        use(tile_b, items_ref[2 * turn])
        make(tile_a, items_ref[2 * turn + 1])
        use(tile_a, items_ref[2 * turn + 1])
        make(tile_b, items_ref[2 * turn + 2])
        return carry

    turns = (count + 1) // 2
    lax.fori_loop(0, turns, one_turn, 0)
    use(tile_b, items_ref[2 * turns])


def item_code(own, other, shift_a, shift_b):
    return own + 64 * other + 4096 * (shift_a + 1) + 16384 * (shift_b + 1)


NO_ITEM = item_code(0, 0, 2, 2)


def item_fields(code):
    own = lax.rem(code, 64)
    other = lax.rem(code // 64, 64)
    shift_a = (lax.rem(code // 4096, 4) - 1).astype(jnp.float32) * UNIT
    shift_b = (code // 16384 - 1).astype(jnp.float32) * UNIT
    return own, other, shift_a, shift_b


def list_items(items_ref, candidates, pair_ref):
    items_ref[0] = NO_ITEM
    count = jnp.int32(0)
    for k, own, code in candidates:
        items_ref[count + 1] = code
        count = count + jnp.where(pair_ref[k, own] > 0, 1, 0)
    items_ref[count + 1] = NO_ITEM
    items_ref[count + 2] = NO_ITEM
    return count


def self_kernel(v_ref, c_ref, out_ref, parts_ref, points_ref, spread_ref, tile_a, tile_b):
    blocks = v_ref.shape[0]
    lanes = spread_ref.shape[3]

    def prepare(at, carry):
        store_parts(parts_ref, at, v_ref[at])
        out_ref[at] = NUGGET * v_ref[at]
        points_ref[at] = c_ref[at] * UNIT
        for axis in range(2):
            spread_ref[at, axis] = across_lanes(points_ref[at, axis : axis + 1], lanes)
        return carry

    lax.fori_loop(0, blocks, prepare, 0)
    tile_b[...] = jnp.zeros_like(tile_b)

    def use(tile_ref, at):
        out_ref[at] += product(dot_nn, parts_ref, at, tile_ref)

    def one_turn(turn, carry):
        first = 2 * turn
        use(tile_b, jnp.maximum(first - 1, 0))
        make_tile(tile_a, spread_ref, first, points_ref, first, 0.0, 0.0)
        use(tile_a, first)
        make_tile(tile_b, spread_ref, first + 1, points_ref, first + 1, 0.0, 0.0)
        return carry

    lax.fori_loop(0, blocks // 2, one_turn, 0)
    use(tile_b, blocks - 1)


def inner_kernel(
    shape, pair_ref, v_ref, c_ref, sum_ref, out_ref, items_ref, parts_ref, points_ref, spread_ref, tile_a, tile_b
):
    rows, cols = shape
    lanes = spread_ref.shape[3]

    def prepare(at, carry):
        store_parts(parts_ref, at, v_ref[at])
        out_ref[at] = sum_ref[at]
        points_ref[at] = c_ref[at] * UNIT
        for axis in range(2):
            spread_ref[at, axis] = across_lanes(points_ref[at, axis : axis + 1], lanes)
        return carry

    lax.fori_loop(0, rows * cols, prepare, 0)
    candidates = []
    for k in range(4):
        shift_a, shift_b = OFFSETS[k]
        for a in range(rows):
            for b in range(cols):
                if 0 <= a + shift_a < rows and 0 <= b + shift_b < cols:
                    own = a * cols + b
                    other = own + shift_a * cols + shift_b
                    candidates.append((k, own, item_code(own, other, shift_a, shift_b)))
    count = list_items(items_ref, candidates, pair_ref)

    def make(tile_ref, code):
        own, other, shift_a, shift_b = item_fields(code)
        make_tile(tile_ref, spread_ref, other, points_ref, own, shift_a, shift_b)

    def use(tile_ref, code):
        own, other, _, _ = item_fields(code)
        out_ref[own] += product(dot_nn, parts_ref, other, tile_ref)
        out_ref[other] += product(dot_nt, parts_ref, own, tile_ref)

    run_items(items_ref, count, tile_a, tile_b, make, use)


def cross_kernel(shape, last, *refs):
    rows, cols = shape
    pair_ref, c_ref, sum_ref = refs[:3]
    halo_v, halo_c = refs[3:7], refs[7:11]
    refs = refs[11:]
    if last:
        v0_ref, v1_ref = refs[:2]
        out_ref, moments_ref = refs[2:4]
        refs = refs[4:]
    else:
        out_ref = refs[0]
        refs = refs[1:]
    items_ref, parts_ref, points_ref, spread_ref, tile_a, tile_b = refs
    lanes = spread_ref.shape[3]
    rhs = out_ref.shape[1]

    def prepare(at, carry):
        out_ref[at] = sum_ref[at]
        points_ref[at] = c_ref[at] * UNIT
        return carry

    lax.fori_loop(0, rows * cols, prepare, 0)

    slots = {}
    for side, length in enumerate((rows, rows, cols + 2, cols + 2)):
        for at in range(length):
            slot = len(slots)
            place = ((at, -1), (at, cols), (-1, at - 1), (rows, at - 1))[side]
            slots[place] = slot
    candidates = []
    for k in range(8):
        shift_a, shift_b = OFFSETS[k]
        for a in range(rows):
            for b in range(cols):
                place = (a + shift_a, b + shift_b)
                if place in slots:
                    own = a * cols + b
                    candidates.append((k, own, item_code(own, slots[place], shift_a, shift_b)))
    count = list_items(items_ref, candidates, pair_ref)

    start = 0
    for side, length in enumerate((rows, rows, cols + 2, cols + 2)):

        def take(at, carry, side=side, start=start):
            store_parts(parts_ref, start + at, halo_v[side][at, 0:rhs])
            for axis in range(2):
                row = halo_c[side][at, rhs + axis : rhs + axis + 1] * UNIT
                spread_ref[start + at, axis] = across_lanes(row, lanes)
            return carry

        lax.fori_loop(0, length, take, 0)
        start += length

    def make(tile_ref, code):
        own, other, shift_a, shift_b = item_fields(code)
        make_tile(tile_ref, spread_ref, other, points_ref, own, shift_a, shift_b)

    def use(tile_ref, code):
        own, other, _, _ = item_fields(code)
        out_ref[own] += product(dot_nn, parts_ref, other, tile_ref)

    run_items(items_ref, count, tile_a, tile_b, make, use)
    if last:
        zero = jnp.zeros(out_ref.shape[1:], jnp.float32)

        def gather(at, sums):
            w0, w1, w2 = v0_ref[at], v1_ref[at], out_ref[at]
            terms = (w0 * w0, w0 * w1, w1 * w1, w1 * w2)
            return tuple(s + t for s, t in zip(sums, terms))

        sums = lax.fori_loop(0, rows * cols, gather, (zero,) * 4)
        folded = [sum(s[:, left : left + lanes] for left in range(0, s.shape[1], lanes)) for s in sums]
        stacked = jnp.concatenate(folded, axis=0)
        line = jnp.sum(jnp.transpose(stacked), axis=0, keepdims=True)
        moments_ref[...] = jnp.broadcast_to(line[None], moments_ref.shape)


def final_kernel(moments_ref, v0_ref, v1_ref, v2_ref, solution_ref, residual_ref):
    rhs, points = v0_ref.shape[1:]
    line = moments_ref[0]
    for at in range(1, moments_ref.shape[0]):
        line = line + moments_ref[at]
    table = across_lanes(line, line.shape[1])
    m00, m01, m11, m12 = (table[k * rhs : (k + 1) * rhs] for k in range(4))
    a = m00 / m01
    norm = m00 - 2.0 * a * m01 + a * a * m11
    grow = 1.0 + norm / m00
    step = norm / (grow * (grow * m01 - 2.0 * a * m11) + a * a * m12)
    first = jnp.concatenate([a + step * grow] * (points // line.shape[1]), axis=1)
    second = jnp.concatenate([step * a] * (points // line.shape[1]), axis=1)

    def one(at, carry):
        w0, w1, w2 = v0_ref[at], v1_ref[at], v2_ref[at]
        solution_ref[at] = first * w0 - second * w1
        residual_ref[at] = w0 - first * w1 + second * w2
        return carry

    lax.fori_loop(0, v0_ref.shape[0], one, 0)


def passed_along(x, axis, by):
    count = lax.axis_size(axis)
    pairs = [(i, i + by) for i in range(count) if 0 <= i + by < count]
    return lax.ppermute(x, axis, pairs)


def per_device(right_side, coords, pair_list):
    rows, cols, rhs, points = right_side.shape
    blocks = rows * cols
    devices = lax.axis_size("region") * lax.axis_size("tile")
    lanes = 128
    f32 = jnp.float32
    field = jax.ShapeDtypeStruct((blocks, rhs, points), f32)
    pairs = pair_list.reshape(8, blocks)
    own_points = coords.reshape(blocks, 2, points)
    vmem = pl.BlockSpec(memory_space=pltpu.VMEM)
    smem = pl.BlockSpec(memory_space=pltpu.SMEM)
    params = pltpu.CompilerParams(vmem_limit_bytes=VMEM_LIMIT)
    tile = pltpu.VMEM((2, points, points), jnp.bfloat16)
    halo = 2 * rows + 2 * (cols + 2)

    def scratch(others, listed):
        shapes = [
            pltpu.VMEM((others, 2 * rhs, points), jnp.bfloat16),
            pltpu.VMEM((blocks, 2, points), f32),
            pltpu.VMEM((others, 2, points, lanes), f32),
            tile,
            tile,
        ]
        return ([pltpu.SMEM((listed + 3,), jnp.int32)] if listed else []) + shapes

    def cost(tiles):
        return pl.CostEstimate(
            flops=tiles * 6 * rhs * points * points,
            transcendentals=tiles * 2 * points * points,
            bytes_accessed=4 * blocks * rhs * points * 4,
        )

    def self_part(v):
        return pl.pallas_call(
            self_kernel, out_shape=field, in_specs=[vmem] * 2, out_specs=vmem,
            scratch_shapes=scratch(blocks, 0), compiler_params=params, cost_estimate=cost(blocks), name="own_blocks",
        )(v, own_points)

    def inner_part(v, summed):
        return pl.pallas_call(
            functools.partial(inner_kernel, (rows, cols)), out_shape=field, in_specs=[smem] + [vmem] * 3,
            out_specs=vmem, scratch_shapes=scratch(blocks, 4 * blocks), compiler_params=params,
            cost_estimate=cost(3 * blocks), name="inner_pairs",
        )(pairs, v, own_points, summed)

    def cross_part(summed, halo_v, halo_c, others=None):
        last = others is not None
        out_shape = (field, jax.ShapeDtypeStruct((devices, 1, 4 * rhs), f32)) if last else field
        return pl.pallas_call(
            functools.partial(cross_kernel, (rows, cols), last), out_shape=out_shape,
            in_specs=[smem] + [vmem] * (12 if last else 10), out_specs=(vmem, vmem) if last else vmem,
            scratch_shapes=scratch(halo, 8 * blocks), compiler_params=params,
            cost_estimate=cost(2 * blocks), name="cross_pairs",
        )(pairs, own_points, summed, *halo_v, *halo_c, *(others or ()))

    def apply(field_v, packed, halo_c, others=None):
        prev_col = passed_along(packed[:, cols - 1], "tile", 1)
        next_col = passed_along(packed[:, 0], "tile", -1)
        summed = self_part(field_v)
        top = jnp.concatenate([prev_col[:1], packed[0], next_col[:1]], axis=0)
        bottom = jnp.concatenate([prev_col[rows - 1 :], packed[rows - 1], next_col[rows - 1 :]], axis=0)
        prev_row = passed_along(bottom, "region", 1)
        next_row = passed_along(top, "region", -1)
        summed = inner_part(field_v, summed)
        halo_v = (prev_col, next_col, prev_row, next_row)
        return cross_part(summed, halo_v, halo_c or halo_v, others), halo_v

    w0 = right_side.reshape(blocks, rhs, points)
    w1, halo_c = apply(w0, jnp.concatenate([right_side, coords], axis=2), None)
    (w2, moments), _ = apply(w1, w1.reshape(right_side.shape), halo_c, (w0, w1))
    moments = lax.all_to_all(moments, ("region", "tile"), 0, 0)
    solution, residual = pl.pallas_call(
        final_kernel, out_shape=(field, field), in_specs=[vmem] * 4, out_specs=(vmem, vmem),
        compiler_params=params, name="final_update",
    )(moments, w0, w1, w2)
    return solution.reshape(right_side.shape), residual.reshape(right_side.shape)


def solution(mesh):
    placed = (
        P("region", "tile", None, None),
        P("region", "tile", None, None),
        P(None, "region", "tile"),
    )
    return jax.shard_map(
        per_device,
        mesh=mesh,
        in_specs=placed,
        out_specs=(P("region", "tile", None, None), P("region", "tile", None, None)),
        check_vma=False,
    )
```

```python
import functools

import jax
import jax.numpy as jnp
from jax import lax
from jax.experimental import pallas as pl
from jax.experimental.pallas import tpu as pltpu
from jax.sharding import PartitionSpec as P

LENGTH_SCALE = 0.2
TAPER_RANGE = 0.5
NUGGET = 3.0
OFFSETS = ((0, 1), (1, 0), (1, 1), (1, -1), (0, -1), (-1, 0), (-1, -1), (-1, 1))
UNIT = 1.4426950408889634 / LENGTH_SCALE
EDGE = UNIT * TAPER_RANGE
WEIGHT = 4.0 * 2.0**-EDGE / EDGE**5
STRIP = 64
VMEM_LIMIT = 10 * 1024 * 1024


def dot_nn(a, b):
    return lax.dot_general(a, b, (((1,), (0,)), ((), ())), preferred_element_type=jnp.float32)


def dot_nt(a, b):
    return lax.dot_general(a, b, (((1,), (1,)), ((), ())), preferred_element_type=jnp.float32)


def split_hi_lo(values):
    hi = values.astype(jnp.bfloat16)
    lo = (values - hi.astype(jnp.float32)).astype(jnp.bfloat16)
    return hi, lo


def across_lanes(row, lanes):
    return jnp.transpose(jnp.broadcast_to(row, (lanes, row.shape[1])))


def spread_points(spread_ref, at, points):
    tall = jnp.transpose(jnp.concatenate([points * UNIT] * 4, axis=0))
    for axis in range(2):
        spread_ref[at, axis] = jnp.broadcast_to(tall[:, axis : axis + 1], spread_ref.shape[2:])


def make_tile(tile_ref, keep_ref, slot, spread_ref, other, points_ref, own, shift_a, shift_b):
    points = tile_ref.shape[1]
    lanes = spread_ref.shape[3]
    own_x = points_ref[own, 0:1] - shift_a
    own_y = points_ref[own, 1:2] - shift_b
    for start in range(0, points, STRIP):
        rows = slice(start, start + STRIP)
        for left in range(0, points, lanes):
            cols = slice(left, left + lanes)
            gap_x = spread_ref[other, 0, rows] - own_x[:, cols]
            gap_y = spread_ref[other, 1, rows] - own_y[:, cols]
            square = jnp.maximum(gap_x * gap_x + gap_y * gap_y, 1e-30)
            rest = jnp.maximum(EDGE - square * lax.rsqrt(square), 0.0)
            rest2 = rest * rest
            cov = (jnp.exp2(rest) * (rest2 * rest2)) * (1.25 * EDGE - rest)
            for part, values in enumerate(split_hi_lo(cov)):
                tile_ref[part, rows, cols] = values
                keep_ref[slot, part, rows, cols] = values


def product(dot, parts_ref, at, high, low):
    rhs = parts_ref.shape[1] // 2
    both = dot(parts_ref[at], high)
    cross = dot(parts_ref[at, 0:rhs], low)
    return both[:rhs] + both[rhs:] + cross


def store_parts(parts_ref, at, values):
    rhs = values.shape[0]
    hi, lo = split_hi_lo(values * WEIGHT)
    parts_ref[at, 0:rhs] = hi
    parts_ref[at, rhs : 2 * rhs] = lo


def make_and_use(turns, item_at, tile_a, tile_b, make, use):
    tile_b[...] = jnp.zeros_like(tile_b)

    def one_turn(turn, carry):
        use(tile_b[0], tile_b[1], item_at(2 * turn))
        make(tile_a, 2 * turn, item_at(2 * turn + 1))
        use(tile_a[0], tile_a[1], item_at(2 * turn + 1))
        make(tile_b, 2 * turn + 1, item_at(2 * turn + 2))
        return carry

    lax.fori_loop(0, turns, one_turn, 0)
    use(tile_b[0], tile_b[1], item_at(2 * turns))


def only_use(turns, item_at, kept_ref, base, use):
    def one_turn(turn, carry):
        for half in range(2):
            slot = base + 2 * turn + half
            use(kept_ref[slot, 0], kept_ref[slot, 1], item_at(2 * turn + half + 1))
        return carry

    lax.fori_loop(0, turns, one_turn, 0)


def item_code(own, other, shift_a, shift_b):
    return own + 64 * other + 4096 * (shift_a + 1) + 16384 * (shift_b + 1)


NO_ITEM = item_code(0, 0, 2, 2)


def item_blocks(code):
    return lax.bitwise_and(code, 63), lax.bitwise_and(lax.shift_right_logical(code, 6), 63)


def item_shifts(code):
    shift_a = lax.bitwise_and(lax.shift_right_logical(code, 12), 3) - 1
    shift_b = lax.shift_right_logical(code, 14) - 1
    return shift_a.astype(jnp.float32) * UNIT, shift_b.astype(jnp.float32) * UNIT


def list_items(items_ref, candidates, pair_ref):
    items_ref[0] = NO_ITEM
    count = jnp.int32(0)
    for k, own, code in candidates:
        items_ref[count + 1] = code
        count = count + jnp.where(pair_ref[k, own] > 0, 1, 0)
    items_ref[count + 1] = NO_ITEM
    items_ref[count + 2] = NO_ITEM
    return lax.shift_right_logical(count + 1, 1)


def inner_candidates(rows, cols):
    found = []
    for k in range(4):
        shift_a, shift_b = OFFSETS[k]
        for a in range(rows):
            for b in range(cols):
                if 0 <= a + shift_a < rows and 0 <= b + shift_b < cols:
                    own = a * cols + b
                    other = own + shift_a * cols + shift_b
                    found.append((k, own, item_code(own, other, shift_a, shift_b)))
    return found


def cross_candidates(rows, cols):
    places = [(a, -1) for a in range(rows)] + [(a, cols) for a in range(rows)]
    places += [(-1, b) for b in range(-1, cols + 1)] + [(rows, b) for b in range(-1, cols + 1)]
    found = []
    for k in range(8):
        shift_a, shift_b = OFFSETS[k]
        for a in range(rows):
            for b in range(cols):
                place = (a + shift_a, b + shift_b)
                if place in places:
                    own = a * cols + b
                    found.append((k, own, item_code(own, places.index(place), shift_a, shift_b)))
    return found


def near_kernel(shape, again, pair_ref, *refs):
    blocks = shape[0] * shape[1]
    if again:
        v_ref, kept_ref, out_ref, items_ref, parts_ref = refs
    else:
        v_ref, c_ref, out_ref, kept_ref, items_ref, parts_ref, points_ref, spread_ref, tile_a, tile_b = refs

    def prepare(at, carry):
        store_parts(parts_ref, at, v_ref[at])
        out_ref[at] = NUGGET * v_ref[at]
        if not again:
            points_ref[at] = c_ref[at] * UNIT
            spread_points(spread_ref, at, c_ref[at])
        return carry

    lax.fori_loop(0, blocks, prepare, 0)
    turns = list_items(items_ref, inner_candidates(*shape), pair_ref)

    def own_item(n):
        return jnp.maximum(n - 1, 0)

    def use_own(high, low, at):
        out_ref[at] += product(dot_nn, parts_ref, at, high, low)

    def use(high, low, code):
        own, other = item_blocks(code)
        out_ref[own] += product(dot_nn, parts_ref, other, high, low)
        out_ref[other] += product(dot_nt, parts_ref, own, high, low)

    if again:
        only_use(blocks // 2, own_item, kept_ref, 0, use_own)
        only_use(turns, lambda n: items_ref[n], kept_ref, blocks, use)
        return

    def make_own(tile_ref, slot, at):
        make_tile(tile_ref, kept_ref, slot, spread_ref, at, points_ref, at, 0.0, 0.0)

    def make(tile_ref, slot, code):
        own, other = item_blocks(code)
        make_tile(tile_ref, kept_ref, blocks + slot, spread_ref, other, points_ref, own, *item_shifts(code))

    make_and_use(blocks // 2, own_item, tile_a, tile_b, make_own, use_own)
    make_and_use(turns, lambda n: items_ref[n], tile_a, tile_b, make, use)


def cross_kernel(shape, again, pair_ref, sum_ref, *refs):
    rows, cols = shape
    halo = refs[:4]
    if again:
        kept_ref, v0_ref, v1_ref, out_ref, moments_ref, items_ref, parts_ref = refs[4:]
    else:
        c_ref, out_ref, kept_ref, items_ref, parts_ref, points_ref, spread_ref, tile_a, tile_b = refs[4:]
    rhs = out_ref.shape[1]

    def prepare(at, carry):
        out_ref[at] = sum_ref[at]
        if not again:
            points_ref[at] = c_ref[at] * UNIT
        return carry

    lax.fori_loop(0, rows * cols, prepare, 0)
    turns = list_items(items_ref, cross_candidates(rows, cols), pair_ref)
    start = 0
    for side in halo:

        def take(at, carry, side=side, start=start):
            store_parts(parts_ref, start + at, side[at, 0:rhs])
            if not again:
                spread_points(spread_ref, start + at, side[at, rhs : rhs + 2])
            return carry

        lax.fori_loop(0, side.shape[0], take, 0)
        start += side.shape[0]

    def use(high, low, code):
        own, other = item_blocks(code)
        out_ref[own] += product(dot_nn, parts_ref, other, high, low)

    if not again:

        def make(tile_ref, slot, code):
            own, other = item_blocks(code)
            make_tile(tile_ref, kept_ref, slot, spread_ref, other, points_ref, own, *item_shifts(code))

        make_and_use(turns, lambda n: items_ref[n], tile_a, tile_b, make, use)
        return

    only_use(turns, lambda n: items_ref[n], kept_ref, 0, use)
    zero = jnp.zeros(out_ref.shape[1:], jnp.float32)

    def gather(at, sums):
        w0, w1, w2 = v0_ref[at], v1_ref[at], out_ref[at]
        terms = (w0 * w0, w0 * w1, w1 * w1, w1 * w2)
        return tuple(s + t for s, t in zip(sums, terms))

    sums = lax.fori_loop(0, rows * cols, gather, (zero,) * 4)
    lanes = moments_ref.shape[2]
    folded = [sum(s[:, left : left + lanes] for left in range(0, s.shape[1], lanes)) for s in sums]
    stacked = jnp.concatenate(folded, axis=0)
    line = jnp.sum(jnp.transpose(stacked), axis=0, keepdims=True)
    moments_ref[...] = jnp.broadcast_to(line[None], moments_ref.shape)


def final_kernel(moments_ref, v0_ref, v1_ref, v2_ref, solution_ref, residual_ref):
    rhs, points = v0_ref.shape[1:]
    line = moments_ref[0]
    for at in range(1, moments_ref.shape[0]):
        line = line + moments_ref[at]
    table = across_lanes(line, line.shape[1])
    m00, m01, m11, m12 = (table[k * rhs : (k + 1) * rhs] for k in range(4))
    a = m00 / m01
    norm = m00 - 2.0 * a * m01 + a * a * m11
    grow = 1.0 + norm / m00
    step = norm / (grow * (grow * m01 - 2.0 * a * m11) + a * a * m12)
    first = jnp.concatenate([a + step * grow] * (points // line.shape[1]), axis=1)
    second = jnp.concatenate([step * a] * (points // line.shape[1]), axis=1)

    def one(at, carry):
        w0, w1, w2 = v0_ref[at], v1_ref[at], v2_ref[at]
        solution_ref[at] = first * w0 - second * w1
        residual_ref[at] = w0 - first * w1 + second * w2
        return carry

    lax.fori_loop(0, v0_ref.shape[0], one, 0)


def passed_along(x, axis, by):
    count = lax.axis_size(axis)
    pairs = [(i, i + by) for i in range(count) if 0 <= i + by < count]
    return lax.ppermute(x, axis, pairs)


def per_device(right_side, coords, pair_list):
    rows, cols, rhs, points = right_side.shape
    blocks = rows * cols
    devices = lax.axis_size("region") * lax.axis_size("tile")
    lanes = 128
    f32 = jnp.float32
    halo = 2 * rows + 2 * (cols + 2)
    near_count = len(inner_candidates(rows, cols))
    cross_count = len(cross_candidates(rows, cols))
    pairs = pair_list.reshape(8, blocks)
    own_points = coords.reshape(blocks, 2, points)
    field = jax.ShapeDtypeStruct((blocks, rhs, points), f32)
    vmem = pl.BlockSpec(memory_space=pltpu.VMEM)
    smem = pl.BlockSpec(memory_space=pltpu.SMEM)

    def tiles(count):
        return jax.ShapeDtypeStruct((count, 2, points, points), jnp.bfloat16)

    def call(kernel, name, inputs, outputs, listed, others, again, count):
        scratch = [pltpu.SMEM((listed + 3,), jnp.int32), pltpu.VMEM((others, 2 * rhs, points), jnp.bfloat16)]
        if not again:
            scratch += [pltpu.VMEM((blocks, 2, points), f32), pltpu.VMEM((others, 2, points, lanes), f32)]
            scratch += [pltpu.VMEM((2, points, points), jnp.bfloat16)] * 2
        return pl.pallas_call(
            functools.partial(kernel, (rows, cols), again), out_shape=outputs,
            in_specs=[smem] + [vmem] * len(inputs), out_specs=(vmem,) * len(outputs), scratch_shapes=scratch,
            compiler_params=pltpu.CompilerParams(vmem_limit_bytes=VMEM_LIMIT), name=name,
            cost_estimate=pl.CostEstimate(
                flops=count * 6 * rhs * points * points, transcendentals=0 if again else count * 2 * points * points,
                bytes_accessed=count * 4 * points * points,
            ),
        )(pairs, *inputs)

    def exchange(packed):
        prev_col = passed_along(packed[:, cols - 1], "tile", 1)
        next_col = passed_along(packed[:, 0], "tile", -1)
        top = jnp.concatenate([prev_col[:1], packed[0], next_col[:1]], axis=0)
        bottom = jnp.concatenate([prev_col[rows - 1 :], packed[rows - 1], next_col[rows - 1 :]], axis=0)
        return prev_col, next_col, passed_along(bottom, "region", 1), passed_along(top, "region", -1)

    w0 = right_side.reshape(blocks, rhs, points)
    round_w0 = exchange(jnp.concatenate([right_side, coords], axis=2))
    part, near_tiles = call(
        near_kernel, "near_first", (w0, own_points), (field, tiles(blocks + near_count + 2)),
        near_count, blocks, False, blocks + near_count,
    )
    w1, cross_tiles = call(
        cross_kernel, "cross_first", (part, *round_w0, own_points), (field, tiles(cross_count + 2)),
        cross_count, halo, False, cross_count,
    )
    round_w1 = exchange(w1.reshape(right_side.shape))
    (part,) = call(
        near_kernel, "near_again", (w1, near_tiles), (field,), near_count, blocks, True, blocks + near_count
    )
    w2, moments = call(
        cross_kernel, "cross_again", (part, *round_w1, cross_tiles, w0, w1),
        (field, jax.ShapeDtypeStruct((devices, 1, 4 * rhs), f32)), cross_count, halo, True, cross_count,
    )
    moments = lax.all_to_all(moments, ("region", "tile"), 0, 0)
    solution, residual = pl.pallas_call(
        final_kernel, out_shape=(field, field), in_specs=[vmem] * 4, out_specs=(vmem, vmem),
        compiler_params=pltpu.CompilerParams(vmem_limit_bytes=VMEM_LIMIT), name="final_update",
    )(moments, w0, w1, w2)
    return solution.reshape(right_side.shape), residual.reshape(right_side.shape)


def solution(mesh):
    placed = (
        P("region", "tile", None, None),
        P("region", "tile", None, None),
        P(None, "region", "tile"),
    )
    return jax.shard_map(
        per_device,
        mesh=mesh,
        in_specs=placed,
        out_specs=(P("region", "tile", None, None), P("region", "tile", None, None)),
        check_vma=False,
    )
```

```python
import functools

import jax
import jax.numpy as jnp
from jax import lax
from jax.experimental import pallas as pl
from jax.experimental.pallas import tpu as pltpu
from jax.sharding import PartitionSpec as P

LENGTH_SCALE = 0.2
TAPER_RANGE = 0.5
NUGGET = 3.0
OFFSETS = ((0, 1), (1, 0), (1, 1), (1, -1), (0, -1), (-1, 0), (-1, -1), (-1, 1))
UNIT = 1.4426950408889634 / LENGTH_SCALE
EDGE = UNIT * TAPER_RANGE
WEIGHT = 4.0 * 2.0**-EDGE / EDGE**5
STRIP = 64
LONG_TURN_LOG2 = 3
VMEM_LIMIT = 10 * 1024 * 1024


def dot_nn(a, b):
    return lax.dot_general(a, b, (((1,), (0,)), ((), ())), preferred_element_type=jnp.float32)


def dot_nt(a, b):
    return lax.dot_general(a, b, (((1,), (1,)), ((), ())), preferred_element_type=jnp.float32)


def split_hi_lo(values):
    hi = values.astype(jnp.bfloat16)
    lo = (values - hi.astype(jnp.float32)).astype(jnp.bfloat16)
    return hi, lo


def across_lanes(row, lanes):
    return jnp.transpose(jnp.broadcast_to(row, (lanes, row.shape[1])))


def make_tile(tile_ref, keep_ref, slot, spread_ref, down, points_ref, along, shift_a, shift_b):
    points = tile_ref.shape[1]
    lanes = spread_ref.shape[3]
    row_x = points_ref[along, 0:1] - shift_a
    row_y = points_ref[along, 1:2] - shift_b
    for start in range(0, points, STRIP):
        rows = slice(start, start + STRIP)
        for left in range(0, points, lanes):
            cols = slice(left, left + lanes)
            gap_x = spread_ref[down, 0, rows] - row_x[:, cols]
            gap_y = spread_ref[down, 1, rows] - row_y[:, cols]
            square = jnp.maximum(gap_x * gap_x + gap_y * gap_y, 1e-30)
            rest = jnp.maximum(EDGE - square * lax.rsqrt(square), 0.0)
            rest2 = rest * rest
            cov = (jnp.exp2(rest) * (rest2 * rest2)) * (1.25 * EDGE - rest)
            for part, values in enumerate(split_hi_lo(cov)):
                tile_ref[part, rows, cols] = values
                keep_ref[slot, part, rows, cols] = values


def product(dot, parts_ref, at, high, low):
    rhs = parts_ref.shape[1] // 2
    both = dot(parts_ref[at], high)
    cross = dot(parts_ref[at, 0:rhs], low)
    return both[:rhs] + both[rhs:] + cross


def store_parts(parts_ref, at, values):
    rhs = values.shape[0]
    hi, lo = split_hi_lo(values * WEIGHT)
    parts_ref[at, 0:rhs] = hi
    parts_ref[at, rhs : 2 * rhs] = lo


def make_and_use(count, tile_a, tile_b, make, use):
    tile_b[...] = jnp.zeros_like(tile_b)
    turns = lax.shift_right_logical(count + 1, 1)

    def one_turn(turn, carry):
        first = 2 * turn
        use(tile_b[0], tile_b[1], jnp.maximum(first - 1, 0))
        make(tile_a, first)
        use(tile_a[0], tile_a[1], first)
        make(tile_b, first + 1)
        return carry

    lax.fori_loop(0, turns, one_turn, 0)
    use(tile_b[0], tile_b[1], jnp.maximum(2 * turns - 1, 0))


def only_use(count, kept_ref, base, use):
    def one_turn(start, length):
        for n in range(length):
            use(kept_ref[base + start + n, 0], kept_ref[base + start + n, 1], start + n)

    whole = lax.shift_right_logical(count, LONG_TURN_LOG2)
    lax.fori_loop(0, whole, lambda turn, c: (one_turn(turn << LONG_TURN_LOG2, 1 << LONG_TURN_LOG2), c)[1], 0)
    lax.fori_loop(whole << LONG_TURN_LOG2, count, lambda n, c: (one_turn(n, 1), c)[1], 0)


def item_code(own, other, shift_a, shift_b):
    return own + 64 * other + 4096 * (shift_a + 1) + 16384 * (shift_b + 1)


NO_ITEM = item_code(0, 0, 2, 2)


def item_blocks(code):
    return lax.bitwise_and(code, 63), lax.bitwise_and(lax.shift_right_logical(code, 6), 63)


def item_shifts(code):
    shift_a = lax.bitwise_and(lax.shift_right_logical(code, 12), 3) - 1
    shift_b = lax.shift_right_logical(code, 14) - 1
    return shift_a.astype(jnp.float32) * UNIT, shift_b.astype(jnp.float32) * UNIT


def list_items(items_ref, candidates, pair_ref):
    cols = pair_ref.shape[2]
    count = jnp.int32(0)
    for k, own, code in candidates:
        items_ref[count + 1] = code
        count = count + jnp.where(pair_ref[k, own // cols, own % cols] > 0, 1, 0)
    items_ref[0] = count
    items_ref[count + 1] = NO_ITEM


def inner_candidates(rows, cols):
    found = []
    for k in range(4):
        shift_a, shift_b = OFFSETS[k]
        for a in range(rows):
            for b in range(cols):
                if 0 <= a + shift_a < rows and 0 <= b + shift_b < cols:
                    own = a * cols + b
                    other = own + shift_a * cols + shift_b
                    found.append((k, own, item_code(own, other, shift_a, shift_b)))
    return found


def cross_candidates(rows, cols):
    places = [(a, -1) for a in range(rows)] + [(a, cols) for a in range(rows)]
    places += [(-1, b) for b in range(-1, cols + 1)] + [(rows, b) for b in range(-1, cols + 1)]
    found = []
    for k in range(8):
        shift_a, shift_b = OFFSETS[k]
        for a in range(rows):
            for b in range(cols):
                place = (a + shift_a, b + shift_b)
                if place in places:
                    own = a * cols + b
                    found.append((k, own, item_code(own, places.index(place), -shift_a, -shift_b)))
    return found


def pack_kernel(v_ref, c_ref, first_ref, last_ref, edge_ref, v_out_ref, c_out_ref):
    rows, cols, rhs = v_ref.shape[:3]
    both = slice(rhs, rhs + 2)
    for column_ref, at in ((first_ref, 0), (last_ref, cols - 1)):
        column_ref[:, 0:rhs] = v_ref[:, at]
        column_ref[:, both] = c_ref[:, at]
    for n, at in enumerate((0, rows - 1)):
        edge_ref[n, :, 0:rhs] = v_ref[at]
        edge_ref[n, :, both] = c_ref[at]
    for row in range(rows):
        v_out_ref[row * cols : (row + 1) * cols] = v_ref[row]
        c_out_ref[row * cols : (row + 1) * cols] = c_ref[row]


def prepare_kernel(pair_ref, v_ref, c_ref, near_ref, cross_ref, parts_ref, points_ref, spread_ref):
    rows, cols = pair_ref.shape[1:]
    lanes = spread_ref.shape[3]

    def one(at, carry):
        store_parts(parts_ref, at, v_ref[at])
        scaled = c_ref[at] * UNIT
        points_ref[at] = scaled
        for axis in range(2):
            spread_ref[at, axis] = across_lanes(scaled[axis : axis + 1], lanes)
        return carry

    lax.fori_loop(0, rows * cols, one, 0, unroll=2)
    list_items(near_ref, inner_candidates(rows, cols), pair_ref)
    list_items(cross_ref, cross_candidates(rows, cols), pair_ref)


def use_own(out_ref, parts_ref, high, low, at):
    out_ref[at] += product(dot_nn, parts_ref, at, high, low)


def use_pair(out_ref, parts_ref, items_ref, high, low, n):
    own, other = item_blocks(items_ref[n + 1])
    out_ref[own] += product(dot_nn, parts_ref, other, high, low)
    out_ref[other] += product(dot_nt, parts_ref, own, high, low)


def use_cross(out_ref, parts_ref, items_ref, high, low, n):
    own, other = item_blocks(items_ref[n + 1])
    out_ref[own] += product(dot_nt, parts_ref, other, high, low)


def near_first_kernel(items_ref, v_ref, parts_ref, points_ref, spread_ref, out_ref, kept_ref, tile_a, tile_b):
    blocks = parts_ref.shape[0]
    out_ref[...] = NUGGET * v_ref[...]

    def make_own(tile_ref, at):
        make_tile(tile_ref, kept_ref, at, spread_ref, at, points_ref, at, 0.0, 0.0)

    def make_pair(tile_ref, n):
        code = items_ref[n + 1]
        own, other = item_blocks(code)
        make_tile(tile_ref, kept_ref, blocks + n, spread_ref, other, points_ref, own, *item_shifts(code))

    make_and_use(blocks, tile_a, tile_b, make_own, functools.partial(use_own, out_ref, parts_ref))
    make_and_use(items_ref[0], tile_a, tile_b, make_pair, functools.partial(use_pair, out_ref, parts_ref, items_ref))


def take_round(round_refs, rhs, parts_ref, points_ref=None):
    start = 0
    for side in round_refs:

        def take(at, carry, side=side, start=start):
            store_parts(parts_ref, start + at, side[at, 0:rhs])
            if points_ref is not None:
                points_ref[start + at] = side[at, rhs : rhs + 2] * UNIT
            return carry

        lax.fori_loop(0, side.shape[0], take, 0)
        start += side.shape[0]


def cross_first_kernel(
    items_ref, sum_ref, west_ref, east_ref, north_ref, south_ref, spread_ref,
    out_ref, kept_ref, parts_ref, points_ref, tile_a, tile_b
):
    out_ref[...] = sum_ref[...]
    take_round((west_ref, east_ref, north_ref, south_ref), sum_ref.shape[1], parts_ref, points_ref)

    def make(tile_ref, n):
        code = items_ref[n + 1]
        own, other = item_blocks(code)
        make_tile(tile_ref, kept_ref, n, spread_ref, own, points_ref, other, *item_shifts(code))

    make_and_use(items_ref[0], tile_a, tile_b, make, functools.partial(use_cross, out_ref, parts_ref, items_ref))


def own_again_kernel(v_ref, kept_ref, out_ref, parts_ref):
    def one(at, carry):
        store_parts(parts_ref, at, v_ref[at])
        out_ref[at] = NUGGET * v_ref[at]
        return carry

    lax.fori_loop(0, parts_ref.shape[0], one, 0, unroll=2)
    only_use(jnp.int32(parts_ref.shape[0]), kept_ref, 0, functools.partial(use_own, out_ref, parts_ref))


def inner_again_kernel(items_ref, sum_ref, parts_ref, kept_ref, out_ref):
    out_ref[...] = sum_ref[...]
    use = functools.partial(use_pair, out_ref, parts_ref, items_ref)
    only_use(items_ref[0], kept_ref, parts_ref.shape[0], use)


def cross_again_kernel(
    items_ref, sum_ref, west_ref, east_ref, north_ref, south_ref, kept_ref, v0_ref, v1_ref,
    out_ref, moments_ref, parts_ref
):
    out_ref[...] = sum_ref[...]
    take_round((west_ref, east_ref, north_ref, south_ref), sum_ref.shape[1], parts_ref)
    only_use(items_ref[0], kept_ref, 0, functools.partial(use_cross, out_ref, parts_ref, items_ref))
    zero = jnp.zeros(out_ref.shape[1:], jnp.float32)

    def gather(at, sums):
        w0, w1, w2 = v0_ref[at], v1_ref[at], out_ref[at]
        terms = (w0 * w0, w0 * w1, w1 * w1, w1 * w2)
        return tuple(s + t for s, t in zip(sums, terms))

    sums = lax.fori_loop(0, out_ref.shape[0], gather, (zero,) * 4)
    lanes = moments_ref.shape[2]
    folded = [sum(s[:, left : left + lanes] for left in range(0, s.shape[1], lanes)) for s in sums]
    stacked = jnp.concatenate(folded, axis=0)
    line = jnp.sum(jnp.transpose(stacked), axis=0, keepdims=True)
    moments_ref[...] = jnp.broadcast_to(line[None], moments_ref.shape)


def final_kernel(moments_ref, v0_ref, v1_ref, v2_ref, solution_ref, residual_ref):
    rhs, points = v0_ref.shape[1:]
    line = moments_ref[0]
    for at in range(1, moments_ref.shape[0]):
        line = line + moments_ref[at]
    table = across_lanes(line, line.shape[1])
    m00, m01, m11, m12 = (table[k * rhs : (k + 1) * rhs] for k in range(4))
    a = m00 / m01
    norm = m00 - 2.0 * a * m01 + a * a * m11
    grow = 1.0 + norm / m00
    step = norm / (grow * (grow * m01 - 2.0 * a * m11) + a * a * m12)
    first = jnp.concatenate([a + step * grow] * (points // line.shape[1]), axis=1)
    second = jnp.concatenate([step * a] * (points // line.shape[1]), axis=1)

    def one(at, carry):
        w0, w1, w2 = v0_ref[at], v1_ref[at], v2_ref[at]
        solution_ref[at] = first * w0 - second * w1
        residual_ref[at] = w0 - first * w1 + second * w2
        return carry

    lax.fori_loop(0, v0_ref.shape[0], one, 0)


def passed_along(x, axis, by):
    count = lax.axis_size(axis)
    pairs = [(i, i + by) for i in range(count) if 0 <= i + by < count]
    return lax.ppermute(x, axis, pairs)


def on_device(kernel, outputs, inputs, scratch=(), listed=False, products=0, made=0):
    vmem = pl.BlockSpec(memory_space=pltpu.VMEM)
    smem = pl.BlockSpec(memory_space=pltpu.SMEM)
    return pl.pallas_call(
        kernel,
        out_shape=tuple(outputs),
        in_specs=[smem if listed and n == 0 else vmem for n in range(len(inputs))],
        out_specs=tuple(smem if out.dtype == jnp.int32 else vmem for out in outputs),
        scratch_shapes=list(scratch),
        compiler_params=pltpu.CompilerParams(vmem_limit_bytes=VMEM_LIMIT),
        cost_estimate=pl.CostEstimate(
            flops=products, transcendentals=made, bytes_accessed=sum(4 * x.size for x in inputs)
        ),
        name=kernel.__name__,
    )(*inputs)


def tiles(count, points):
    return jax.ShapeDtypeStruct((count, 2, points, points), jnp.bfloat16)


def per_device(right_side, coords, pair_list):
    rows, cols, rhs, points = right_side.shape
    blocks = rows * cols
    devices = lax.axis_size("region") * lax.axis_size("tile")
    lanes = 128
    f32, bf16, i32 = jnp.float32, jnp.bfloat16, jnp.int32
    array = jax.ShapeDtypeStruct
    halo = 2 * rows + 2 * (cols + 2)
    near_count = len(inner_candidates(rows, cols))
    cross_count = len(cross_candidates(rows, cols))
    field = array((blocks, rhs, points), f32)
    column = array((rows, rhs + 2, points), f32)
    tile = pltpu.VMEM((2, points, points), bf16)
    parts_round = pltpu.VMEM((halo, 2 * rhs, points), bf16)
    each = 6 * rhs * points * points

    def columns_round(first, last):
        return passed_along(last, "tile", 1), passed_along(first, "tile", -1)

    def rows_round(first, last, west, east):
        top = jnp.concatenate([west[:1], first, east[:1]], axis=0)
        bottom = jnp.concatenate([west[rows - 1 :], last, east[rows - 1 :]], axis=0)
        return passed_along(bottom, "region", 1), passed_along(top, "region", -1)

    first, last, edges, w0, stations = on_device(
        pack_kernel, (column, column, array((2, cols, rhs + 2, points), f32), field, array((blocks, 2, points), f32)),
        (right_side, coords),
    )
    west, east = columns_round(first, last)
    near_items, cross_items, parts, own_points, spread = on_device(
        prepare_kernel,
        (array((near_count + 3,), i32), array((cross_count + 3,), i32), array((blocks, 2 * rhs, points), bf16),
         array((blocks, 2, points), f32), array((blocks, 2, points, lanes), f32)),
        (pair_list, w0, stations), listed=True, products=blocks * each,
    )
    west, east, parts = lax.optimization_barrier((west, east, parts))
    north, south = rows_round(edges[0], edges[1], west, east)
    part, near_tiles = on_device(
        near_first_kernel, (field, tiles(blocks + near_count + 2, points)),
        (near_items, w0, parts, own_points, spread), (tile, tile), True,
        (blocks + near_count) * each, (blocks + near_count) * 2 * points * points,
    )
    w1, cross_tiles = on_device(
        cross_first_kernel, (field, tiles(cross_count + 2, points)),
        (cross_items, part, west, east, north, south, spread),
        (parts_round, pltpu.VMEM((halo, 2, points), f32), tile, tile), True,
        cross_count * each, cross_count * 2 * points * points,
    )
    w1_grid = w1.reshape(right_side.shape)
    west, east = columns_round(w1_grid[:, 0], w1_grid[:, cols - 1])
    part, parts = on_device(
        own_again_kernel, (field, array((blocks, 2 * rhs, points), bf16)), (w1, near_tiles), products=blocks * each
    )
    west, east, part = lax.optimization_barrier((west, east, part))
    north, south = rows_round(w1_grid[0], w1_grid[rows - 1], west, east)
    (part,) = on_device(
        inner_again_kernel, (field,), (near_items, part, parts, near_tiles), (), True, near_count * each
    )
    w2, moments = on_device(
        cross_again_kernel, (field, array((devices, 1, 4 * rhs), f32)),
        (cross_items, part, west, east, north, south, cross_tiles, w0, w1), (parts_round,), True, cross_count * each,
    )
    moments = lax.all_to_all(moments, ("region", "tile"), 0, 0)
    solution, residual = on_device(final_kernel, (field, field), (moments, w0, w1, w2))
    return solution.reshape(right_side.shape), residual.reshape(right_side.shape)


def solution(mesh):
    placed = (
        P("region", "tile", None, None),
        P("region", "tile", None, None),
        P(None, "region", "tile"),
    )
    return jax.shard_map(
        per_device,
        mesh=mesh,
        in_specs=placed,
        out_specs=(P("region", "tile", None, None), P("region", "tile", None, None)),
        check_vma=False,
    )
```

```python
import functools

import jax
import jax.numpy as jnp
from jax import lax
from jax.experimental import pallas as pl
from jax.experimental.pallas import tpu as pltpu
from jax.sharding import PartitionSpec as P

LENGTH_SCALE = 0.2
TAPER_RANGE = 0.5
NUGGET = 3.0
OFFSETS = ((0, 1), (1, 0), (1, 1), (1, -1), (0, -1), (-1, 0), (-1, -1), (-1, 1))
UNIT = 1.4426950408889634 / LENGTH_SCALE
EDGE = UNIT * TAPER_RANGE
WEIGHT = 4.0 * 2.0**-EDGE / EDGE**5
STRIP = 64
LONG_TURN_LOG2 = 3
VMEM_LIMIT = 10 * 1024 * 1024


def dot_nn(a, b):
    return lax.dot_general(a, b, (((1,), (0,)), ((), ())), preferred_element_type=jnp.float32)


def dot_nt(a, b):
    return lax.dot_general(a, b, (((1,), (1,)), ((), ())), preferred_element_type=jnp.float32)


def split_hi_lo(values):
    hi = values.astype(jnp.bfloat16)
    lo = (values - hi.astype(jnp.float32)).astype(jnp.bfloat16)
    return hi, lo


def across_lanes(row, lanes):
    return jnp.transpose(jnp.broadcast_to(row, (lanes, row.shape[1])))


def make_tile(keep_ref, slot, spread_ref, down, points_ref, along, shift_a, shift_b):
    points = keep_ref.shape[2]
    lanes = spread_ref.shape[3]
    row_x = points_ref[along, 0:1] - shift_a
    row_y = points_ref[along, 1:2] - shift_b
    for start in range(0, points, STRIP):
        rows = slice(start, start + STRIP)
        for left in range(0, points, lanes):
            cols = slice(left, left + lanes)
            gap_x = spread_ref[down, 0, rows] - row_x[:, cols]
            gap_y = spread_ref[down, 1, rows] - row_y[:, cols]
            square = jnp.maximum(gap_x * gap_x + gap_y * gap_y, 1e-30)
            rest = jnp.maximum(EDGE - square * lax.rsqrt(square), 0.0)
            rest2 = rest * rest
            cov = (jnp.exp2(rest) * (rest2 * rest2)) * (1.25 * EDGE - rest)
            for part, values in enumerate(split_hi_lo(cov)):
                keep_ref[slot, part, rows, cols] = values


def product(dot, parts_ref, at, high, low):
    rhs = parts_ref.shape[1] // 2
    both = dot(parts_ref[at], high)
    cross = dot(parts_ref[at, 0:rhs], low)
    return both[:rhs] + both[rhs:] + cross


def store_parts(parts_ref, at, values):
    rhs = values.shape[0]
    hi, lo = split_hi_lo(values * WEIGHT)
    parts_ref[at, 0:rhs] = hi
    parts_ref[at, rhs : 2 * rhs] = lo


def in_turns(count, step):
    turns = lax.shift_right_logical(count + 1, 1)

    def one_turn(turn, carry):
        step(2 * turn)
        step(2 * turn + 1)
        return carry

    lax.fori_loop(0, turns, one_turn, 0)


def only_use(count, kept_ref, base, use):
    def one_turn(start, length):
        for n in range(length):
            use(kept_ref[base + start + n, 0], kept_ref[base + start + n, 1], start + n)

    whole = lax.shift_right_logical(count, LONG_TURN_LOG2)
    lax.fori_loop(0, whole, lambda turn, c: (one_turn(turn << LONG_TURN_LOG2, 1 << LONG_TURN_LOG2), c)[1], 0)
    lax.fori_loop(whole << LONG_TURN_LOG2, count, lambda n, c: (one_turn(n, 1), c)[1], 0)


def item_code(own, other, shift_a, shift_b):
    return own + 64 * other + 4096 * (shift_a + 1) + 16384 * (shift_b + 1)


NO_ITEM = item_code(0, 0, 2, 2)


def item_blocks(code):
    return lax.bitwise_and(code, 63), lax.bitwise_and(lax.shift_right_logical(code, 6), 63)


def item_shifts(code):
    shift_a = lax.bitwise_and(lax.shift_right_logical(code, 12), 3) - 1
    shift_b = lax.shift_right_logical(code, 14) - 1
    return shift_a.astype(jnp.float32) * UNIT, shift_b.astype(jnp.float32) * UNIT


def list_items(items_ref, candidates, pair_ref):
    cols = pair_ref.shape[2]
    count = jnp.int32(0)
    for k, own, code in candidates:
        items_ref[count + 1] = code
        count = count + jnp.where(pair_ref[k, own // cols, own % cols] > 0, 1, 0)
    items_ref[0] = count
    items_ref[count + 1] = NO_ITEM


def inner_candidates(rows, cols):
    found = []
    for k in range(4):
        shift_a, shift_b = OFFSETS[k]
        for a in range(rows):
            for b in range(cols):
                if 0 <= a + shift_a < rows and 0 <= b + shift_b < cols:
                    own = a * cols + b
                    other = own + shift_a * cols + shift_b
                    found.append((k, own, item_code(own, other, shift_a, shift_b)))
    return found


def cross_candidates(rows, cols):
    places = [(a, -1) for a in range(rows)] + [(a, cols) for a in range(rows)]
    places += [(-1, b) for b in range(-1, cols + 1)] + [(rows, b) for b in range(-1, cols + 1)]
    found = []
    for k in range(8):
        shift_a, shift_b = OFFSETS[k]
        for a in range(rows):
            for b in range(cols):
                place = (a + shift_a, b + shift_b)
                if place in places:
                    own = a * cols + b
                    found.append((k, own, item_code(own, places.index(place), -shift_a, -shift_b)))
    return found


def pack_kernel(v_ref, c_ref, first_ref, last_ref, edge_ref, v_out_ref, c_out_ref):
    rows, cols, rhs = v_ref.shape[:3]
    both = slice(rhs, rhs + 2)
    for column_ref, at in ((first_ref, 0), (last_ref, cols - 1)):
        column_ref[:, 0:rhs] = v_ref[:, at]
        column_ref[:, both] = c_ref[:, at]
    for n, at in enumerate((0, rows - 1)):
        edge_ref[n, :, 0:rhs] = v_ref[at]
        edge_ref[n, :, both] = c_ref[at]
    for row in range(rows):
        v_out_ref[row * cols : (row + 1) * cols] = v_ref[row]
        c_out_ref[row * cols : (row + 1) * cols] = c_ref[row]


def prepare_kernel(pair_ref, v_ref, c_ref, near_ref, cross_ref, parts_ref, points_ref, spread_ref):
    rows, cols = pair_ref.shape[1:]
    lanes = spread_ref.shape[3]

    def one(at, carry):
        store_parts(parts_ref, at, v_ref[at])
        scaled = c_ref[at] * UNIT
        points_ref[at] = scaled
        for axis in range(2):
            spread_ref[at, axis] = across_lanes(scaled[axis : axis + 1], lanes)
        return carry

    lax.fori_loop(0, rows * cols, one, 0, unroll=2)
    list_items(near_ref, inner_candidates(rows, cols), pair_ref)
    list_items(cross_ref, cross_candidates(rows, cols), pair_ref)


def use_own(out_ref, parts_ref, high, low, at):
    out_ref[at] += product(dot_nn, parts_ref, at, high, low)


def use_pair(out_ref, parts_ref, items_ref, high, low, n):
    own, other = item_blocks(items_ref[n + 1])
    out_ref[own] += product(dot_nn, parts_ref, other, high, low)
    out_ref[other] += product(dot_nt, parts_ref, own, high, low)


def use_cross(out_ref, parts_ref, items_ref, high, low, n):
    own, other = item_blocks(items_ref[n + 1])
    out_ref[own] += product(dot_nt, parts_ref, other, high, low)


def near_first_kernel(items_ref, v_ref, parts_ref, points_ref, spread_ref, out_ref, kept_ref):
    blocks = parts_ref.shape[0]
    out_ref[...] = NUGGET * v_ref[...]

    def make_own(at):
        make_tile(kept_ref, at, spread_ref, at, points_ref, at, 0.0, 0.0)

    def make_pair(n):
        code = items_ref[n + 1]
        own, other = item_blocks(code)
        make_tile(kept_ref, blocks + n, spread_ref, other, points_ref, own, *item_shifts(code))

    in_turns(jnp.int32(blocks), make_own)
    in_turns(items_ref[0], make_pair)
    only_use(jnp.int32(blocks), kept_ref, 0, functools.partial(use_own, out_ref, parts_ref))
    only_use(items_ref[0], kept_ref, blocks, functools.partial(use_pair, out_ref, parts_ref, items_ref))


def take_round(round_refs, rhs, parts_ref, points_ref=None):
    start = 0
    for side in round_refs:

        def take(at, carry, side=side, start=start):
            store_parts(parts_ref, start + at, side[at, 0:rhs])
            if points_ref is not None:
                points_ref[start + at] = side[at, rhs : rhs + 2] * UNIT
            return carry

        lax.fori_loop(0, side.shape[0], take, 0)
        start += side.shape[0]


def cross_first_kernel(
    items_ref, sum_ref, west_ref, east_ref, north_ref, south_ref, spread_ref,
    out_ref, kept_ref, parts_ref, points_ref
):
    out_ref[...] = sum_ref[...]
    take_round((west_ref, east_ref, north_ref, south_ref), sum_ref.shape[1], parts_ref, points_ref)

    def make(n):
        code = items_ref[n + 1]
        own, other = item_blocks(code)
        make_tile(kept_ref, n, spread_ref, own, points_ref, other, *item_shifts(code))

    in_turns(items_ref[0], make)
    only_use(items_ref[0], kept_ref, 0, functools.partial(use_cross, out_ref, parts_ref, items_ref))


def own_again_kernel(v_ref, kept_ref, out_ref, parts_ref):
    def one(at, carry):
        store_parts(parts_ref, at, v_ref[at])
        out_ref[at] = NUGGET * v_ref[at]
        return carry

    lax.fori_loop(0, parts_ref.shape[0], one, 0, unroll=2)
    only_use(jnp.int32(parts_ref.shape[0]), kept_ref, 0, functools.partial(use_own, out_ref, parts_ref))


def inner_again_kernel(items_ref, sum_ref, parts_ref, kept_ref, out_ref):
    out_ref[...] = sum_ref[...]
    use = functools.partial(use_pair, out_ref, parts_ref, items_ref)
    only_use(items_ref[0], kept_ref, parts_ref.shape[0], use)


def cross_again_kernel(
    items_ref, sum_ref, west_ref, east_ref, north_ref, south_ref, kept_ref, v0_ref, v1_ref,
    out_ref, moments_ref, parts_ref
):
    out_ref[...] = sum_ref[...]
    take_round((west_ref, east_ref, north_ref, south_ref), sum_ref.shape[1], parts_ref)
    only_use(items_ref[0], kept_ref, 0, functools.partial(use_cross, out_ref, parts_ref, items_ref))
    zero = jnp.zeros(out_ref.shape[1:], jnp.float32)

    def gather(at, sums):
        w0, w1, w2 = v0_ref[at], v1_ref[at], out_ref[at]
        terms = (w0 * w0, w0 * w1, w1 * w1, w1 * w2)
        return tuple(s + t for s, t in zip(sums, terms))

    sums = lax.fori_loop(0, out_ref.shape[0], gather, (zero,) * 4)
    lanes = moments_ref.shape[2]
    folded = [sum(s[:, left : left + lanes] for left in range(0, s.shape[1], lanes)) for s in sums]
    stacked = jnp.concatenate(folded, axis=0)
    line = jnp.sum(jnp.transpose(stacked), axis=0, keepdims=True)
    moments_ref[...] = jnp.broadcast_to(line[None], moments_ref.shape)


def final_kernel(moments_ref, v0_ref, v1_ref, v2_ref, solution_ref, residual_ref):
    rhs, points = v0_ref.shape[1:]
    line = moments_ref[0]
    for at in range(1, moments_ref.shape[0]):
        line = line + moments_ref[at]
    table = across_lanes(line, line.shape[1])
    m00, m01, m11, m12 = (table[k * rhs : (k + 1) * rhs] for k in range(4))
    a = m00 / m01
    norm = m00 - 2.0 * a * m01 + a * a * m11
    grow = 1.0 + norm / m00
    step = norm / (grow * (grow * m01 - 2.0 * a * m11) + a * a * m12)
    first = jnp.concatenate([a + step * grow] * (points // line.shape[1]), axis=1)
    second = jnp.concatenate([step * a] * (points // line.shape[1]), axis=1)

    def one(at, carry):
        w0, w1, w2 = v0_ref[at], v1_ref[at], v2_ref[at]
        solution_ref[at] = first * w0 - second * w1
        residual_ref[at] = w0 - first * w1 + second * w2
        return carry

    lax.fori_loop(0, v0_ref.shape[0], one, 0)


def swapped(first, last, axis):
    count = lax.axis_size(axis)
    even = lax.rem(lax.axis_index(axis), 2) == 0
    swap_up = [(i, i ^ 1) for i in range(count) if i ^ 1 < count]
    swap_down = [(i, ((i + 1) ^ 1) - 1) for i in range(count) if 0 <= ((i + 1) ^ 1) - 1 < count]
    got_up = lax.ppermute(jnp.where(even, last, first), axis, swap_up)
    got_down = lax.ppermute(jnp.where(even, first, last), axis, swap_down)
    return jnp.where(even, got_down, got_up), jnp.where(even, got_up, got_down)


def on_device(kernel, outputs, inputs, scratch=(), listed=False, products=0, made=0):
    vmem = pl.BlockSpec(memory_space=pltpu.VMEM)
    smem = pl.BlockSpec(memory_space=pltpu.SMEM)
    return pl.pallas_call(
        kernel,
        out_shape=tuple(outputs),
        in_specs=[smem if listed and n == 0 else vmem for n in range(len(inputs))],
        out_specs=tuple(smem if out.dtype == jnp.int32 else vmem for out in outputs),
        scratch_shapes=list(scratch),
        compiler_params=pltpu.CompilerParams(vmem_limit_bytes=VMEM_LIMIT),
        cost_estimate=pl.CostEstimate(
            flops=products, transcendentals=made, bytes_accessed=sum(4 * x.size for x in inputs)
        ),
        name=kernel.__name__,
    )(*inputs)


def tiles(count, points):
    return jax.ShapeDtypeStruct((count, 2, points, points), jnp.bfloat16)


def per_device(right_side, coords, pair_list):
    rows, cols, rhs, points = right_side.shape
    blocks = rows * cols
    devices = lax.axis_size("region") * lax.axis_size("tile")
    lanes = 128
    f32, bf16, i32 = jnp.float32, jnp.bfloat16, jnp.int32
    array = jax.ShapeDtypeStruct
    halo = 2 * rows + 2 * (cols + 2)
    near_count = len(inner_candidates(rows, cols))
    cross_count = len(cross_candidates(rows, cols))
    field = array((blocks, rhs, points), f32)
    column = array((rows, rhs + 2, points), f32)
    parts_round = pltpu.VMEM((halo, 2 * rhs, points), bf16)
    each = 6 * rhs * points * points

    def rows_round(first, last, west, east):
        top = jnp.concatenate([west[:1], first, east[:1]], axis=0)
        bottom = jnp.concatenate([west[rows - 1 :], last, east[rows - 1 :]], axis=0)
        return swapped(top, bottom, "region")

    first, last, edges, w0, stations = on_device(
        pack_kernel, (column, column, array((2, cols, rhs + 2, points), f32), field, array((blocks, 2, points), f32)),
        (right_side, coords),
    )
    west, east = swapped(first, last, "tile")
    near_items, cross_items, parts, own_points, spread = on_device(
        prepare_kernel,
        (array((near_count + 3,), i32), array((cross_count + 3,), i32), array((blocks, 2 * rhs, points), bf16),
         array((blocks, 2, points), f32), array((blocks, 2, points, lanes), f32)),
        (pair_list, w0, stations), listed=True, products=blocks * each,
    )
    west, east, parts = lax.optimization_barrier((west, east, parts))
    north, south = rows_round(edges[0], edges[1], west, east)
    part, near_tiles = on_device(
        near_first_kernel, (field, tiles(blocks + near_count + 2, points)),
        (near_items, w0, parts, own_points, spread), (), True,
        (blocks + near_count) * each, (blocks + near_count) * 2 * points * points,
    )
    w1, cross_tiles = on_device(
        cross_first_kernel, (field, tiles(cross_count + 2, points)),
        (cross_items, part, west, east, north, south, spread),
        (parts_round, pltpu.VMEM((halo, 2, points), f32)), True,
        cross_count * each, cross_count * 2 * points * points,
    )
    w1_grid = w1.reshape(right_side.shape)
    west, east = swapped(w1_grid[:, 0], w1_grid[:, cols - 1], "tile")
    part, parts = on_device(
        own_again_kernel, (field, array((blocks, 2 * rhs, points), bf16)), (w1, near_tiles), products=blocks * each
    )
    west, east, part = lax.optimization_barrier((west, east, part))
    north, south = rows_round(w1_grid[0], w1_grid[rows - 1], west, east)
    (part,) = on_device(
        inner_again_kernel, (field,), (near_items, part, parts, near_tiles), (), True, near_count * each
    )
    w2, moments = on_device(
        cross_again_kernel, (field, array((devices, 1, 4 * rhs), f32)),
        (cross_items, part, west, east, north, south, cross_tiles, w0, w1), (parts_round,), True, cross_count * each,
    )
    moments = lax.all_to_all(moments, ("region", "tile"), 0, 0)
    solution, residual = on_device(final_kernel, (field, field), (moments, w0, w1, w2))
    return solution.reshape(right_side.shape), residual.reshape(right_side.shape)


def solution(mesh):
    placed = (
        P("region", "tile", None, None),
        P("region", "tile", None, None),
        P(None, "region", "tile"),
    )
    return jax.shard_map(
        per_device,
        mesh=mesh,
        in_specs=placed,
        out_specs=(P("region", "tile", None, None), P("region", "tile", None, None)),
        check_vma=False,
    )
```

```python
import functools

import jax
import jax.numpy as jnp
from jax import lax
from jax.experimental import pallas as pl
from jax.experimental.pallas import tpu as pltpu
from jax.sharding import PartitionSpec as P

LENGTH_SCALE = 0.2
TAPER_RANGE = 0.5
NUGGET = 3.0
OFFSETS = ((0, 1), (1, 0), (1, 1), (1, -1), (0, -1), (-1, 0), (-1, -1), (-1, 1))
UNIT = 1.4426950408889634 / LENGTH_SCALE
EDGE = UNIT * TAPER_RANGE
WEIGHT = 4.0 * 2.0**-EDGE / EDGE**5
STRIP = 64
LONG_TURN_LOG2 = 3
VMEM_LIMIT = 10 * 1024 * 1024


def dot_nn(a, b):
    return lax.dot_general(a, b, (((1,), (0,)), ((), ())), preferred_element_type=jnp.float32)


def dot_nt(a, b):
    return lax.dot_general(a, b, (((1,), (1,)), ((), ())), preferred_element_type=jnp.float32)


def split_hi_lo(values):
    hi = values.astype(jnp.bfloat16)
    lo = (values - hi.astype(jnp.float32)).astype(jnp.bfloat16)
    return hi, lo


def across_lanes(row, lanes):
    return jnp.transpose(jnp.broadcast_to(row, (lanes, row.shape[1])))


def make_tile(keep_ref, slot, spread_ref, down, points_ref, along, shift_a, shift_b):
    points = keep_ref.shape[2]
    lanes = spread_ref.shape[3]
    row_x = points_ref[along, 0:1] - shift_a
    row_y = points_ref[along, 1:2] - shift_b
    for start in range(0, points, STRIP):
        rows = slice(start, start + STRIP)
        for left in range(0, points, lanes):
            cols = slice(left, left + lanes)
            gap_x = spread_ref[down, 0, rows] - row_x[:, cols]
            gap_y = spread_ref[down, 1, rows] - row_y[:, cols]
            square = jnp.maximum(gap_x * gap_x + gap_y * gap_y, 1e-30)
            rest = jnp.maximum(EDGE - square * lax.rsqrt(square), 0.0)
            rest2 = rest * rest
            cov = (jnp.exp2(rest) * (rest2 * rest2)) * (1.25 * EDGE - rest)
            for part, values in enumerate(split_hi_lo(cov)):
                keep_ref[slot, part, rows, cols] = values


def product(dot, parts_ref, at, high, low):
    rhs = parts_ref.shape[1] // 2
    both = dot(parts_ref[at], high)
    cross = dot(parts_ref[at, 0:rhs], low)
    return both[:rhs] + both[rhs:] + cross


def store_parts(parts_ref, at, values):
    rhs = values.shape[0]
    hi, lo = split_hi_lo(values * WEIGHT)
    parts_ref[at, 0:rhs] = hi
    parts_ref[at, rhs : 2 * rhs] = lo


def in_turns(count, step):
    turns = lax.shift_right_logical(count + 1, 1)

    def one_turn(turn, carry):
        step(2 * turn)
        step(2 * turn + 1)
        return carry

    lax.fori_loop(0, turns, one_turn, 0)


def only_use(count, kept_ref, base, use):
    def one_turn(start, length):
        for n in range(length):
            use(kept_ref[base + start + n, 0], kept_ref[base + start + n, 1], start + n)

    whole = lax.shift_right_logical(count, LONG_TURN_LOG2)
    lax.fori_loop(0, whole, lambda turn, c: (one_turn(turn << LONG_TURN_LOG2, 1 << LONG_TURN_LOG2), c)[1], 0)
    lax.fori_loop(whole << LONG_TURN_LOG2, count, lambda n, c: (one_turn(n, 1), c)[1], 0)


def item_code(own, other, shift_a, shift_b):
    return own + 64 * other + 4096 * (shift_a + 1) + 16384 * (shift_b + 1)


NO_ITEM = item_code(0, 0, 2, 2)


def item_blocks(code):
    return lax.bitwise_and(code, 63), lax.bitwise_and(lax.shift_right_logical(code, 6), 63)


def item_shifts(code):
    shift_a = lax.bitwise_and(lax.shift_right_logical(code, 12), 3) - 1
    shift_b = lax.shift_right_logical(code, 14) - 1
    return shift_a.astype(jnp.float32) * UNIT, shift_b.astype(jnp.float32) * UNIT


def list_items(items_ref, candidates, pair_ref):
    cols = pair_ref.shape[1]
    count = jnp.int32(0)
    for k, own, code in candidates:
        items_ref[count + 1] = code
        count = count + jnp.where(pair_ref[own // cols, own % cols, k] > 0, 1, 0)
    items_ref[0] = count
    items_ref[count + 1] = NO_ITEM


def inner_candidates(rows, cols):
    found = []
    for k in range(4):
        shift_a, shift_b = OFFSETS[k]
        for a in range(rows):
            for b in range(cols):
                if 0 <= a + shift_a < rows and 0 <= b + shift_b < cols:
                    own = a * cols + b
                    other = own + shift_a * cols + shift_b
                    found.append((k, own, item_code(own, other, shift_a, shift_b)))
    return found


def cross_candidates(rows, cols):
    places = [(a, -1) for a in range(rows)] + [(a, cols) for a in range(rows)]
    places += [(-1, b) for b in range(-1, cols + 1)] + [(rows, b) for b in range(-1, cols + 1)]
    found = []
    for k in range(8):
        shift_a, shift_b = OFFSETS[k]
        for a in range(rows):
            for b in range(cols):
                place = (a + shift_a, b + shift_b)
                if place in places:
                    own = a * cols + b
                    found.append((k, own, item_code(own, places.index(place), -shift_a, -shift_b)))
    return found


def pack_kernel(v_hbm, c_hbm, pair_hbm, first_ref, last_ref, edge_ref, v_ref, c_ref, pair_ref, sems):
    rows, cols, rhs = v_hbm.shape[:3]
    fetches = []
    for row in range(rows):
        own = pl.ds(row * cols, cols)
        fetches.append(pltpu.make_async_copy(v_hbm.at[row], v_ref.at[own], sems.at[2 * row]))
        fetches.append(pltpu.make_async_copy(c_hbm.at[row], c_ref.at[own], sems.at[2 * row + 1]))
    fetches.append(pltpu.make_async_copy(pair_hbm, pair_ref, sems.at[2 * rows]))
    for fetch in fetches:
        fetch.start()
    for fetch in fetches:
        fetch.wait()
    both = slice(rhs, rhs + 2)
    for row in range(rows):
        for column_ref, at in ((first_ref, row * cols), (last_ref, row * cols + cols - 1)):
            column_ref[row, 0:rhs] = v_ref[at]
            column_ref[row, both] = c_ref[at]
    for n, row in enumerate((0, rows - 1)):
        own = slice(row * cols, (row + 1) * cols)
        edge_ref[n, :, 0:rhs] = v_ref[own]
        edge_ref[n, :, both] = c_ref[own]


def prepare_kernel(pair_ref, v_ref, c_ref, near_ref, cross_ref, parts_ref, points_ref):
    rows, cols = pair_ref.shape[:2]

    def one(at, carry):
        store_parts(parts_ref, at, v_ref[at])
        points_ref[at] = c_ref[at] * UNIT
        return carry

    lax.fori_loop(0, rows * cols, one, 0, unroll=2)
    list_items(near_ref, inner_candidates(rows, cols), pair_ref)
    list_items(cross_ref, cross_candidates(rows, cols), pair_ref)


def use_own(out_ref, parts_ref, high, low, at):
    out_ref[at] += product(dot_nn, parts_ref, at, high, low)


def use_pair(out_ref, parts_ref, items_ref, high, low, n):
    own, other = item_blocks(items_ref[n + 1])
    out_ref[own] += product(dot_nn, parts_ref, other, high, low)
    out_ref[other] += product(dot_nt, parts_ref, own, high, low)


def use_cross(out_ref, parts_ref, items_ref, high, low, n):
    own, other = item_blocks(items_ref[n + 1])
    out_ref[own] += product(dot_nt, parts_ref, other, high, low)


def near_first_kernel(items_ref, v_ref, parts_ref, points_ref, out_ref, kept_ref, spread_ref):
    blocks = parts_ref.shape[0]
    out_ref[...] = NUGGET * v_ref[...]

    def make_own(at):
        for axis in range(2):
            spread_ref[at, axis] = across_lanes(points_ref[at, axis : axis + 1], spread_ref.shape[3])
        make_tile(kept_ref, at, spread_ref, at, points_ref, at, 0.0, 0.0)

    def make_pair(n):
        code = items_ref[n + 1]
        own, other = item_blocks(code)
        make_tile(kept_ref, blocks + n, spread_ref, other, points_ref, own, *item_shifts(code))

    in_turns(jnp.int32(blocks), make_own)
    in_turns(items_ref[0], make_pair)
    only_use(jnp.int32(blocks), kept_ref, 0, functools.partial(use_own, out_ref, parts_ref))
    only_use(items_ref[0], kept_ref, blocks, functools.partial(use_pair, out_ref, parts_ref, items_ref))


def take_round(round_refs, rhs, parts_ref, points_ref=None):
    start = 0
    for side in round_refs:

        def take(at, carry, side=side, start=start):
            store_parts(parts_ref, start + at, side[at, 0:rhs])
            if points_ref is not None:
                points_ref[start + at] = side[at, rhs : rhs + 2] * UNIT
            return carry

        lax.fori_loop(0, side.shape[0], take, 0)
        start += side.shape[0]


def cross_first_kernel(
    items_ref, sum_ref, west_ref, east_ref, north_ref, south_ref, spread_ref,
    out_ref, kept_ref, parts_ref, points_ref
):
    out_ref[...] = sum_ref[...]
    take_round((west_ref, east_ref, north_ref, south_ref), sum_ref.shape[1], parts_ref, points_ref)

    def make(n):
        code = items_ref[n + 1]
        own, other = item_blocks(code)
        make_tile(kept_ref, n, spread_ref, own, points_ref, other, *item_shifts(code))

    in_turns(items_ref[0], make)
    only_use(items_ref[0], kept_ref, 0, functools.partial(use_cross, out_ref, parts_ref, items_ref))


def own_again_kernel(v_ref, kept_ref, out_ref, parts_ref):
    def one(at, carry):
        store_parts(parts_ref, at, v_ref[at])
        out_ref[at] = NUGGET * v_ref[at]
        return carry

    lax.fori_loop(0, parts_ref.shape[0], one, 0, unroll=2)
    only_use(jnp.int32(parts_ref.shape[0]), kept_ref, 0, functools.partial(use_own, out_ref, parts_ref))


def inner_again_kernel(items_ref, sum_ref, parts_ref, kept_ref, out_ref):
    out_ref[...] = sum_ref[...]
    use = functools.partial(use_pair, out_ref, parts_ref, items_ref)
    only_use(items_ref[0], kept_ref, parts_ref.shape[0], use)


def cross_again_kernel(
    items_ref, sum_ref, west_ref, east_ref, north_ref, south_ref, kept_ref, v0_ref, v1_ref,
    out_ref, moments_ref, parts_ref
):
    out_ref[...] = sum_ref[...]
    take_round((west_ref, east_ref, north_ref, south_ref), sum_ref.shape[1], parts_ref)
    only_use(items_ref[0], kept_ref, 0, functools.partial(use_cross, out_ref, parts_ref, items_ref))
    zero = jnp.zeros(out_ref.shape[1:], jnp.float32)

    def gather(at, sums):
        w0, w1, w2 = v0_ref[at], v1_ref[at], out_ref[at]
        terms = (w0 * w0, w0 * w1, w1 * w1, w1 * w2)
        return tuple(s + t for s, t in zip(sums, terms))

    sums = lax.fori_loop(0, out_ref.shape[0], gather, (zero,) * 4)
    lanes = moments_ref.shape[2]
    folded = [sum(s[:, left : left + lanes] for left in range(0, s.shape[1], lanes)) for s in sums]
    stacked = jnp.concatenate(folded, axis=0)
    line = jnp.sum(jnp.transpose(stacked), axis=0, keepdims=True)
    moments_ref[...] = jnp.broadcast_to(line[None], moments_ref.shape)


def final_kernel(moments_ref, v0_ref, v1_ref, v2_ref, solution_ref, residual_ref):
    rhs, points = v0_ref.shape[1:]
    line = moments_ref[0]
    for at in range(1, moments_ref.shape[0]):
        line = line + moments_ref[at]
    table = across_lanes(line, line.shape[1])
    m00, m01, m11, m12 = (table[k * rhs : (k + 1) * rhs] for k in range(4))
    a = m00 / m01
    norm = m00 - 2.0 * a * m01 + a * a * m11
    grow = 1.0 + norm / m00
    step = norm / (grow * (grow * m01 - 2.0 * a * m11) + a * a * m12)
    first = jnp.concatenate([a + step * grow] * (points // line.shape[1]), axis=1)
    second = jnp.concatenate([step * a] * (points // line.shape[1]), axis=1)

    def one(at, carry):
        w0, w1, w2 = v0_ref[at], v1_ref[at], v2_ref[at]
        solution_ref[at] = first * w0 - second * w1
        residual_ref[at] = w0 - first * w1 + second * w2
        return carry

    lax.fori_loop(0, v0_ref.shape[0], one, 0)


def swapped(first, last, axis):
    count = lax.axis_size(axis)
    even = lax.rem(lax.axis_index(axis), 2) == 0
    swap_up = [(i, i ^ 1) for i in range(count) if i ^ 1 < count]
    swap_down = [(i, ((i + 1) ^ 1) - 1) for i in range(count) if 0 <= ((i + 1) ^ 1) - 1 < count]
    got_up = lax.ppermute(jnp.where(even, last, first), axis, swap_up)
    got_down = lax.ppermute(jnp.where(even, first, last), axis, swap_down)
    return jnp.where(even, got_down, got_up), jnp.where(even, got_up, got_down)


def on_device(kernel, outputs, inputs, scratch=(), listed=False, products=0, made=0, where=pltpu.VMEM):
    vmem = pl.BlockSpec(memory_space=pltpu.VMEM)
    smem = pl.BlockSpec(memory_space=pltpu.SMEM)
    source = pl.BlockSpec(memory_space=where)
    return pl.pallas_call(
        kernel,
        out_shape=tuple(outputs),
        in_specs=[smem if listed and n == 0 else source for n in range(len(inputs))],
        out_specs=tuple(smem if out.dtype == jnp.int32 else vmem for out in outputs),
        scratch_shapes=list(scratch),
        compiler_params=pltpu.CompilerParams(vmem_limit_bytes=VMEM_LIMIT),
        cost_estimate=pl.CostEstimate(
            flops=products, transcendentals=made, bytes_accessed=sum(4 * x.size for x in inputs)
        ),
        name=kernel.__name__,
    )(*inputs)


def tiles(count, points):
    return jax.ShapeDtypeStruct((count, 2, points, points), jnp.bfloat16)


def per_device(right_side, coords, pair_list):
    pair_list = jnp.transpose(pair_list, (1, 2, 0))
    rows, cols, rhs, points = right_side.shape
    blocks = rows * cols
    devices = lax.axis_size("region") * lax.axis_size("tile")
    lanes = 128
    f32, bf16, i32 = jnp.float32, jnp.bfloat16, jnp.int32
    array = jax.ShapeDtypeStruct
    halo = 2 * rows + 2 * (cols + 2)
    near_count = len(inner_candidates(rows, cols))
    cross_count = len(cross_candidates(rows, cols))
    field = array((blocks, rhs, points), f32)
    column = array((rows, rhs + 2, points), f32)
    parts_round = pltpu.VMEM((halo, 2 * rhs, points), bf16)
    each = 6 * rhs * points * points

    def rows_round(first, last, west, east):
        top = jnp.concatenate([west[:1], first, east[:1]], axis=0)
        bottom = jnp.concatenate([west[rows - 1 :], last, east[rows - 1 :]], axis=0)
        return swapped(top, bottom, "region")

    fetched = (
        column, column, array((2, cols, rhs + 2, points), f32), field, array((blocks, 2, points), f32),
        array(pair_list.shape, i32),
    )
    first, last, edges, w0, stations, pairs = on_device(
        pack_kernel, fetched,
        tuple(pltpu.with_memory_space_constraint(x, pltpu.HBM) for x in (right_side, coords, pair_list)),
        (pltpu.SemaphoreType.DMA((2 * rows + 1,)),), where=pltpu.HBM,
    )
    west, east = swapped(first, last, "tile")
    near_items, cross_items, parts, own_points = on_device(
        prepare_kernel,
        (array((near_count + 3,), i32), array((cross_count + 3,), i32), array((blocks, 2 * rhs, points), bf16),
         array((blocks, 2, points), f32)),
        (pairs, w0, stations), listed=True, products=blocks * each,
    )
    west, east, parts = lax.optimization_barrier((west, east, parts))
    north, south = rows_round(edges[0], edges[1], west, east)
    part, near_tiles, spread = on_device(
        near_first_kernel,
        (field, tiles(blocks + near_count + 2, points), array((blocks, 2, points, lanes), f32)),
        (near_items, w0, parts, own_points), (), True,
        (blocks + near_count) * each, (blocks + near_count) * 2 * points * points,
    )
    w1, cross_tiles = on_device(
        cross_first_kernel, (field, tiles(cross_count + 2, points)),
        (cross_items, part, west, east, north, south, spread),
        (parts_round, pltpu.VMEM((halo, 2, points), f32)), True,
        cross_count * each, cross_count * 2 * points * points,
    )
    w1_grid = w1.reshape(right_side.shape)
    west, east = swapped(w1_grid[:, 0], w1_grid[:, cols - 1], "tile")
    part, parts = on_device(
        own_again_kernel, (field, array((blocks, 2 * rhs, points), bf16)), (w1, near_tiles), products=blocks * each
    )
    west, east, part = lax.optimization_barrier((west, east, part))
    north, south = rows_round(w1_grid[0], w1_grid[rows - 1], west, east)
    (part,) = on_device(
        inner_again_kernel, (field,), (near_items, part, parts, near_tiles), (), True, near_count * each
    )
    w2, moments = on_device(
        cross_again_kernel, (field, array((devices, 1, 4 * rhs), f32)),
        (cross_items, part, west, east, north, south, cross_tiles, w0, w1), (parts_round,), True, cross_count * each,
    )
    moments = lax.all_to_all(moments, ("region", "tile"), 0, 0)
    solution, residual = on_device(final_kernel, (field, field), (moments, w0, w1, w2))
    return solution.reshape(right_side.shape), residual.reshape(right_side.shape)


def solution(mesh):
    placed = (
        P("region", "tile", None, None),
        P("region", "tile", None, None),
        P(None, "region", "tile"),
    )
    return jax.shard_map(
        per_device,
        mesh=mesh,
        in_specs=placed,
        out_specs=(P("region", "tile", None, None), P("region", "tile", None, None)),
        check_vma=False,
    )
```

```python
import functools

import jax
import jax.numpy as jnp
from jax import lax
from jax.experimental import pallas as pl
from jax.experimental.pallas import tpu as pltpu
from jax.sharding import PartitionSpec as P

LENGTH_SCALE = 0.2
TAPER_RANGE = 0.5
NUGGET = 3.0
OFFSETS = ((0, 1), (1, 0), (1, 1), (1, -1), (0, -1), (-1, 0), (-1, -1), (-1, 1))
UNIT = 1.4426950408889634 / LENGTH_SCALE
EDGE = UNIT * TAPER_RANGE
WEIGHT = 4.0 * 2.0**-EDGE / EDGE**5
STRIP = 64
LONG_TURN_LOG2 = 3
VMEM_LIMIT = 10 * 1024 * 1024


def dot_nn(a, b):
    return lax.dot_general(a, b, (((1,), (0,)), ((), ())), preferred_element_type=jnp.float32)


def dot_nt(a, b):
    return lax.dot_general(a, b, (((1,), (1,)), ((), ())), preferred_element_type=jnp.float32)


def split_hi_lo(values):
    hi = values.astype(jnp.bfloat16)
    lo = (values - hi.astype(jnp.float32)).astype(jnp.bfloat16)
    return hi, lo


def across_lanes(row, lanes):
    return jnp.transpose(jnp.broadcast_to(row, (lanes, row.shape[1])))


def make_tile(keep_ref, slot, spread_ref, down, points_ref, along, shift_a, shift_b):
    points = keep_ref.shape[2]
    lanes = spread_ref.shape[3]
    row_x = points_ref[along, 0:1] - shift_a
    row_y = points_ref[along, 1:2] - shift_b
    for start in range(0, points, STRIP):
        rows = slice(start, start + STRIP)
        for left in range(0, points, lanes):
            cols = slice(left, left + lanes)
            gap_x = spread_ref[down, 0, rows] - row_x[:, cols]
            gap_y = spread_ref[down, 1, rows] - row_y[:, cols]
            square = jnp.maximum(gap_x * gap_x + gap_y * gap_y, 1e-30)
            rest = jnp.maximum(EDGE - square * lax.rsqrt(square), 0.0)
            rest2 = rest * rest
            cov = (jnp.exp2(rest) * (rest2 * rest2)) * (1.25 * EDGE - rest)
            for part, values in enumerate(split_hi_lo(cov)):
                keep_ref[slot, part, rows, cols] = values


def product(dot, parts_ref, at, high, low):
    rhs = parts_ref.shape[1] // 2
    both = dot(parts_ref[at], high)
    cross = dot(parts_ref[at, 0:rhs], low)
    return both[:rhs] + both[rhs:] + cross


def store_parts(parts_ref, at, values):
    rhs = values.shape[0]
    hi, lo = split_hi_lo(values * WEIGHT)
    parts_ref[at, 0:rhs] = hi
    parts_ref[at, rhs : 2 * rhs] = lo


def in_turns(count, step):
    turns = lax.shift_right_logical(count + 1, 1)

    def one_turn(turn, carry):
        step(2 * turn)
        step(2 * turn + 1)
        return carry

    lax.fori_loop(0, turns, one_turn, 0)


def only_use(count, kept_ref, use):
    def one_turn(start, length):
        for n in range(length):
            use(kept_ref[start + n, 0], kept_ref[start + n, 1], start + n)

    whole = lax.shift_right_logical(count, LONG_TURN_LOG2)
    lax.fori_loop(0, whole, lambda turn, c: (one_turn(turn << LONG_TURN_LOG2, 1 << LONG_TURN_LOG2), c)[1], 0)
    lax.fori_loop(whole << LONG_TURN_LOG2, count, lambda n, c: (one_turn(n, 1), c)[1], 0)


def item_code(own, other, shift_a, shift_b):
    return own + 64 * other + 4096 * (shift_a + 1) + 16384 * (shift_b + 1)


NO_ITEM = item_code(0, 0, 2, 2)


def item_blocks(code):
    return lax.bitwise_and(code, 63), lax.bitwise_and(lax.shift_right_logical(code, 6), 63)


def item_shifts(code):
    shift_a = lax.bitwise_and(lax.shift_right_logical(code, 12), 3) - 1
    shift_b = lax.shift_right_logical(code, 14) - 1
    return shift_a.astype(jnp.float32) * UNIT, shift_b.astype(jnp.float32) * UNIT


def list_items(items_ref, candidates, pair_ref):
    cols = pair_ref.shape[1]
    count = jnp.int32(0)
    for k, own, code in candidates:
        items_ref[count + 1] = code
        count = count + jnp.where(pair_ref[own // cols, own % cols, k] > 0, 1, 0)
    items_ref[0] = count
    items_ref[count + 1] = NO_ITEM


def inner_candidates(rows, cols):
    found = []
    for k in range(4):
        shift_a, shift_b = OFFSETS[k]
        for a in range(rows):
            for b in range(cols):
                if 0 <= a + shift_a < rows and 0 <= b + shift_b < cols:
                    own = a * cols + b
                    other = own + shift_a * cols + shift_b
                    found.append((k, own, item_code(own, other, shift_a, shift_b)))
    return found


def cross_candidates(rows, cols):
    places = [(a, -1) for a in range(rows)] + [(a, cols) for a in range(rows)]
    places += [(-1, b) for b in range(-1, cols + 1)] + [(rows, b) for b in range(-1, cols + 1)]
    found = []
    for k in range(8):
        shift_a, shift_b = OFFSETS[k]
        for a in range(rows):
            for b in range(cols):
                place = (a + shift_a, b + shift_b)
                if place in places:
                    own = a * cols + b
                    found.append((k, own, item_code(own, places.index(place), -shift_a, -shift_b)))
    return found


def pack_kernel(v_hbm, c_hbm, pair_hbm, first_ref, last_ref, edge_ref, v_ref, c_ref, pair_ref, sems):
    rows, cols, rhs = v_hbm.shape[:3]
    fetches = []
    for row in range(rows):
        own = pl.ds(row * cols, cols)
        fetches.append(pltpu.make_async_copy(v_hbm.at[row], v_ref.at[own], sems.at[2 * row]))
        fetches.append(pltpu.make_async_copy(c_hbm.at[row], c_ref.at[own], sems.at[2 * row + 1]))
    fetches.append(pltpu.make_async_copy(pair_hbm, pair_ref, sems.at[2 * rows]))
    for fetch in fetches:
        fetch.start()
    for fetch in fetches:
        fetch.wait()
    both = slice(rhs, rhs + 2)
    for row in range(rows):
        for column_ref, at in ((first_ref, row * cols), (last_ref, row * cols + cols - 1)):
            column_ref[row, 0:rhs] = v_ref[at]
            column_ref[row, both] = c_ref[at]
    for n, row in enumerate((0, rows - 1)):
        own = slice(row * cols, (row + 1) * cols)
        edge_ref[n, :, 0:rhs] = v_ref[own]
        edge_ref[n, :, both] = c_ref[own]


def use_own(out_ref, parts_ref, high, low, at):
    out_ref[at] += product(dot_nn, parts_ref, at, high, low)


def use_pair(out_ref, parts_ref, items_ref, high, low, n):
    own, other = item_blocks(items_ref[n + 1])
    out_ref[own] += product(dot_nn, parts_ref, other, high, low)
    out_ref[other] += product(dot_nt, parts_ref, own, high, low)


def use_cross(out_ref, parts_ref, items_ref, high, low, n):
    own, other = item_blocks(items_ref[n + 1])
    out_ref[own] += product(dot_nt, parts_ref, other, high, low)


def own_first_kernel(
    pair_ref, v_ref, c_ref, near_ref, cross_ref, out_ref, kept_ref, parts_ref, points_ref, spread_ref
):
    rows, cols = pair_ref.shape[:2]
    lanes = spread_ref.shape[3]

    def one(at):
        store_parts(parts_ref, at, v_ref[at])
        out_ref[at] = NUGGET * v_ref[at]
        scaled = c_ref[at] * UNIT
        points_ref[at] = scaled
        for axis in range(2):
            spread_ref[at, axis] = across_lanes(scaled[axis : axis + 1], lanes)
        make_tile(kept_ref, at, spread_ref, at, points_ref, at, 0.0, 0.0)

    def one_pair(turn, carry):
        one(2 * turn)
        one(2 * turn + 1)
        return carry

    lax.fori_loop(0, rows * cols // 2, one_pair, 0)
    only_use(jnp.int32(rows * cols), kept_ref, functools.partial(use_own, out_ref, parts_ref))
    list_items(near_ref, inner_candidates(rows, cols), pair_ref)
    list_items(cross_ref, cross_candidates(rows, cols), pair_ref)


def inner_first_kernel(items_ref, sum_ref, parts_ref, points_ref, spread_ref, out_ref, kept_ref):
    out_ref[...] = sum_ref[...]

    def make(n):
        code = items_ref[n + 1]
        own, other = item_blocks(code)
        make_tile(kept_ref, n, spread_ref, other, points_ref, own, *item_shifts(code))

    in_turns(items_ref[0], make)
    only_use(items_ref[0], kept_ref, functools.partial(use_pair, out_ref, parts_ref, items_ref))


def take_round(round_refs, rhs, parts_ref, points_ref=None):
    start = 0
    for side in round_refs:

        def take(at, carry, side=side, start=start):
            store_parts(parts_ref, start + at, side[at, 0:rhs])
            if points_ref is not None:
                points_ref[start + at] = side[at, rhs : rhs + 2] * UNIT
            return carry

        lax.fori_loop(0, side.shape[0], take, 0)
        start += side.shape[0]


def cross_first_kernel(
    items_ref, sum_ref, west_ref, east_ref, north_ref, south_ref, spread_ref,
    out_ref, kept_ref, parts_ref, points_ref
):
    out_ref[...] = sum_ref[...]
    take_round((west_ref, east_ref, north_ref, south_ref), sum_ref.shape[1], parts_ref, points_ref)

    def make(n):
        code = items_ref[n + 1]
        own, other = item_blocks(code)
        make_tile(kept_ref, n, spread_ref, own, points_ref, other, *item_shifts(code))

    in_turns(items_ref[0], make)
    only_use(items_ref[0], kept_ref, functools.partial(use_cross, out_ref, parts_ref, items_ref))


def inner_again_kernel(items_ref, v_ref, kept_ref, out_ref, parts_ref):
    def one(at, carry):
        store_parts(parts_ref, at, v_ref[at])
        out_ref[at] = NUGGET * v_ref[at]
        return carry

    lax.fori_loop(0, parts_ref.shape[0], one, 0, unroll=2)
    only_use(items_ref[0], kept_ref, functools.partial(use_pair, out_ref, parts_ref, items_ref))


def own_again_kernel(sum_ref, parts_ref, kept_ref, out_ref):
    out_ref[...] = sum_ref[...]
    only_use(jnp.int32(parts_ref.shape[0]), kept_ref, functools.partial(use_own, out_ref, parts_ref))


def cross_again_kernel(
    items_ref, sum_ref, west_ref, east_ref, north_ref, south_ref, kept_ref, v0_ref, v1_ref,
    out_ref, moments_ref, parts_ref
):
    out_ref[...] = sum_ref[...]
    take_round((west_ref, east_ref, north_ref, south_ref), sum_ref.shape[1], parts_ref)
    only_use(items_ref[0], kept_ref, functools.partial(use_cross, out_ref, parts_ref, items_ref))
    zero = jnp.zeros(out_ref.shape[1:], jnp.float32)

    def gather(at, sums):
        w0, w1, w2 = v0_ref[at], v1_ref[at], out_ref[at]
        terms = (w0 * w0, w0 * w1, w1 * w1, w1 * w2)
        return tuple(s + t for s, t in zip(sums, terms))

    sums = lax.fori_loop(0, out_ref.shape[0], gather, (zero,) * 4)
    lanes = moments_ref.shape[2]
    folded = [sum(s[:, left : left + lanes] for left in range(0, s.shape[1], lanes)) for s in sums]
    stacked = jnp.concatenate(folded, axis=0)
    line = jnp.sum(jnp.transpose(stacked), axis=0, keepdims=True)
    moments_ref[...] = jnp.broadcast_to(line[None], moments_ref.shape)


def final_kernel(moments_ref, v0_ref, v1_ref, v2_ref, solution_ref, residual_ref):
    rhs, points = v0_ref.shape[1:]
    line = moments_ref[0]
    for at in range(1, moments_ref.shape[0]):
        line = line + moments_ref[at]
    table = across_lanes(line, line.shape[1])
    m00, m01, m11, m12 = (table[k * rhs : (k + 1) * rhs] for k in range(4))
    a = m00 / m01
    norm = m00 - 2.0 * a * m01 + a * a * m11
    grow = 1.0 + norm / m00
    step = norm / (grow * (grow * m01 - 2.0 * a * m11) + a * a * m12)
    first = jnp.concatenate([a + step * grow] * (points // line.shape[1]), axis=1)
    second = jnp.concatenate([step * a] * (points // line.shape[1]), axis=1)

    def one(at, carry):
        w0, w1, w2 = v0_ref[at], v1_ref[at], v2_ref[at]
        solution_ref[at] = first * w0 - second * w1
        residual_ref[at] = w0 - first * w1 + second * w2
        return carry

    lax.fori_loop(0, v0_ref.shape[0], one, 0)


def swapped(first, last, axis):
    count = lax.axis_size(axis)
    even = lax.rem(lax.axis_index(axis), 2) == 0
    swap_up = [(i, i ^ 1) for i in range(count) if i ^ 1 < count]
    swap_down = [(i, ((i + 1) ^ 1) - 1) for i in range(count) if 0 <= ((i + 1) ^ 1) - 1 < count]
    got_up = lax.ppermute(jnp.where(even, last, first), axis, swap_up)
    got_down = lax.ppermute(jnp.where(even, first, last), axis, swap_down)
    return jnp.where(even, got_down, got_up), jnp.where(even, got_up, got_down)


def on_device(kernel, outputs, inputs, scratch=(), listed=False, products=0, made=0, where=pltpu.VMEM):
    vmem = pl.BlockSpec(memory_space=pltpu.VMEM)
    smem = pl.BlockSpec(memory_space=pltpu.SMEM)
    source = pl.BlockSpec(memory_space=where)
    return pl.pallas_call(
        kernel,
        out_shape=tuple(outputs),
        in_specs=[smem if listed and n == 0 else source for n in range(len(inputs))],
        out_specs=tuple(smem if out.dtype == jnp.int32 else vmem for out in outputs),
        scratch_shapes=list(scratch),
        compiler_params=pltpu.CompilerParams(vmem_limit_bytes=VMEM_LIMIT),
        cost_estimate=pl.CostEstimate(
            flops=products, transcendentals=made, bytes_accessed=sum(4 * x.size for x in inputs)
        ),
        name=kernel.__name__,
    )(*inputs)


def tiles(count, points):
    return jax.ShapeDtypeStruct((count, 2, points, points), jnp.bfloat16)


def per_device(right_side, coords, pair_list):
    pair_list = jnp.transpose(pair_list, (1, 2, 0))
    rows, cols, rhs, points = right_side.shape
    blocks = rows * cols
    devices = lax.axis_size("region") * lax.axis_size("tile")
    lanes = 128
    f32, bf16, i32 = jnp.float32, jnp.bfloat16, jnp.int32
    array = jax.ShapeDtypeStruct
    halo = 2 * rows + 2 * (cols + 2)
    near_count = len(inner_candidates(rows, cols))
    cross_count = len(cross_candidates(rows, cols))
    field = array((blocks, rhs, points), f32)
    column = array((rows, rhs + 2, points), f32)
    parts_round = pltpu.VMEM((halo, 2 * rhs, points), bf16)
    each = 6 * rhs * points * points

    def rows_round(first, last, west, east):
        top = jnp.concatenate([west[:1], first, east[:1]], axis=0)
        bottom = jnp.concatenate([west[rows - 1 :], last, east[rows - 1 :]], axis=0)
        return swapped(top, bottom, "region")

    fetched = (
        column, column, array((2, cols, rhs + 2, points), f32), field, array((blocks, 2, points), f32),
        array(pair_list.shape, i32),
    )
    first, last, edges, w0, stations, pairs = on_device(
        pack_kernel, fetched,
        tuple(pltpu.with_memory_space_constraint(x, pltpu.HBM) for x in (right_side, coords, pair_list)),
        (pltpu.SemaphoreType.DMA((2 * rows + 1,)),), where=pltpu.HBM,
    )
    west, east = swapped(first, last, "tile")
    parts_field = array((blocks, 2 * rhs, points), bf16)
    near_items, cross_items, part, own_tiles, parts, own_points, spread = on_device(
        own_first_kernel,
        (array((near_count + 3,), i32), array((cross_count + 3,), i32), field, tiles(blocks, points), parts_field,
         array((blocks, 2, points), f32), array((blocks, 2, points, lanes), f32)),
        (pairs, w0, stations), listed=True, products=blocks * each, made=blocks * 2 * points * points,
    )
    west, east, part = lax.optimization_barrier((west, east, part))
    north, south = rows_round(edges[0], edges[1], west, east)
    part, near_tiles = on_device(
        inner_first_kernel, (field, tiles(near_count + 2, points)), (near_items, part, parts, own_points, spread),
        (), True, near_count * each, near_count * 2 * points * points,
    )
    w1, cross_tiles = on_device(
        cross_first_kernel, (field, tiles(cross_count + 2, points)),
        (cross_items, part, west, east, north, south, spread),
        (parts_round, pltpu.VMEM((halo, 2, points), f32)), True,
        cross_count * each, cross_count * 2 * points * points,
    )
    w1_grid = w1.reshape(right_side.shape)
    west, east = swapped(w1_grid[:, 0], w1_grid[:, cols - 1], "tile")
    part, parts = on_device(
        inner_again_kernel, (field, parts_field), (near_items, w1, near_tiles), (), True, near_count * each
    )
    west, east, part = lax.optimization_barrier((west, east, part))
    north, south = rows_round(w1_grid[0], w1_grid[rows - 1], west, east)
    (part,) = on_device(own_again_kernel, (field,), (part, parts, own_tiles), products=blocks * each)
    w2, moments = on_device(
        cross_again_kernel, (field, array((devices, 1, 4 * rhs), f32)),
        (cross_items, part, west, east, north, south, cross_tiles, w0, w1), (parts_round,), True, cross_count * each,
    )
    moments = lax.all_to_all(moments, ("region", "tile"), 0, 0)
    solution, residual = on_device(final_kernel, (field, field), (moments, w0, w1, w2))
    return solution.reshape(right_side.shape), residual.reshape(right_side.shape)


def solution(mesh):
    placed = (
        P("region", "tile", None, None),
        P("region", "tile", None, None),
        P(None, "region", "tile"),
    )
    return jax.shard_map(
        per_device,
        mesh=mesh,
        in_specs=placed,
        out_specs=(P("region", "tile", None, None), P("region", "tile", None, None)),
        check_vma=False,
    )
```

```python
import functools

import jax
import jax.numpy as jnp
from jax import lax
from jax.experimental import pallas as pl
from jax.experimental.pallas import tpu as pltpu
from jax.sharding import PartitionSpec as P

LENGTH_SCALE = 0.2
TAPER_RANGE = 0.5
NUGGET = 3.0
OFFSETS = ((0, 1), (1, 0), (1, 1), (1, -1), (0, -1), (-1, 0), (-1, -1), (-1, 1))
UNIT = 1.4426950408889634 / LENGTH_SCALE
EDGE = UNIT * TAPER_RANGE
WEIGHT = 4.0 * 2.0**-EDGE / EDGE**5
STRIP = 64
LONG_TURN_LOG2 = 3
VMEM_LIMIT = 10 * 1024 * 1024


def dot_nn(a, b):
    return lax.dot_general(a, b, (((1,), (0,)), ((), ())), preferred_element_type=jnp.float32)


def dot_nt(a, b):
    return lax.dot_general(a, b, (((1,), (1,)), ((), ())), preferred_element_type=jnp.float32)


def split_hi_lo(values):
    hi = values.astype(jnp.bfloat16)
    lo = (values - hi.astype(jnp.float32)).astype(jnp.bfloat16)
    return hi, lo


def across_lanes(row, lanes):
    return jnp.transpose(jnp.broadcast_to(row, (lanes, row.shape[1])))


def make_tile(keep_ref, slot, spread_ref, down, points_ref, along, shift_a, shift_b):
    points = keep_ref.shape[2]
    lanes = spread_ref.shape[3]
    row_x = points_ref[along, 0:1] - shift_a
    row_y = points_ref[along, 1:2] - shift_b
    for start in range(0, points, STRIP):
        rows = slice(start, start + STRIP)
        for left in range(0, points, lanes):
            cols = slice(left, left + lanes)
            gap_x = spread_ref[down, 0, rows] - row_x[:, cols]
            gap_y = spread_ref[down, 1, rows] - row_y[:, cols]
            square = jnp.maximum(gap_x * gap_x + gap_y * gap_y, 1e-30)
            rest = jnp.maximum(EDGE - square * lax.rsqrt(square), 0.0)
            rest2 = rest * rest
            cov = (jnp.exp2(rest) * (rest2 * rest2)) * (1.25 * EDGE - rest)
            for part, values in enumerate(split_hi_lo(cov)):
                keep_ref[slot, part, rows, cols] = values


def product(dot, parts_ref, at, high, low):
    rhs = parts_ref.shape[1] // 2
    both = dot(parts_ref[at], high)
    cross = dot(parts_ref[at, 0:rhs], low)
    return both[:rhs] + both[rhs:] + cross


def store_parts(parts_ref, at, values):
    rhs = values.shape[0]
    hi, lo = split_hi_lo(values * WEIGHT)
    parts_ref[at, 0:rhs] = hi
    parts_ref[at, rhs : 2 * rhs] = lo


def in_turns(count, step):
    turns = lax.shift_right_logical(count + 1, 1)

    def one_turn(turn, carry):
        step(2 * turn)
        step(2 * turn + 1)
        return carry

    lax.fori_loop(0, turns, one_turn, 0)


def only_use(count, kept_ref, use):
    def one_turn(start, length):
        for n in range(length):
            use(kept_ref[start + n, 0], kept_ref[start + n, 1], start + n)

    whole = lax.shift_right_logical(count, LONG_TURN_LOG2)
    lax.fori_loop(0, whole, lambda turn, c: (one_turn(turn << LONG_TURN_LOG2, 1 << LONG_TURN_LOG2), c)[1], 0)
    lax.fori_loop(whole << LONG_TURN_LOG2, count, lambda n, c: (one_turn(n, 1), c)[1], 0)


def item_code(own, other, shift_a, shift_b):
    return own + 64 * other + 4096 * (shift_a + 1) + 16384 * (shift_b + 1)


NO_ITEM = item_code(0, 0, 2, 2)


def item_blocks(code):
    return lax.bitwise_and(code, 63), lax.bitwise_and(lax.shift_right_logical(code, 6), 63)


def item_shifts(code):
    shift_a = lax.bitwise_and(lax.shift_right_logical(code, 12), 3) - 1
    shift_b = lax.shift_right_logical(code, 14) - 1
    return shift_a.astype(jnp.float32) * UNIT, shift_b.astype(jnp.float32) * UNIT


def list_items(items_ref, candidates, pair_ref):
    cols = pair_ref.shape[1]
    count = jnp.int32(0)
    for k, own, code in candidates:
        items_ref[count + 1] = code
        count = count + jnp.where(pair_ref[own // cols, own % cols, k] > 0, 1, 0)
    items_ref[0] = count
    items_ref[count + 1] = NO_ITEM


def inner_candidates(rows, cols):
    found = []
    for k in range(4):
        shift_a, shift_b = OFFSETS[k]
        for a in range(rows):
            for b in range(cols):
                if 0 <= a + shift_a < rows and 0 <= b + shift_b < cols:
                    own = a * cols + b
                    other = own + shift_a * cols + shift_b
                    found.append((k, own, item_code(own, other, shift_a, shift_b)))
    return found


def cross_candidates(rows, cols):
    places = [(a, -1) for a in range(rows)] + [(a, cols) for a in range(rows)]
    places += [(-1, b) for b in range(-1, cols + 1)] + [(rows, b) for b in range(-1, cols + 1)]
    found = []
    for k in range(8):
        shift_a, shift_b = OFFSETS[k]
        for a in range(rows):
            for b in range(cols):
                place = (a + shift_a, b + shift_b)
                if place in places:
                    own = a * cols + b
                    found.append((k, own, item_code(own, places.index(place), -shift_a, -shift_b)))
    return found


def pack_kernel(v_hbm, c_hbm, pair_hbm, first_ref, last_ref, edge_ref, v_ref, c_ref, pair_ref, sems):
    rows, cols, rhs = v_hbm.shape[:3]
    fetches = []
    for row in range(rows):
        own = pl.ds(row * cols, cols)
        fetches.append(pltpu.make_async_copy(v_hbm.at[row], v_ref.at[own], sems.at[2 * row]))
        fetches.append(pltpu.make_async_copy(c_hbm.at[row], c_ref.at[own], sems.at[2 * row + 1]))
    fetches.append(pltpu.make_async_copy(pair_hbm, pair_ref, sems.at[2 * rows]))
    for fetch in fetches:
        fetch.start()
    for fetch in fetches:
        fetch.wait()
    both = slice(rhs, rhs + 2)
    for row in range(rows):
        for column_ref, at in ((first_ref, row * cols), (last_ref, row * cols + cols - 1)):
            column_ref[row, 0:rhs] = v_ref[at]
            column_ref[row, both] = c_ref[at]
    for n, row in enumerate((0, rows - 1)):
        own = slice(row * cols, (row + 1) * cols)
        edge_ref[n, :, 0:rhs] = v_ref[own]
        edge_ref[n, :, both] = c_ref[own]


def use_own(out_ref, parts_ref, high, low, at):
    out_ref[at] += product(dot_nn, parts_ref, at, high, low)


def use_pair(out_ref, parts_ref, items_ref, high, low, n):
    own, other = item_blocks(items_ref[n + 1])
    out_ref[own] += product(dot_nn, parts_ref, other, high, low)
    out_ref[other] += product(dot_nt, parts_ref, own, high, low)


def use_cross(out_ref, parts_ref, items_ref, high, low, n):
    own, other = item_blocks(items_ref[n + 1])
    out_ref[own] += product(dot_nt, parts_ref, other, high, low)


def own_first_kernel(
    pair_ref, v_ref, c_ref, near_ref, cross_ref, out_ref, kept_ref, parts_ref, points_ref, spread_ref
):
    rows, cols = pair_ref.shape[:2]
    lanes = spread_ref.shape[3]

    def one(at):
        store_parts(parts_ref, at, v_ref[at])
        out_ref[at] = NUGGET * v_ref[at]
        scaled = c_ref[at] * UNIT
        points_ref[at] = scaled
        for axis in range(2):
            spread_ref[at, axis] = across_lanes(scaled[axis : axis + 1], lanes)
        make_tile(kept_ref, at, spread_ref, at, points_ref, at, 0.0, 0.0)

    def one_pair(turn, carry):
        one(2 * turn)
        one(2 * turn + 1)
        return carry

    lax.fori_loop(0, rows * cols // 2, one_pair, 0)
    only_use(jnp.int32(rows * cols), kept_ref, functools.partial(use_own, out_ref, parts_ref))
    list_items(near_ref, inner_candidates(rows, cols), pair_ref)
    list_items(cross_ref, cross_candidates(rows, cols), pair_ref)


def inner_first_kernel(items_ref, sum_ref, parts_ref, points_ref, spread_ref, out_ref, kept_ref):
    out_ref[...] = sum_ref[...]

    def make(n):
        code = items_ref[n + 1]
        own, other = item_blocks(code)
        make_tile(kept_ref, n, spread_ref, other, points_ref, own, *item_shifts(code))

    in_turns(items_ref[0], make)
    only_use(items_ref[0], kept_ref, functools.partial(use_pair, out_ref, parts_ref, items_ref))


def take_round(round_refs, rhs, parts_ref, points_ref=None):
    start = 0
    for side in round_refs:

        def take(at, carry, side=side, start=start):
            store_parts(parts_ref, start + at, side[at, 0:rhs])
            if points_ref is not None:
                points_ref[start + at] = side[at, rhs : rhs + 2] * UNIT
            return carry

        lax.fori_loop(0, side.shape[0], take, 0)
        start += side.shape[0]


def cross_first_kernel(
    items_ref, sum_ref, west_ref, east_ref, north_ref, south_ref, spread_ref,
    out_ref, kept_ref, parts_ref, points_ref
):
    out_ref[...] = sum_ref[...]
    take_round((west_ref, east_ref, north_ref, south_ref), sum_ref.shape[1], parts_ref, points_ref)

    def make(n):
        code = items_ref[n + 1]
        own, other = item_blocks(code)
        make_tile(kept_ref, n, spread_ref, own, points_ref, other, *item_shifts(code))

    in_turns(items_ref[0], make)
    only_use(items_ref[0], kept_ref, functools.partial(use_cross, out_ref, parts_ref, items_ref))


def own_again_kernel(v_ref, kept_ref, out_ref, parts_ref):
    def one(at, carry):
        store_parts(parts_ref, at, v_ref[at])
        out_ref[at] = NUGGET * v_ref[at]
        return carry

    lax.fori_loop(0, parts_ref.shape[0], one, 0, unroll=2)
    only_use(jnp.int32(parts_ref.shape[0]), kept_ref, functools.partial(use_own, out_ref, parts_ref))


def inner_again_kernel(items_ref, sum_ref, parts_ref, kept_ref, out_ref):
    out_ref[...] = sum_ref[...]
    only_use(items_ref[0], kept_ref, functools.partial(use_pair, out_ref, parts_ref, items_ref))


def cross_again_kernel(
    items_ref, sum_ref, west_ref, east_ref, north_ref, south_ref, kept_ref, v0_ref, v1_ref,
    out_ref, moments_ref, parts_ref
):
    out_ref[...] = sum_ref[...]
    take_round((west_ref, east_ref, north_ref, south_ref), sum_ref.shape[1], parts_ref)
    only_use(items_ref[0], kept_ref, functools.partial(use_cross, out_ref, parts_ref, items_ref))
    zero = jnp.zeros(out_ref.shape[1:], jnp.float32)

    def gather(at, sums):
        w0, w1, w2 = v0_ref[at], v1_ref[at], out_ref[at]
        terms = (w0 * w0, w0 * w1, w1 * w1, w1 * w2)
        return tuple(s + t for s, t in zip(sums, terms))

    sums = lax.fori_loop(0, out_ref.shape[0], gather, (zero,) * 4)
    lanes = moments_ref.shape[2]
    folded = [sum(s[:, left : left + lanes] for left in range(0, s.shape[1], lanes)) for s in sums]
    stacked = jnp.concatenate(folded, axis=0)
    line = jnp.sum(jnp.transpose(stacked), axis=0, keepdims=True)
    moments_ref[...] = jnp.broadcast_to(line[None], moments_ref.shape)


def final_kernel(moments_ref, v0_ref, v1_ref, v2_ref, solution_ref, residual_ref):
    rhs, points = v0_ref.shape[1:]
    line = moments_ref[0]
    for at in range(1, moments_ref.shape[0]):
        line = line + moments_ref[at]
    table = across_lanes(line, line.shape[1])
    m00, m01, m11, m12 = (table[k * rhs : (k + 1) * rhs] for k in range(4))
    a = m00 / m01
    norm = m00 - 2.0 * a * m01 + a * a * m11
    grow = 1.0 + norm / m00
    step = norm / (grow * (grow * m01 - 2.0 * a * m11) + a * a * m12)
    first = jnp.concatenate([a + step * grow] * (points // line.shape[1]), axis=1)
    second = jnp.concatenate([step * a] * (points // line.shape[1]), axis=1)

    def one(at, carry):
        w0, w1, w2 = v0_ref[at], v1_ref[at], v2_ref[at]
        solution_ref[at] = first * w0 - second * w1
        residual_ref[at] = w0 - first * w1 + second * w2
        return carry

    lax.fori_loop(0, v0_ref.shape[0], one, 0)


def swapped(first, last, axis):
    count = lax.axis_size(axis)
    even = lax.rem(lax.axis_index(axis), 2) == 0
    swap_up = [(i, i ^ 1) for i in range(count) if i ^ 1 < count]
    swap_down = [(i, ((i + 1) ^ 1) - 1) for i in range(count) if 0 <= ((i + 1) ^ 1) - 1 < count]
    got_up = lax.ppermute(jnp.where(even, last, first), axis, swap_up)
    got_down = lax.ppermute(jnp.where(even, first, last), axis, swap_down)
    return jnp.where(even, got_down, got_up), jnp.where(even, got_up, got_down)


def on_device(kernel, outputs, inputs, scratch=(), listed=False, products=0, made=0, where=pltpu.VMEM):
    vmem = pl.BlockSpec(memory_space=pltpu.VMEM)
    smem = pl.BlockSpec(memory_space=pltpu.SMEM)
    source = pl.BlockSpec(memory_space=where)
    return pl.pallas_call(
        kernel,
        out_shape=tuple(outputs),
        in_specs=[smem if listed and n == 0 else source for n in range(len(inputs))],
        out_specs=tuple(smem if out.dtype == jnp.int32 else vmem for out in outputs),
        scratch_shapes=list(scratch),
        compiler_params=pltpu.CompilerParams(vmem_limit_bytes=VMEM_LIMIT),
        cost_estimate=pl.CostEstimate(
            flops=products, transcendentals=made, bytes_accessed=sum(4 * x.size for x in inputs)
        ),
        name=kernel.__name__,
    )(*inputs)


def tiles(count, points):
    return jax.ShapeDtypeStruct((count, 2, points, points), jnp.bfloat16)


def per_device(right_side, coords, pair_list):
    pair_list = jnp.transpose(pair_list, (1, 2, 0))
    rows, cols, rhs, points = right_side.shape
    blocks = rows * cols
    devices = lax.axis_size("region") * lax.axis_size("tile")
    lanes = 128
    f32, bf16, i32 = jnp.float32, jnp.bfloat16, jnp.int32
    array = jax.ShapeDtypeStruct
    halo = 2 * rows + 2 * (cols + 2)
    near_count = len(inner_candidates(rows, cols))
    cross_count = len(cross_candidates(rows, cols))
    field = array((blocks, rhs, points), f32)
    column = array((rows, rhs + 2, points), f32)
    parts_round = pltpu.VMEM((halo, 2 * rhs, points), bf16)
    each = 6 * rhs * points * points

    def rows_round(first, last, west, east):
        top = jnp.concatenate([west[:1], first, east[:1]], axis=0)
        bottom = jnp.concatenate([west[rows - 1 :], last, east[rows - 1 :]], axis=0)
        return swapped(top, bottom, "region")

    fetched = (
        column, column, array((2, cols, rhs + 2, points), f32), field, array((blocks, 2, points), f32),
        array(pair_list.shape, i32),
    )
    first, last, edges, w0, stations, pairs = on_device(
        pack_kernel, fetched,
        tuple(pltpu.with_memory_space_constraint(x, pltpu.HBM) for x in (right_side, coords, pair_list)),
        (pltpu.SemaphoreType.DMA((2 * rows + 1,)),), where=pltpu.HBM,
    )
    west, east = swapped(first, last, "tile")
    parts_field = array((blocks, 2 * rhs, points), bf16)
    near_items, cross_items, part, own_tiles, parts, own_points, spread = on_device(
        own_first_kernel,
        (array((near_count + 3,), i32), array((cross_count + 3,), i32), field, tiles(blocks, points), parts_field,
         array((blocks, 2, points), f32), array((blocks, 2, points, lanes), f32)),
        (pairs, w0, stations), listed=True, products=blocks * each, made=blocks * 2 * points * points,
    )
    west, east, part = lax.optimization_barrier((west, east, part))
    north, south = rows_round(edges[0], edges[1], west, east)
    part, near_tiles = on_device(
        inner_first_kernel, (field, tiles(near_count + 2, points)), (near_items, part, parts, own_points, spread),
        (), True, near_count * each, near_count * 2 * points * points,
    )
    w1, cross_tiles = on_device(
        cross_first_kernel, (field, tiles(cross_count + 2, points)),
        (cross_items, part, west, east, north, south, spread),
        (parts_round, pltpu.VMEM((halo, 2, points), f32)), True,
        cross_count * each, cross_count * 2 * points * points,
    )
    w1_grid = w1.reshape(right_side.shape)
    west, east = swapped(w1_grid[:, 0], w1_grid[:, cols - 1], "tile")
    part, parts = on_device(own_again_kernel, (field, parts_field), (w1, own_tiles), products=blocks * each)
    west, east, part = lax.optimization_barrier((west, east, part))
    north, south = rows_round(w1_grid[0], w1_grid[rows - 1], west, east)
    (part,) = on_device(
        inner_again_kernel, (field,), (near_items, part, parts, near_tiles), (), True, near_count * each
    )
    w2, moments = on_device(
        cross_again_kernel, (field, array((devices, 1, 4 * rhs), f32)),
        (cross_items, part, west, east, north, south, cross_tiles, w0, w1), (parts_round,), True, cross_count * each,
    )
    moments = lax.all_to_all(moments, ("region", "tile"), 0, 0)
    solution, residual = on_device(final_kernel, (field, field), (moments, w0, w1, w2))
    return solution.reshape(right_side.shape), residual.reshape(right_side.shape)


def solution(mesh):
    placed = (
        P("region", "tile", None, None),
        P("region", "tile", None, None),
        P(None, "region", "tile"),
    )
    return jax.shard_map(
        per_device,
        mesh=mesh,
        in_specs=placed,
        out_specs=(P("region", "tile", None, None), P("region", "tile", None, None)),
        check_vma=False,
    )
```

```python
import functools

import jax
import jax.numpy as jnp
from jax import lax
from jax.experimental import pallas as pl
from jax.experimental.pallas import tpu as pltpu
from jax.sharding import PartitionSpec as P

LENGTH_SCALE = 0.2
TAPER_RANGE = 0.5
NUGGET = 3.0
OFFSETS = ((0, 1), (1, 0), (1, 1), (1, -1), (0, -1), (-1, 0), (-1, -1), (-1, 1))
UNIT = 1.4426950408889634 / LENGTH_SCALE
EDGE = UNIT * TAPER_RANGE
WEIGHT = 4.0 * 2.0**-EDGE / EDGE**5
STRIP = 64
LONG_TURN_LOG2 = 3
VMEM_LIMIT = 10 * 1024 * 1024


def dot_nn(a, b):
    return lax.dot_general(a, b, (((1,), (0,)), ((), ())), preferred_element_type=jnp.float32)


def dot_nt(a, b):
    return lax.dot_general(a, b, (((1,), (1,)), ((), ())), preferred_element_type=jnp.float32)


def split_hi_lo(values):
    hi = values.astype(jnp.bfloat16)
    lo = (values - hi.astype(jnp.float32)).astype(jnp.bfloat16)
    return hi, lo


def across_lanes(row, lanes):
    return jnp.transpose(jnp.broadcast_to(row, (lanes, row.shape[1])))


def make_tile(keep_ref, slot, spread_ref, down, points_ref, along, shift_a, shift_b):
    points = keep_ref.shape[2]
    lanes = spread_ref.shape[3]
    row_x = points_ref[along, 0:1] - shift_a
    row_y = points_ref[along, 1:2] - shift_b
    for start in range(0, points, STRIP):
        rows = slice(start, start + STRIP)
        for left in range(0, points, lanes):
            cols = slice(left, left + lanes)
            gap_x = spread_ref[down, 0, rows] - row_x[:, cols]
            gap_y = spread_ref[down, 1, rows] - row_y[:, cols]
            square = jnp.maximum(gap_x * gap_x + gap_y * gap_y, 1e-30)
            rest = jnp.maximum(EDGE - square * lax.rsqrt(square), 0.0)
            rest2 = rest * rest
            cov = (jnp.exp2(rest) * (rest2 * rest2)) * (1.25 * EDGE - rest)
            for part, values in enumerate(split_hi_lo(cov)):
                keep_ref[slot, part, rows, cols] = values


def product(dot, parts_ref, at, high, low):
    rhs = parts_ref.shape[1] // 2
    both = dot(parts_ref[at], high)
    cross = dot(parts_ref[at, 0:rhs], low)
    return both[:rhs] + both[rhs:] + cross


def store_parts(parts_ref, at, values):
    rhs = values.shape[0]
    hi, lo = split_hi_lo(values * WEIGHT)
    parts_ref[at, 0:rhs] = hi
    parts_ref[at, rhs : 2 * rhs] = lo


def in_turns(count, step):
    turns = lax.shift_right_logical(count + 1, 1)

    def one_turn(turn, carry):
        step(2 * turn)
        step(2 * turn + 1)
        return carry

    lax.fori_loop(0, turns, one_turn, 0)


def only_use(first, last, kept_ref, use):
    def one_turn(start, length):
        for n in range(length):
            use(kept_ref[start + n, 0], kept_ref[start + n, 1], start + n)

    whole = lax.shift_right_logical(last - first, LONG_TURN_LOG2)
    lax.fori_loop(0, whole, lambda turn, c: (one_turn(first + (turn << LONG_TURN_LOG2), 1 << LONG_TURN_LOG2), c)[1], 0)
    lax.fori_loop(first + (whole << LONG_TURN_LOG2), last, lambda n, c: (one_turn(n, 1), c)[1], 0)


def item_code(own, other, shift_a, shift_b):
    return own + 64 * other + 4096 * (shift_a + 1) + 16384 * (shift_b + 1)


NO_ITEM = item_code(0, 0, 2, 2)


def item_blocks(code):
    return lax.bitwise_and(code, 63), lax.bitwise_and(lax.shift_right_logical(code, 6), 63)


def item_shifts(code):
    shift_a = lax.bitwise_and(lax.shift_right_logical(code, 12), 3) - 1
    shift_b = lax.shift_right_logical(code, 14) - 1
    return shift_a.astype(jnp.float32) * UNIT, shift_b.astype(jnp.float32) * UNIT


def list_items(items_ref, candidates, pair_ref):
    cols = pair_ref.shape[1]
    count = jnp.int32(0)
    for k, own, code in candidates:
        items_ref[count + 1] = code
        count = count + jnp.where(pair_ref[own // cols, own % cols, k] > 0, 1, 0)
    items_ref[0] = count
    items_ref[count + 1] = NO_ITEM


def inner_candidates(rows, cols):
    found = []
    for k in range(4):
        shift_a, shift_b = OFFSETS[k]
        for a in range(rows):
            for b in range(cols):
                if 0 <= a + shift_a < rows and 0 <= b + shift_b < cols:
                    own = a * cols + b
                    other = own + shift_a * cols + shift_b
                    found.append((k, own, item_code(own, other, shift_a, shift_b)))
    return found


def cross_candidates(rows, cols):
    places = [(-1, b) for b in range(cols)] + [(rows, b) for b in range(cols)]
    places += [(a, -1) for a in range(-1, rows + 1)] + [(a, cols) for a in range(-1, rows + 1)]
    found = []
    for k in range(8):
        shift_a, shift_b = OFFSETS[k]
        for a in range(rows):
            for b in range(cols):
                place = (a + shift_a, b + shift_b)
                if place in places:
                    own = a * cols + b
                    found.append((k, own, item_code(own, places.index(place), -shift_a, -shift_b)))
    return found


def pack_kernel(v_hbm, c_hbm, pair_hbm, first_ref, last_ref, edge_ref, v_ref, c_ref, pair_ref, sems):
    rows, cols, rhs = v_hbm.shape[:3]
    fetches = []
    for row in range(rows):
        own = pl.ds(row * cols, cols)
        fetches.append(pltpu.make_async_copy(v_hbm.at[row], v_ref.at[own], sems.at[2 * row]))
        fetches.append(pltpu.make_async_copy(c_hbm.at[row], c_ref.at[own], sems.at[2 * row + 1]))
    fetches.append(pltpu.make_async_copy(pair_hbm, pair_ref, sems.at[2 * rows]))
    for fetch in fetches:
        fetch.start()
    for fetch in fetches:
        fetch.wait()
    both = slice(rhs, rhs + 2)
    for row in range(rows):
        for column_ref, at in ((first_ref, row * cols), (last_ref, row * cols + cols - 1)):
            column_ref[row, 0:rhs] = v_ref[at]
            column_ref[row, both] = c_ref[at]
    for n, row in enumerate((0, rows - 1)):
        own = slice(row * cols, (row + 1) * cols)
        edge_ref[n, :, 0:rhs] = v_ref[own]
        edge_ref[n, :, both] = c_ref[own]


def use_own(out_ref, parts_ref, high, low, at):
    out_ref[at] += product(dot_nn, parts_ref, at, high, low)


def use_pair(out_ref, parts_ref, items_ref, high, low, n):
    own, other = item_blocks(items_ref[n + 1])
    out_ref[own] += product(dot_nn, parts_ref, other, high, low)
    out_ref[other] += product(dot_nt, parts_ref, own, high, low)


def use_cross(out_ref, parts_ref, items_ref, high, low, n):
    own, other = item_blocks(items_ref[n + 1])
    out_ref[own] += product(dot_nt, parts_ref, other, high, low)


def own_first_kernel(
    pair_ref, v_ref, c_ref, near_ref, cross_ref, out_ref, kept_ref, parts_ref, points_ref, spread_ref
):
    rows, cols = pair_ref.shape[:2]
    lanes = spread_ref.shape[3]

    def one(at):
        store_parts(parts_ref, at, v_ref[at])
        out_ref[at] = NUGGET * v_ref[at]
        scaled = c_ref[at] * UNIT
        points_ref[at] = scaled
        for axis in range(2):
            spread_ref[at, axis] = across_lanes(scaled[axis : axis + 1], lanes)
        make_tile(kept_ref, at, spread_ref, at, points_ref, at, 0.0, 0.0)

    def one_pair(turn, carry):
        one(2 * turn)
        one(2 * turn + 1)
        return carry

    lax.fori_loop(0, rows * cols // 2, one_pair, 0)
    only_use(0, jnp.int32(rows * cols), kept_ref, functools.partial(use_own, out_ref, parts_ref))
    list_items(near_ref, inner_candidates(rows, cols), pair_ref)
    list_items(cross_ref, cross_candidates(rows, cols), pair_ref)


def inner_first_kernel(items_ref, sum_ref, parts_ref, points_ref, spread_ref, out_ref, kept_ref):
    out_ref[...] = sum_ref[...]

    def make(n):
        code = items_ref[n + 1]
        own, other = item_blocks(code)
        make_tile(kept_ref, n, spread_ref, other, points_ref, own, *item_shifts(code))

    in_turns(items_ref[0], make)
    only_use(0, items_ref[0], kept_ref, functools.partial(use_pair, out_ref, parts_ref, items_ref))


def take_round(round_refs, rhs, parts_ref, points_ref=None):
    start = 0
    for side in round_refs:

        def take(at, carry, side=side, start=start):
            store_parts(parts_ref, start + at, side[at, 0:rhs])
            if points_ref is not None:
                points_ref[start + at] = side[at, rhs : rhs + 2] * UNIT
            return carry

        lax.fori_loop(0, side.shape[0], take, 0)
        start += side.shape[0]


def cross_first_kernel(
    items_ref, sum_ref, north_ref, south_ref, west_ref, east_ref, spread_ref,
    out_ref, kept_ref, parts_ref, points_ref
):
    out_ref[...] = sum_ref[...]
    take_round((north_ref, south_ref, west_ref, east_ref), sum_ref.shape[1], parts_ref, points_ref)

    def make(n):
        code = items_ref[n + 1]
        own, other = item_blocks(code)
        make_tile(kept_ref, n, spread_ref, own, points_ref, other, *item_shifts(code))

    in_turns(items_ref[0], make)
    only_use(0, items_ref[0], kept_ref, functools.partial(use_cross, out_ref, parts_ref, items_ref))


def first_share(count):
    return lax.shift_right_logical(5 * count, 3)


def near_again_kernel(items_ref, v_ref, own_ref, kept_ref, out_ref, parts_ref):
    def one(at, carry):
        store_parts(parts_ref, at, v_ref[at])
        out_ref[at] = NUGGET * v_ref[at]
        return carry

    lax.fori_loop(0, parts_ref.shape[0], one, 0, unroll=2)
    only_use(0, jnp.int32(parts_ref.shape[0]), own_ref, functools.partial(use_own, out_ref, parts_ref))
    use = functools.partial(use_pair, out_ref, parts_ref, items_ref)
    only_use(0, first_share(items_ref[0]), kept_ref, use)


def rest_again_kernel(items_ref, sum_ref, parts_ref, kept_ref, out_ref):
    out_ref[...] = sum_ref[...]
    use = functools.partial(use_pair, out_ref, parts_ref, items_ref)
    only_use(first_share(items_ref[0]), items_ref[0], kept_ref, use)


def cross_again_kernel(
    items_ref, sum_ref, north_ref, south_ref, west_ref, east_ref, kept_ref, v0_ref, v1_ref,
    out_ref, moments_ref, parts_ref
):
    out_ref[...] = sum_ref[...]
    take_round((north_ref, south_ref, west_ref, east_ref), sum_ref.shape[1], parts_ref)
    only_use(0, items_ref[0], kept_ref, functools.partial(use_cross, out_ref, parts_ref, items_ref))
    zero = jnp.zeros(out_ref.shape[1:], jnp.float32)

    def gather(at, sums):
        w0, w1, w2 = v0_ref[at], v1_ref[at], out_ref[at]
        terms = (w0 * w0, w0 * w1, w1 * w1, w1 * w2)
        return tuple(s + t for s, t in zip(sums, terms))

    sums = lax.fori_loop(0, out_ref.shape[0], gather, (zero,) * 4)
    lanes = moments_ref.shape[2]
    folded = [sum(s[:, left : left + lanes] for left in range(0, s.shape[1], lanes)) for s in sums]
    stacked = jnp.concatenate(folded, axis=0)
    line = jnp.sum(jnp.transpose(stacked), axis=0, keepdims=True)
    moments_ref[...] = jnp.broadcast_to(line[None], moments_ref.shape)


def final_kernel(moments_ref, v0_ref, v1_ref, v2_ref, solution_ref, residual_ref):
    rhs, points = v0_ref.shape[1:]
    line = moments_ref[0]
    for at in range(1, moments_ref.shape[0]):
        line = line + moments_ref[at]
    table = across_lanes(line, line.shape[1])
    m00, m01, m11, m12 = (table[k * rhs : (k + 1) * rhs] for k in range(4))
    a = m00 / m01
    norm = m00 - 2.0 * a * m01 + a * a * m11
    grow = 1.0 + norm / m00
    step = norm / (grow * (grow * m01 - 2.0 * a * m11) + a * a * m12)
    first = jnp.concatenate([a + step * grow] * (points // line.shape[1]), axis=1)
    second = jnp.concatenate([step * a] * (points // line.shape[1]), axis=1)

    def one(at, carry):
        w0, w1, w2 = v0_ref[at], v1_ref[at], v2_ref[at]
        solution_ref[at] = first * w0 - second * w1
        residual_ref[at] = w0 - first * w1 + second * w2
        return carry

    lax.fori_loop(0, v0_ref.shape[0], one, 0)


def swapped(first, last, axis):
    count = lax.axis_size(axis)
    even = lax.rem(lax.axis_index(axis), 2) == 0
    swap_up = [(i, i ^ 1) for i in range(count) if i ^ 1 < count]
    swap_down = [(i, ((i + 1) ^ 1) - 1) for i in range(count) if 0 <= ((i + 1) ^ 1) - 1 < count]
    got_up = lax.ppermute(jnp.where(even, last, first), axis, swap_up)
    got_down = lax.ppermute(jnp.where(even, first, last), axis, swap_down)
    return jnp.where(even, got_down, got_up), jnp.where(even, got_up, got_down)


def on_device(kernel, outputs, inputs, scratch=(), listed=False, products=0, made=0, where=pltpu.VMEM):
    vmem = pl.BlockSpec(memory_space=pltpu.VMEM)
    smem = pl.BlockSpec(memory_space=pltpu.SMEM)
    source = pl.BlockSpec(memory_space=where)
    return pl.pallas_call(
        kernel,
        out_shape=tuple(outputs),
        in_specs=[smem if listed and n == 0 else source for n in range(len(inputs))],
        out_specs=tuple(smem if out.dtype == jnp.int32 else vmem for out in outputs),
        scratch_shapes=list(scratch),
        compiler_params=pltpu.CompilerParams(vmem_limit_bytes=VMEM_LIMIT),
        cost_estimate=pl.CostEstimate(
            flops=products, transcendentals=made, bytes_accessed=sum(4 * x.size for x in inputs)
        ),
        name=kernel.__name__,
    )(*inputs)


def tiles(count, points):
    return jax.ShapeDtypeStruct((count, 2, points, points), jnp.bfloat16)


def per_device(right_side, coords, pair_list):
    pair_list = jnp.transpose(pair_list, (1, 2, 0))
    rows, cols, rhs, points = right_side.shape
    blocks = rows * cols
    devices = lax.axis_size("region") * lax.axis_size("tile")
    lanes = 128
    f32, bf16, i32 = jnp.float32, jnp.bfloat16, jnp.int32
    array = jax.ShapeDtypeStruct
    halo = 2 * rows + 2 * (cols + 2)
    near_count = len(inner_candidates(rows, cols))
    cross_count = len(cross_candidates(rows, cols))
    field = array((blocks, rhs, points), f32)
    column = array((rows, rhs + 2, points), f32)
    parts_round = pltpu.VMEM((halo, 2 * rhs, points), bf16)
    each = 6 * rhs * points * points

    def columns_round(first, last, north, south):
        first = jnp.concatenate([north[:1], first, south[:1]], axis=0)
        last = jnp.concatenate([north[cols - 1 :], last, south[cols - 1 :]], axis=0)
        return swapped(first, last, "tile")

    fetched = (
        column, column, array((2, cols, rhs + 2, points), f32), field, array((blocks, 2, points), f32),
        array(pair_list.shape, i32),
    )
    first, last, edges, w0, stations, pairs = on_device(
        pack_kernel, fetched,
        tuple(pltpu.with_memory_space_constraint(x, pltpu.HBM) for x in (right_side, coords, pair_list)),
        (pltpu.SemaphoreType.DMA((2 * rows + 1,)),), where=pltpu.HBM,
    )
    north, south = swapped(edges[0], edges[1], "region")
    parts_field = array((blocks, 2 * rhs, points), bf16)
    near_items, cross_items, part, own_tiles, parts, own_points, spread = on_device(
        own_first_kernel,
        (array((near_count + 3,), i32), array((cross_count + 3,), i32), field, tiles(blocks, points), parts_field,
         array((blocks, 2, points), f32), array((blocks, 2, points, lanes), f32)),
        (pairs, w0, stations), listed=True, products=blocks * each, made=blocks * 2 * points * points,
    )
    north, south, part = lax.optimization_barrier((north, south, part))
    west, east = columns_round(first, last, north, south)
    part, near_tiles = on_device(
        inner_first_kernel, (field, tiles(near_count + 2, points)), (near_items, part, parts, own_points, spread),
        (), True, near_count * each, near_count * 2 * points * points,
    )
    w1, cross_tiles = on_device(
        cross_first_kernel, (field, tiles(cross_count + 2, points)),
        (cross_items, part, north, south, west, east, spread),
        (parts_round, pltpu.VMEM((halo, 2, points), f32)), True,
        cross_count * each, cross_count * 2 * points * points,
    )
    w1_grid = w1.reshape(right_side.shape)
    north, south = swapped(w1_grid[0], w1_grid[rows - 1], "region")
    part, parts = on_device(
        near_again_kernel, (field, parts_field), (near_items, w1, own_tiles, near_tiles), (), True,
        (blocks + near_count) * each,
    )
    north, south, part = lax.optimization_barrier((north, south, part))
    west, east = columns_round(w1_grid[:, 0], w1_grid[:, cols - 1], north, south)
    (part,) = on_device(
        rest_again_kernel, (field,), (near_items, part, parts, near_tiles), (), True, near_count * each
    )
    w2, moments = on_device(
        cross_again_kernel, (field, array((devices, 1, 4 * rhs), f32)),
        (cross_items, part, north, south, west, east, cross_tiles, w0, w1), (parts_round,), True, cross_count * each,
    )
    moments = lax.all_to_all(moments, ("region", "tile"), 0, 0)
    solution, residual = on_device(final_kernel, (field, field), (moments, w0, w1, w2))
    return solution.reshape(right_side.shape), residual.reshape(right_side.shape)


def solution(mesh):
    placed = (
        P("region", "tile", None, None),
        P("region", "tile", None, None),
        P(None, "region", "tile"),
    )
    return jax.shard_map(
        per_device,
        mesh=mesh,
        in_specs=placed,
        out_specs=(P("region", "tile", None, None), P("region", "tile", None, None)),
        check_vma=False,
    )
```

```python
import functools

import jax
import jax.numpy as jnp
from jax import lax
from jax.experimental import pallas as pl
from jax.experimental.pallas import tpu as pltpu
from jax.sharding import PartitionSpec as P

LENGTH_SCALE = 0.2
TAPER_RANGE = 0.5
NUGGET = 3.0
OFFSETS = ((0, 1), (1, 0), (1, 1), (1, -1), (0, -1), (-1, 0), (-1, -1), (-1, 1))
UNIT = 1.4426950408889634 / LENGTH_SCALE
EDGE = UNIT * TAPER_RANGE
WEIGHT = 4.0 * 2.0**-EDGE / EDGE**5
STRIP = 64
LONG_TURN_LOG2 = 3
VMEM_LIMIT = 10 * 1024 * 1024


def dot_nn(a, b):
    return lax.dot_general(a, b, (((1,), (0,)), ((), ())), preferred_element_type=jnp.float32)


def dot_nt(a, b):
    return lax.dot_general(a, b, (((1,), (1,)), ((), ())), preferred_element_type=jnp.float32)


def split_hi_lo(values):
    hi = values.astype(jnp.bfloat16)
    lo = (values - hi.astype(jnp.float32)).astype(jnp.bfloat16)
    return hi, lo


def across_lanes(row, lanes):
    return jnp.transpose(jnp.broadcast_to(row, (lanes, row.shape[1])))


def make_tile(keep_ref, slot, spread_ref, down, points_ref, along, shift_a, shift_b):
    points = keep_ref.shape[2]
    lanes = spread_ref.shape[3]
    row_x = points_ref[along, 0:1] - shift_a
    row_y = points_ref[along, 1:2] - shift_b
    for start in range(0, points, STRIP):
        rows = slice(start, start + STRIP)
        for left in range(0, points, lanes):
            cols = slice(left, left + lanes)
            gap_x = spread_ref[down, 0, rows] - row_x[:, cols]
            gap_y = spread_ref[down, 1, rows] - row_y[:, cols]
            square = jnp.maximum(gap_x * gap_x + gap_y * gap_y, 1e-30)
            rest = jnp.maximum(EDGE - square * lax.rsqrt(square), 0.0)
            rest2 = rest * rest
            cov = (jnp.exp2(rest) * (rest2 * rest2)) * (1.25 * EDGE - rest)
            for part, values in enumerate(split_hi_lo(cov)):
                keep_ref[slot, part, rows, cols] = values


def product(dot, parts_ref, at, high, low):
    rhs = parts_ref.shape[1] // 2
    both = dot(parts_ref[at], high)
    cross = dot(parts_ref[at, 0:rhs], low)
    return both[:rhs] + both[rhs:] + cross


def store_parts(parts_ref, at, values):
    rhs = values.shape[0]
    hi, lo = split_hi_lo(values * WEIGHT)
    parts_ref[at, 0:rhs] = hi
    parts_ref[at, rhs : 2 * rhs] = lo


def in_turns(count, step):
    turns = lax.shift_right_logical(count + 1, 1)

    def one_turn(turn, carry):
        step(2 * turn)
        step(2 * turn + 1)
        return carry

    lax.fori_loop(0, turns, one_turn, 0)


def only_use(first, last, kept_ref, use):
    def one_turn(start, length):
        for n in range(length):
            use(kept_ref[start + n, 0], kept_ref[start + n, 1], start + n)

    whole = lax.shift_right_logical(last - first, LONG_TURN_LOG2)
    lax.fori_loop(0, whole, lambda turn, c: (one_turn(first + (turn << LONG_TURN_LOG2), 1 << LONG_TURN_LOG2), c)[1], 0)
    lax.fori_loop(first + (whole << LONG_TURN_LOG2), last, lambda n, c: (one_turn(n, 1), c)[1], 0)


def item_code(own, other, shift_a, shift_b):
    return own + 64 * other + 4096 * (shift_a + 1) + 16384 * (shift_b + 1)


NO_ITEM = item_code(0, 0, 2, 2)


def item_blocks_of(code):
    return code % 64, code // 64 % 64


def item_blocks(code):
    return lax.bitwise_and(code, 63), lax.bitwise_and(lax.shift_right_logical(code, 6), 63)


def item_shifts(code):
    shift_a = lax.bitwise_and(lax.shift_right_logical(code, 12), 3) - 1
    shift_b = lax.shift_right_logical(code, 14) - 1
    return shift_a.astype(jnp.float32) * UNIT, shift_b.astype(jnp.float32) * UNIT


def list_items(items_ref, candidates, pair_ref, more=()):
    cols = pair_ref.shape[1]
    count = jnp.int32(0)
    for part in (candidates, more):
        for k, own, code in part:
            items_ref[count + 1] = code
            count = count + jnp.where(pair_ref[own // cols, own % cols, k] > 0, 1, 0)
        if part is candidates:
            items_ref[len(candidates) + len(more) + 2] = count
    items_ref[0] = count
    items_ref[count + 1] = NO_ITEM


def inner_candidates(rows, cols):
    found = []
    for k in range(4):
        shift_a, shift_b = OFFSETS[k]
        for a in range(rows):
            for b in range(cols):
                if 0 <= a + shift_a < rows and 0 <= b + shift_b < cols:
                    own = a * cols + b
                    other = own + shift_a * cols + shift_b
                    found.append((k, own, item_code(own, other, shift_a, shift_b)))
    return found


def cross_candidates(rows, cols):
    places = [(-1, b) for b in range(cols)] + [(rows, b) for b in range(cols)]
    places += [(a, -1) for a in range(-1, rows + 1)] + [(a, cols) for a in range(-1, rows + 1)]
    found = []
    for k in range(8):
        shift_a, shift_b = OFFSETS[k]
        for a in range(rows):
            for b in range(cols):
                place = (a + shift_a, b + shift_b)
                if place in places:
                    own = a * cols + b
                    found.append((k, own, item_code(own, places.index(place), -shift_a, -shift_b)))
    in_rows = [item for item in found if item_blocks_of(item[2])[1] < 2 * cols]
    return in_rows, [item for item in found if item not in in_rows]


def pack_kernel(v_hbm, c_hbm, pair_hbm, first_ref, last_ref, edge_ref, v_ref, c_ref, pair_ref, sems):
    rows, cols, rhs = v_hbm.shape[:3]
    fetches = []
    for row in range(rows):
        own = pl.ds(row * cols, cols)
        fetches.append(pltpu.make_async_copy(v_hbm.at[row], v_ref.at[own], sems.at[2 * row]))
        fetches.append(pltpu.make_async_copy(c_hbm.at[row], c_ref.at[own], sems.at[2 * row + 1]))
    fetches.append(pltpu.make_async_copy(pair_hbm, pair_ref, sems.at[2 * rows]))
    for fetch in fetches:
        fetch.start()
    for fetch in fetches:
        fetch.wait()
    both = slice(rhs, rhs + 2)
    for row in range(rows):
        for column_ref, at in ((first_ref, row * cols), (last_ref, row * cols + cols - 1)):
            column_ref[row, 0:rhs] = v_ref[at]
            column_ref[row, both] = c_ref[at]
    for n, row in enumerate((0, rows - 1)):
        own = slice(row * cols, (row + 1) * cols)
        edge_ref[n, :, 0:rhs] = v_ref[own]
        edge_ref[n, :, both] = c_ref[own]


def use_own(out_ref, parts_ref, high, low, at):
    out_ref[at] += product(dot_nn, parts_ref, at, high, low)


def use_pair(out_ref, parts_ref, items_ref, high, low, n):
    own, other = item_blocks(items_ref[n + 1])
    out_ref[own] += product(dot_nn, parts_ref, other, high, low)
    out_ref[other] += product(dot_nt, parts_ref, own, high, low)


def use_cross(out_ref, parts_ref, items_ref, high, low, n):
    own, other = item_blocks(items_ref[n + 1])
    out_ref[own] += product(dot_nt, parts_ref, other, high, low)


def own_first_kernel(
    pair_ref, v_ref, c_ref, near_ref, cross_ref, out_ref, kept_ref, parts_ref, points_ref, spread_ref
):
    rows, cols = pair_ref.shape[:2]
    lanes = spread_ref.shape[3]

    def one(at):
        store_parts(parts_ref, at, v_ref[at])
        out_ref[at] = NUGGET * v_ref[at]
        scaled = c_ref[at] * UNIT
        points_ref[at] = scaled
        for axis in range(2):
            spread_ref[at, axis] = across_lanes(scaled[axis : axis + 1], lanes)
        make_tile(kept_ref, at, spread_ref, at, points_ref, at, 0.0, 0.0)

    def one_pair(turn, carry):
        one(2 * turn)
        one(2 * turn + 1)
        return carry

    lax.fori_loop(0, rows * cols // 2, one_pair, 0)
    only_use(0, jnp.int32(rows * cols), kept_ref, functools.partial(use_own, out_ref, parts_ref))
    list_items(near_ref, inner_candidates(rows, cols), pair_ref)
    in_rows, in_columns = cross_candidates(rows, cols)
    list_items(cross_ref, in_rows, pair_ref, in_columns)


def inner_first_kernel(items_ref, sum_ref, parts_ref, points_ref, spread_ref, out_ref, kept_ref):
    out_ref[...] = sum_ref[...]

    def make(n):
        code = items_ref[n + 1]
        own, other = item_blocks(code)
        make_tile(kept_ref, n, spread_ref, other, points_ref, own, *item_shifts(code))

    in_turns(items_ref[0], make)
    only_use(0, items_ref[0], kept_ref, functools.partial(use_pair, out_ref, parts_ref, items_ref))


def take_round(round_refs, rhs, parts_ref, points_ref=None, start=0):
    for side in round_refs:

        def take(at, carry, side=side, start=start):
            store_parts(parts_ref, start + at, side[at, 0:rhs])
            if points_ref is not None:
                points_ref[start + at] = side[at, rhs : rhs + 2] * UNIT
            return carry

        lax.fori_loop(0, side.shape[0], take, 0)
        start += side.shape[0]


def cross_first_kernel(
    items_ref, sum_ref, north_ref, south_ref, west_ref, east_ref, spread_ref,
    out_ref, kept_ref, parts_ref, points_ref
):
    out_ref[...] = sum_ref[...]
    take_round((north_ref, south_ref, west_ref, east_ref), sum_ref.shape[1], parts_ref, points_ref)

    def make(n):
        code = items_ref[n + 1]
        own, other = item_blocks(code)
        make_tile(kept_ref, n, spread_ref, own, points_ref, other, *item_shifts(code))

    in_turns(items_ref[0], make)
    only_use(0, items_ref[0], kept_ref, functools.partial(use_cross, out_ref, parts_ref, items_ref))


def first_share(count):
    return lax.shift_right_logical(5 * count, 3)


def near_again_kernel(items_ref, v_ref, own_ref, kept_ref, out_ref, parts_ref):
    def one(at, carry):
        store_parts(parts_ref, at, v_ref[at])
        out_ref[at] = NUGGET * v_ref[at]
        return carry

    lax.fori_loop(0, parts_ref.shape[0], one, 0, unroll=2)
    only_use(0, jnp.int32(parts_ref.shape[0]), own_ref, functools.partial(use_own, out_ref, parts_ref))
    use = functools.partial(use_pair, out_ref, parts_ref, items_ref)
    only_use(0, first_share(items_ref[0]), kept_ref, use)


def rest_again_kernel(
    near_ref, cross_ref, sum_ref, parts_ref, near_kept_ref, north_ref, south_ref, cross_kept_ref, out_ref, round_ref
):
    out_ref[...] = sum_ref[...]
    use = functools.partial(use_pair, out_ref, parts_ref, near_ref)
    only_use(first_share(near_ref[0]), near_ref[0], near_kept_ref, use)
    take_round((north_ref, south_ref), sum_ref.shape[1], round_ref)
    in_rows = cross_ref[cross_ref.shape[0] - 1]
    only_use(0, in_rows, cross_kept_ref, functools.partial(use_cross, out_ref, round_ref, cross_ref))


def cross_again_kernel(
    items_ref, sum_ref, west_ref, east_ref, kept_ref, v0_ref, v1_ref, out_ref, moments_ref, parts_ref
):
    out_ref[...] = sum_ref[...]
    start = parts_ref.shape[0] - west_ref.shape[0] - east_ref.shape[0]
    take_round((west_ref, east_ref), sum_ref.shape[1], parts_ref, start=start)
    in_rows = items_ref[items_ref.shape[0] - 1]
    only_use(in_rows, items_ref[0], kept_ref, functools.partial(use_cross, out_ref, parts_ref, items_ref))
    zero = jnp.zeros(out_ref.shape[1:], jnp.float32)

    def gather(at, sums):
        w0, w1, w2 = v0_ref[at], v1_ref[at], out_ref[at]
        terms = (w0 * w0, w0 * w1, w1 * w1, w1 * w2)
        return tuple(s + t for s, t in zip(sums, terms))

    sums = lax.fori_loop(0, out_ref.shape[0], gather, (zero,) * 4)
    lanes = moments_ref.shape[2]
    folded = [sum(s[:, left : left + lanes] for left in range(0, s.shape[1], lanes)) for s in sums]
    stacked = jnp.concatenate(folded, axis=0)
    line = jnp.sum(jnp.transpose(stacked), axis=0, keepdims=True)
    moments_ref[...] = jnp.broadcast_to(line[None], moments_ref.shape)


def final_kernel(moments_ref, v0_ref, v1_ref, v2_ref, solution_ref, residual_ref):
    rhs, points = v0_ref.shape[1:]
    line = moments_ref[0]
    for at in range(1, moments_ref.shape[0]):
        line = line + moments_ref[at]
    table = across_lanes(line, line.shape[1])
    m00, m01, m11, m12 = (table[k * rhs : (k + 1) * rhs] for k in range(4))
    a = m00 / m01
    norm = m00 - 2.0 * a * m01 + a * a * m11
    grow = 1.0 + norm / m00
    step = norm / (grow * (grow * m01 - 2.0 * a * m11) + a * a * m12)
    first = jnp.concatenate([a + step * grow] * (points // line.shape[1]), axis=1)
    second = jnp.concatenate([step * a] * (points // line.shape[1]), axis=1)

    def one(at, carry):
        w0, w1, w2 = v0_ref[at], v1_ref[at], v2_ref[at]
        solution_ref[at] = first * w0 - second * w1
        residual_ref[at] = w0 - first * w1 + second * w2
        return carry

    lax.fori_loop(0, v0_ref.shape[0], one, 0)


def swapped(first, last, axis):
    count = lax.axis_size(axis)
    even = lax.rem(lax.axis_index(axis), 2) == 0
    swap_up = [(i, i ^ 1) for i in range(count) if i ^ 1 < count]
    swap_down = [(i, ((i + 1) ^ 1) - 1) for i in range(count) if 0 <= ((i + 1) ^ 1) - 1 < count]
    got_up = lax.ppermute(jnp.where(even, last, first), axis, swap_up)
    got_down = lax.ppermute(jnp.where(even, first, last), axis, swap_down)
    return jnp.where(even, got_down, got_up), jnp.where(even, got_up, got_down)


def on_device(kernel, outputs, inputs, scratch=(), listed=False, products=0, made=0, where=pltpu.VMEM):
    vmem = pl.BlockSpec(memory_space=pltpu.VMEM)
    smem = pl.BlockSpec(memory_space=pltpu.SMEM)
    source = pl.BlockSpec(memory_space=where)
    return pl.pallas_call(
        kernel,
        out_shape=tuple(outputs),
        in_specs=[smem if listed and x.dtype == jnp.int32 else source for x in inputs],
        out_specs=tuple(smem if out.dtype == jnp.int32 else vmem for out in outputs),
        scratch_shapes=list(scratch),
        compiler_params=pltpu.CompilerParams(vmem_limit_bytes=VMEM_LIMIT),
        cost_estimate=pl.CostEstimate(
            flops=products, transcendentals=made, bytes_accessed=sum(4 * x.size for x in inputs)
        ),
        name=kernel.__name__,
    )(*inputs)


def tiles(count, points):
    return jax.ShapeDtypeStruct((count, 2, points, points), jnp.bfloat16)


def per_device(right_side, coords, pair_list):
    pair_list = jnp.transpose(pair_list, (1, 2, 0))
    rows, cols, rhs, points = right_side.shape
    blocks = rows * cols
    devices = lax.axis_size("region") * lax.axis_size("tile")
    lanes = 128
    f32, bf16, i32 = jnp.float32, jnp.bfloat16, jnp.int32
    array = jax.ShapeDtypeStruct
    halo = 2 * rows + 2 * (cols + 2)
    near_count = len(inner_candidates(rows, cols))
    cross_count = sum(len(part) for part in cross_candidates(rows, cols))
    field = array((blocks, rhs, points), f32)
    column = array((rows, rhs + 2, points), f32)
    parts_round = pltpu.VMEM((halo, 2 * rhs, points), bf16)
    each = 6 * rhs * points * points

    def columns_round(first, last, north, south):
        first = jnp.concatenate([north[:1], first, south[:1]], axis=0)
        last = jnp.concatenate([north[cols - 1 :], last, south[cols - 1 :]], axis=0)
        return swapped(first, last, "tile")

    fetched = (
        column, column, array((2, cols, rhs + 2, points), f32), field, array((blocks, 2, points), f32),
        array(pair_list.shape, i32),
    )
    first, last, edges, w0, stations, pairs = on_device(
        pack_kernel, fetched,
        tuple(pltpu.with_memory_space_constraint(x, pltpu.HBM) for x in (right_side, coords, pair_list)),
        (pltpu.SemaphoreType.DMA((2 * rows + 1,)),), where=pltpu.HBM,
    )
    north, south = swapped(edges[0], edges[1], "region")
    parts_field = array((blocks, 2 * rhs, points), bf16)
    near_items, cross_items, part, own_tiles, parts, own_points, spread = on_device(
        own_first_kernel,
        (array((near_count + 3,), i32), array((cross_count + 3,), i32), field, tiles(blocks, points), parts_field,
         array((blocks, 2, points), f32), array((blocks, 2, points, lanes), f32)),
        (pairs, w0, stations), listed=True, products=blocks * each, made=blocks * 2 * points * points,
    )
    north, south, part = lax.optimization_barrier((north, south, part))
    west, east = columns_round(first, last, north, south)
    part, near_tiles = on_device(
        inner_first_kernel, (field, tiles(near_count + 2, points)), (near_items, part, parts, own_points, spread),
        (), True, near_count * each, near_count * 2 * points * points,
    )
    w1, cross_tiles = on_device(
        cross_first_kernel, (field, tiles(cross_count + 2, points)),
        (cross_items, part, north, south, west, east, spread),
        (parts_round, pltpu.VMEM((halo, 2, points), f32)), True,
        cross_count * each, cross_count * 2 * points * points,
    )
    w1_grid = w1.reshape(right_side.shape)
    north, south = swapped(w1_grid[0], w1_grid[rows - 1], "region")
    part, parts = on_device(
        near_again_kernel, (field, parts_field), (near_items, w1, own_tiles, near_tiles), (), True,
        (blocks + near_count) * each,
    )
    north, south, part = lax.optimization_barrier((north, south, part))
    west, east = columns_round(w1_grid[:, 0], w1_grid[:, cols - 1], north, south)
    (part,) = on_device(
        rest_again_kernel, (field,),
        (near_items, cross_items, part, parts, near_tiles, north, south, cross_tiles), (parts_round,), True,
        near_count * each,
    )
    w2, moments = on_device(
        cross_again_kernel, (field, array((devices, 1, 4 * rhs), f32)),
        (cross_items, part, west, east, cross_tiles, w0, w1), (parts_round,), True, cross_count * each,
    )
    moments = lax.all_to_all(moments, ("region", "tile"), 0, 0)
    solution, residual = on_device(final_kernel, (field, field), (moments, w0, w1, w2))
    return solution.reshape(right_side.shape), residual.reshape(right_side.shape)


def solution(mesh):
    placed = (
        P("region", "tile", None, None),
        P("region", "tile", None, None),
        P(None, "region", "tile"),
    )
    return jax.shard_map(
        per_device,
        mesh=mesh,
        in_specs=placed,
        out_specs=(P("region", "tile", None, None), P("region", "tile", None, None)),
        check_vma=False,
    )
```

```python
import functools

import jax
import jax.numpy as jnp
from jax import lax
from jax.experimental import pallas as pl
from jax.experimental.pallas import tpu as pltpu
from jax.sharding import PartitionSpec as P

LENGTH_SCALE = 0.2
TAPER_RANGE = 0.5
NUGGET = 3.0
OFFSETS = ((0, 1), (1, 0), (1, 1), (1, -1), (0, -1), (-1, 0), (-1, -1), (-1, 1))
UNIT = 1.4426950408889634 / LENGTH_SCALE
EDGE = UNIT * TAPER_RANGE
WEIGHT = 4.0 * 2.0**-EDGE / EDGE**5
STRIP = 64
LONG_TURN_LOG2 = 3
OWN_TURN_LOG2 = 2
VMEM_LIMIT = 10 * 1024 * 1024


def dot_nn(a, b):
    return lax.dot_general(a, b, (((1,), (0,)), ((), ())), preferred_element_type=jnp.float32)


def dot_nt(a, b):
    return lax.dot_general(a, b, (((1,), (1,)), ((), ())), preferred_element_type=jnp.float32)


def split_hi_lo(values):
    hi = values.astype(jnp.bfloat16)
    lo = (values - hi.astype(jnp.float32)).astype(jnp.bfloat16)
    return hi, lo


def across_lanes(row, lanes):
    return jnp.transpose(jnp.broadcast_to(row, (lanes, row.shape[1])))


def make_tile(keep_ref, slot, down_x, down_y, points_ref, along, shift_a, shift_b):
    points = keep_ref.shape[2]
    lanes = down_x.shape[1]
    row_x = points_ref[along, 0:1] - shift_a
    row_y = points_ref[along, 1:2] - shift_b
    for start in range(0, points, STRIP):
        rows = slice(start, start + STRIP)
        for left in range(0, points, lanes):
            cols = slice(left, left + lanes)
            gap_x = down_x[rows] - row_x[:, cols]
            gap_y = down_y[rows] - row_y[:, cols]
            square = jnp.maximum(gap_x * gap_x + gap_y * gap_y, 1e-30)
            rest = jnp.maximum(EDGE - square * lax.rsqrt(square), 0.0)
            rest2 = rest * rest
            cov = (jnp.exp2(rest) * (rest2 * rest2)) * (1.25 * EDGE - rest)
            for part, values in enumerate(split_hi_lo(cov)):
                keep_ref[slot, part, rows, cols] = values


def product(dot, parts_ref, at, high, low):
    rhs = parts_ref.shape[1] // 2
    both = dot(parts_ref[at], high)
    cross = dot(parts_ref[at, 0:rhs], low)
    return both[:rhs] + both[rhs:] + cross


def store_parts(parts_ref, at, values):
    rhs = values.shape[0]
    hi, lo = split_hi_lo(values * WEIGHT)
    parts_ref[at, 0:rhs] = hi
    parts_ref[at, rhs : 2 * rhs] = lo


def in_turns(count, step, log2=2):
    whole = lax.shift_right_logical(count, log2)

    def one_turn(turn, carry):
        for n in range(1 << log2):
            step((turn << log2) + n)
        return carry

    lax.fori_loop(0, whole, one_turn, 0)
    lax.fori_loop(whole << log2, count, lambda n, c: (step(n), c)[1], 0)


def only_use(first, last, kept_ref, use):
    def one_turn(start, length):
        for n in range(length):
            use(kept_ref[start + n, 0], kept_ref[start + n, 1], start + n)

    whole = lax.shift_right_logical(last - first, LONG_TURN_LOG2)
    lax.fori_loop(0, whole, lambda turn, c: (one_turn(first + (turn << LONG_TURN_LOG2), 1 << LONG_TURN_LOG2), c)[1], 0)
    lax.fori_loop(first + (whole << LONG_TURN_LOG2), last, lambda n, c: (one_turn(n, 1), c)[1], 0)


def item_code(own, other, shift_a, shift_b):
    return own + 64 * other + 4096 * (shift_a + 1) + 16384 * (shift_b + 1)


NO_ITEM = item_code(0, 0, 2, 2)


def item_blocks_of(code):
    return code % 64, code // 64 % 64


def item_blocks(code):
    return lax.bitwise_and(code, 63), lax.bitwise_and(lax.shift_right_logical(code, 6), 63)


def item_shifts(code):
    shift_a = lax.bitwise_and(lax.shift_right_logical(code, 12), 3) - 1
    shift_b = lax.shift_right_logical(code, 14) - 1
    return shift_a.astype(jnp.float32) * UNIT, shift_b.astype(jnp.float32) * UNIT


def list_items(items_ref, candidates, pair_ref, more=()):
    cols = pair_ref.shape[1]
    count = jnp.int32(0)
    for part in (candidates, more):
        for k, own, code in part:
            items_ref[count + 1] = code
            count = count + jnp.where(pair_ref[own // cols, own % cols, k] > 0, 1, 0)
        if part is candidates:
            items_ref[len(candidates) + len(more) + 2] = count
    items_ref[0] = count
    items_ref[count + 1] = NO_ITEM


def inner_candidates(rows, cols):
    found = []
    for k in range(4):
        shift_a, shift_b = OFFSETS[k]
        for a in range(rows):
            for b in range(cols):
                if 0 <= a + shift_a < rows and 0 <= b + shift_b < cols:
                    own = a * cols + b
                    other = own + shift_a * cols + shift_b
                    found.append((k, own, item_code(own, other, shift_a, shift_b)))
    return found


def cross_candidates(rows, cols):
    places = [(-1, b) for b in range(cols)] + [(rows, b) for b in range(cols)]
    places += [(a, -1) for a in range(-1, rows + 1)] + [(a, cols) for a in range(-1, rows + 1)]
    found = []
    for k in range(8):
        shift_a, shift_b = OFFSETS[k]
        for a in range(rows):
            for b in range(cols):
                place = (a + shift_a, b + shift_b)
                if place in places:
                    own = a * cols + b
                    found.append((k, own, item_code(own, places.index(place), -shift_a, -shift_b)))
    in_rows = [item for item in found if item_blocks_of(item[2])[1] < 2 * cols]
    return in_rows, [item for item in found if item not in in_rows]


def pack_kernel(v_hbm, c_hbm, pair_hbm, first_ref, last_ref, edge_ref, v_ref, c_ref, pair_ref, sems):
    rows, cols, rhs = v_hbm.shape[:3]
    fetches = []
    for row in range(rows):
        own = pl.ds(row * cols, cols)
        fetches.append(pltpu.make_async_copy(v_hbm.at[row], v_ref.at[own], sems.at[2 * row]))
        fetches.append(pltpu.make_async_copy(c_hbm.at[row], c_ref.at[own], sems.at[2 * row + 1]))
    fetches.append(pltpu.make_async_copy(pair_hbm, pair_ref, sems.at[2 * rows]))
    for fetch in fetches:
        fetch.start()
    for fetch in fetches:
        fetch.wait()
    both = slice(rhs, rhs + 2)
    for row in range(rows):
        for column_ref, at in ((first_ref, row * cols), (last_ref, row * cols + cols - 1)):
            column_ref[row, 0:rhs] = v_ref[at]
            column_ref[row, both] = c_ref[at]
    for n, row in enumerate((0, rows - 1)):
        own = slice(row * cols, (row + 1) * cols)
        edge_ref[n, :, 0:rhs] = v_ref[own]
        edge_ref[n, :, both] = c_ref[own]


def use_own(out_ref, parts_ref, high, low, at):
    out_ref[at] += product(dot_nn, parts_ref, at, high, low)


def use_pair(out_ref, parts_ref, items_ref, high, low, n):
    own, other = item_blocks(items_ref[n + 1])
    out_ref[own] += product(dot_nn, parts_ref, other, high, low)
    out_ref[other] += product(dot_nt, parts_ref, own, high, low)


def use_cross(out_ref, parts_ref, items_ref, high, low, n):
    own, other = item_blocks(items_ref[n + 1])
    out_ref[own] += product(dot_nt, parts_ref, other, high, low)


def own_first_kernel(
    pair_ref, v_ref, c_ref, near_ref, cross_ref, out_ref, kept_ref, parts_ref, points_ref, spread_ref
):
    rows, cols = pair_ref.shape[:2]
    lanes = spread_ref.shape[3]

    def one(at):
        store_parts(parts_ref, at, v_ref[at])
        out_ref[at] = NUGGET * v_ref[at]
        scaled = c_ref[at] * UNIT
        points_ref[at] = scaled
        down = [across_lanes(scaled[axis : axis + 1], lanes) for axis in range(2)]
        make_tile(kept_ref, at, *down, points_ref, at, 0.0, 0.0)
        for axis in range(2):
            spread_ref[at, axis] = down[axis]

    in_turns(jnp.int32(rows * cols), one, OWN_TURN_LOG2)
    only_use(0, jnp.int32(rows * cols), kept_ref, functools.partial(use_own, out_ref, parts_ref))
    list_items(near_ref, inner_candidates(rows, cols), pair_ref)
    in_rows, in_columns = cross_candidates(rows, cols)
    list_items(cross_ref, in_rows, pair_ref, in_columns)


def inner_first_kernel(items_ref, sum_ref, parts_ref, points_ref, spread_ref, out_ref, kept_ref):
    out_ref[...] = sum_ref[...]

    def make(n):
        code = items_ref[n + 1]
        own, other = item_blocks(code)
        make_tile(kept_ref, n, spread_ref.at[other, 0], spread_ref.at[other, 1], points_ref, own, *item_shifts(code))

    in_turns(items_ref[0], make)
    only_use(0, items_ref[0], kept_ref, functools.partial(use_pair, out_ref, parts_ref, items_ref))


def take_round(round_refs, rhs, parts_ref, points_ref=None, start=0):
    for side in round_refs:

        def take(at, carry, side=side, start=start):
            store_parts(parts_ref, start + at, side[at, 0:rhs])
            if points_ref is not None:
                points_ref[start + at] = side[at, rhs : rhs + 2] * UNIT
            return carry

        lax.fori_loop(0, side.shape[0], take, 0)
        start += side.shape[0]


def cross_first_kernel(
    items_ref, sum_ref, north_ref, south_ref, west_ref, east_ref, spread_ref,
    out_ref, kept_ref, parts_ref, points_ref
):
    out_ref[...] = sum_ref[...]
    take_round((north_ref, south_ref, west_ref, east_ref), sum_ref.shape[1], parts_ref, points_ref)

    def make(n):
        code = items_ref[n + 1]
        own, other = item_blocks(code)
        make_tile(kept_ref, n, spread_ref.at[own, 0], spread_ref.at[own, 1], points_ref, other, *item_shifts(code))

    in_turns(items_ref[0], make)
    only_use(0, items_ref[0], kept_ref, functools.partial(use_cross, out_ref, parts_ref, items_ref))


def first_share(count):
    return lax.shift_right_logical(5 * count, 3)


def near_again_kernel(items_ref, v_ref, own_ref, kept_ref, out_ref, parts_ref):
    def one(at, carry):
        store_parts(parts_ref, at, v_ref[at])
        out_ref[at] = NUGGET * v_ref[at]
        return carry

    lax.fori_loop(0, parts_ref.shape[0], one, 0, unroll=2)
    only_use(0, jnp.int32(parts_ref.shape[0]), own_ref, functools.partial(use_own, out_ref, parts_ref))
    use = functools.partial(use_pair, out_ref, parts_ref, items_ref)
    only_use(0, first_share(items_ref[0]), kept_ref, use)


def rest_again_kernel(
    near_ref, cross_ref, sum_ref, parts_ref, near_kept_ref, north_ref, south_ref, cross_kept_ref, out_ref, round_ref
):
    out_ref[...] = sum_ref[...]
    use = functools.partial(use_pair, out_ref, parts_ref, near_ref)
    only_use(first_share(near_ref[0]), near_ref[0], near_kept_ref, use)
    take_round((north_ref, south_ref), sum_ref.shape[1], round_ref)
    in_rows = cross_ref[cross_ref.shape[0] - 1]
    only_use(0, in_rows, cross_kept_ref, functools.partial(use_cross, out_ref, round_ref, cross_ref))


def cross_again_kernel(
    items_ref, sum_ref, west_ref, east_ref, kept_ref, v0_ref, v1_ref, out_ref, moments_ref, parts_ref
):
    out_ref[...] = sum_ref[...]
    start = parts_ref.shape[0] - west_ref.shape[0] - east_ref.shape[0]
    take_round((west_ref, east_ref), sum_ref.shape[1], parts_ref, start=start)
    in_rows = items_ref[items_ref.shape[0] - 1]
    only_use(in_rows, items_ref[0], kept_ref, functools.partial(use_cross, out_ref, parts_ref, items_ref))
    zero = jnp.zeros(out_ref.shape[1:], jnp.float32)

    def gather(at, sums):
        w0, w1, w2 = v0_ref[at], v1_ref[at], out_ref[at]
        terms = (w0 * w0, w0 * w1, w1 * w1, w1 * w2)
        return tuple(s + t for s, t in zip(sums, terms))

    sums = lax.fori_loop(0, out_ref.shape[0], gather, (zero,) * 4)
    lanes = moments_ref.shape[2]
    folded = [sum(s[:, left : left + lanes] for left in range(0, s.shape[1], lanes)) for s in sums]
    stacked = jnp.concatenate(folded, axis=0)
    line = jnp.sum(jnp.transpose(stacked), axis=0, keepdims=True)
    moments_ref[...] = jnp.broadcast_to(line[None], moments_ref.shape)


def final_kernel(moments_ref, v0_ref, v1_ref, v2_ref, solution_ref, residual_ref):
    rhs, points = v0_ref.shape[1:]
    line = moments_ref[0]
    for at in range(1, moments_ref.shape[0]):
        line = line + moments_ref[at]
    table = across_lanes(line, line.shape[1])
    m00, m01, m11, m12 = (table[k * rhs : (k + 1) * rhs] for k in range(4))
    a = m00 / m01
    norm = m00 - 2.0 * a * m01 + a * a * m11
    grow = 1.0 + norm / m00
    step = norm / (grow * (grow * m01 - 2.0 * a * m11) + a * a * m12)
    first = jnp.concatenate([a + step * grow] * (points // line.shape[1]), axis=1)
    second = jnp.concatenate([step * a] * (points // line.shape[1]), axis=1)

    def one(at, carry):
        w0, w1, w2 = v0_ref[at], v1_ref[at], v2_ref[at]
        solution_ref[at] = first * w0 - second * w1
        residual_ref[at] = w0 - first * w1 + second * w2
        return carry

    lax.fori_loop(0, v0_ref.shape[0], one, 0)


def swapped(first, last, axis):
    count = lax.axis_size(axis)
    even = lax.rem(lax.axis_index(axis), 2) == 0
    swap_up = [(i, i ^ 1) for i in range(count) if i ^ 1 < count]
    swap_down = [(i, ((i + 1) ^ 1) - 1) for i in range(count) if 0 <= ((i + 1) ^ 1) - 1 < count]
    got_up = lax.ppermute(jnp.where(even, last, first), axis, swap_up)
    got_down = lax.ppermute(jnp.where(even, first, last), axis, swap_down)
    return jnp.where(even, got_down, got_up), jnp.where(even, got_up, got_down)


def on_device(kernel, outputs, inputs, scratch=(), listed=False, products=0, made=0, where=pltpu.VMEM):
    vmem = pl.BlockSpec(memory_space=pltpu.VMEM)
    smem = pl.BlockSpec(memory_space=pltpu.SMEM)
    source = pl.BlockSpec(memory_space=where)
    return pl.pallas_call(
        kernel,
        out_shape=tuple(outputs),
        in_specs=[smem if listed and x.dtype == jnp.int32 else source for x in inputs],
        out_specs=tuple(smem if out.dtype == jnp.int32 else vmem for out in outputs),
        scratch_shapes=list(scratch),
        compiler_params=pltpu.CompilerParams(vmem_limit_bytes=VMEM_LIMIT),
        cost_estimate=pl.CostEstimate(
            flops=products, transcendentals=made, bytes_accessed=sum(4 * x.size for x in inputs)
        ),
        name=kernel.__name__,
    )(*inputs)


def tiles(count, points):
    return jax.ShapeDtypeStruct((count, 2, points, points), jnp.bfloat16)


def per_device(right_side, coords, pair_list):
    pair_list = jnp.transpose(pair_list, (1, 2, 0))
    rows, cols, rhs, points = right_side.shape
    blocks = rows * cols
    devices = lax.axis_size("region") * lax.axis_size("tile")
    lanes = 128
    f32, bf16, i32 = jnp.float32, jnp.bfloat16, jnp.int32
    array = jax.ShapeDtypeStruct
    halo = 2 * rows + 2 * (cols + 2)
    near_count = len(inner_candidates(rows, cols))
    cross_count = sum(len(part) for part in cross_candidates(rows, cols))
    field = array((blocks, rhs, points), f32)
    column = array((rows, rhs + 2, points), f32)
    parts_round = pltpu.VMEM((halo, 2 * rhs, points), bf16)
    each = 6 * rhs * points * points

    def columns_round(first, last, north, south):
        first = jnp.concatenate([north[:1], first, south[:1]], axis=0)
        last = jnp.concatenate([north[cols - 1 :], last, south[cols - 1 :]], axis=0)
        return swapped(first, last, "tile")

    fetched = (
        column, column, array((2, cols, rhs + 2, points), f32), field, array((blocks, 2, points), f32),
        array(pair_list.shape, i32),
    )
    first, last, edges, w0, stations, pairs = on_device(
        pack_kernel, fetched,
        tuple(pltpu.with_memory_space_constraint(x, pltpu.HBM) for x in (right_side, coords, pair_list)),
        (pltpu.SemaphoreType.DMA((2 * rows + 1,)),), where=pltpu.HBM,
    )
    north, south = swapped(edges[0], edges[1], "region")
    parts_field = array((blocks, 2 * rhs, points), bf16)
    near_items, cross_items, part, own_tiles, parts, own_points, spread = on_device(
        own_first_kernel,
        (array((near_count + 3,), i32), array((cross_count + 3,), i32), field, tiles(blocks, points), parts_field,
         array((blocks, 2, points), f32), array((blocks, 2, points, lanes), f32)),
        (pairs, w0, stations), listed=True, products=blocks * each, made=blocks * 2 * points * points,
    )
    north, south, part = lax.optimization_barrier((north, south, part))
    west, east = columns_round(first, last, north, south)
    part, near_tiles = on_device(
        inner_first_kernel, (field, tiles(near_count + 2, points)), (near_items, part, parts, own_points, spread),
        (), True, near_count * each, near_count * 2 * points * points,
    )
    w1, cross_tiles = on_device(
        cross_first_kernel, (field, tiles(cross_count + 2, points)),
        (cross_items, part, north, south, west, east, spread),
        (parts_round, pltpu.VMEM((halo, 2, points), f32)), True,
        cross_count * each, cross_count * 2 * points * points,
    )
    w1_grid = w1.reshape(right_side.shape)
    north, south = swapped(w1_grid[0], w1_grid[rows - 1], "region")
    part, parts = on_device(
        near_again_kernel, (field, parts_field), (near_items, w1, own_tiles, near_tiles), (), True,
        (blocks + near_count) * each,
    )
    north, south, part = lax.optimization_barrier((north, south, part))
    west, east = columns_round(w1_grid[:, 0], w1_grid[:, cols - 1], north, south)
    (part,) = on_device(
        rest_again_kernel, (field,),
        (near_items, cross_items, part, parts, near_tiles, north, south, cross_tiles), (parts_round,), True,
        near_count * each,
    )
    w2, moments = on_device(
        cross_again_kernel, (field, array((devices, 1, 4 * rhs), f32)),
        (cross_items, part, west, east, cross_tiles, w0, w1), (parts_round,), True, cross_count * each,
    )
    moments = lax.all_to_all(moments, ("region", "tile"), 0, 0)
    solution, residual = on_device(final_kernel, (field, field), (moments, w0, w1, w2))
    return solution.reshape(right_side.shape), residual.reshape(right_side.shape)


def solution(mesh):
    placed = (
        P("region", "tile", None, None),
        P("region", "tile", None, None),
        P(None, "region", "tile"),
    )
    return jax.shard_map(
        per_device,
        mesh=mesh,
        in_specs=placed,
        out_specs=(P("region", "tile", None, None), P("region", "tile", None, None)),
        check_vma=False,
    )
```

```python
import functools

import jax
import jax.numpy as jnp
from jax import lax
from jax.experimental import pallas as pl
from jax.experimental.pallas import tpu as pltpu
from jax.sharding import PartitionSpec as P

LENGTH_SCALE = 0.2
TAPER_RANGE = 0.5
NUGGET = 3.0
OFFSETS = ((0, 1), (1, 0), (1, 1), (1, -1), (0, -1), (-1, 0), (-1, -1), (-1, 1))
UNIT = 1.4426950408889634 / LENGTH_SCALE
EDGE = UNIT * TAPER_RANGE
WEIGHT = 4.0 * 2.0**-EDGE / EDGE**5
CHUNK = 128
VMEM_LIMIT = 10 * 1024 * 1024


def dot_nn(a, b):
    return lax.dot_general(a, b, (((1,), (0,)), ((), ())), preferred_element_type=jnp.float32)


def dot_nt(a, b):
    return lax.dot_general(a, b, (((1,), (1,)), ((), ())), preferred_element_type=jnp.float32)


def split_hi_lo(values):
    hi = values.astype(jnp.bfloat16)
    lo = (values - hi.astype(jnp.float32)).astype(jnp.bfloat16)
    return hi, lo


def across_lanes(row, lanes):
    return jnp.transpose(jnp.broadcast_to(row, (lanes, row.shape[1])))


def tile_rows(rows, down_x, down_y, points_ref, along, shift_a, shift_b):
    points = points_ref.shape[2]
    lanes = down_x.shape[1]
    row_x = points_ref[along, 0:1] - shift_a
    row_y = points_ref[along, 1:2] - shift_b
    halves = []
    for left in range(0, points, lanes):
        cols = slice(left, left + lanes)
        gap_x = down_x[rows] - row_x[:, cols]
        gap_y = down_y[rows] - row_y[:, cols]
        square = jnp.maximum(gap_x * gap_x + gap_y * gap_y, 1e-30)
        rest = jnp.maximum(EDGE - square * lax.rsqrt(square), 0.0)
        rest2 = rest * rest
        halves.append((jnp.exp2(rest) * (rest2 * rest2)) * (1.25 * EDGE - rest))
    return split_hi_lo(jnp.concatenate(halves, axis=1))


def make_tile(keep_ref, slot, down_x, down_y, points_ref, along, shift_a, shift_b, use):
    points = keep_ref.shape[2]
    for start in range(0, points, CHUNK):
        rows = slice(start, start + CHUNK)
        hi, lo = tile_rows(rows, down_x, down_y, points_ref, along, shift_a, shift_b)
        keep_ref[slot, 0, rows] = hi
        keep_ref[slot, 1, rows] = lo
        use(hi, lo, rows)


def product(dot, parts_ref, at, high, low):
    rhs = parts_ref.shape[1] // 2
    both = dot(parts_ref[at], high)
    cross = dot(parts_ref[at, 0:rhs], low)
    return both[:rhs] + both[rhs:] + cross


def store_parts(parts_ref, at, values):
    rhs = values.shape[0]
    hi, lo = split_hi_lo(values * WEIGHT)
    parts_ref[at, 0:rhs] = hi
    parts_ref[at, rhs : 2 * rhs] = lo


def in_turns(first, last, step, log2s=(3, 2, 1, 0)):
    for log2 in log2s:
        turns = lax.shift_right_logical(last - first, log2)

        def one_turn(turn, carry, first=first, log2=log2):
            for n in range(1 << log2):
                step(first + (turn << log2) + n)
            return carry

        lax.fori_loop(0, turns, one_turn, 0)
        first = first + (turns << log2)


def only_use(first, last, kept_ref, use):
    in_turns(first, last, lambda n: use(kept_ref[n, 0], kept_ref[n, 1], n))


def item_code(own, other, shift_a, shift_b):
    return own + 64 * other + 4096 * (shift_a + 1) + 16384 * (shift_b + 1)


NO_ITEM = item_code(0, 0, 2, 2)


def item_blocks_of(code):
    return code % 64, code // 64 % 64


def item_blocks(code):
    return lax.bitwise_and(code, 63), lax.bitwise_and(lax.shift_right_logical(code, 6), 63)


def item_shifts(code):
    shift_a = lax.bitwise_and(lax.shift_right_logical(code, 12), 3) - 1
    shift_b = lax.shift_right_logical(code, 14) - 1
    return shift_a.astype(jnp.float32) * UNIT, shift_b.astype(jnp.float32) * UNIT


def list_items(items_ref, candidates, pair_ref, more=()):
    cols = pair_ref.shape[1]
    count = jnp.int32(0)
    for part in (candidates, more):
        for k, own, code in part:
            items_ref[count + 1] = code
            count = count + jnp.where(pair_ref[own // cols, own % cols, k] > 0, 1, 0)
        if part is candidates:
            items_ref[len(candidates) + len(more) + 2] = count
    items_ref[0] = count
    items_ref[count + 1] = NO_ITEM


def inner_candidates(rows, cols):
    found = []
    for k in range(4):
        shift_a, shift_b = OFFSETS[k]
        for a in range(rows):
            for b in range(cols):
                if 0 <= a + shift_a < rows and 0 <= b + shift_b < cols:
                    own = a * cols + b
                    other = own + shift_a * cols + shift_b
                    found.append((k, own, item_code(own, other, shift_a, shift_b)))
    return found


def cross_candidates(rows, cols):
    places = [(-1, b) for b in range(cols)] + [(rows, b) for b in range(cols)]
    places += [(a, -1) for a in range(-1, rows + 1)] + [(a, cols) for a in range(-1, rows + 1)]
    found = []
    for k in range(8):
        shift_a, shift_b = OFFSETS[k]
        for a in range(rows):
            for b in range(cols):
                place = (a + shift_a, b + shift_b)
                if place in places:
                    own = a * cols + b
                    found.append((k, own, item_code(own, places.index(place), -shift_a, -shift_b)))
    in_rows = [item for item in found if item_blocks_of(item[2])[1] < 2 * cols]
    return in_rows, [item for item in found if item not in in_rows]


def pack_kernel(v_hbm, c_hbm, pair_hbm, first_ref, last_ref, edge_ref, v_ref, c_ref, pair_ref, sems):
    rows, cols, rhs = v_hbm.shape[:3]
    fetches = []
    for row in range(rows):
        own = pl.ds(row * cols, cols)
        fetches.append(pltpu.make_async_copy(v_hbm.at[row], v_ref.at[own], sems.at[2 * row]))
        fetches.append(pltpu.make_async_copy(c_hbm.at[row], c_ref.at[own], sems.at[2 * row + 1]))
    fetches.append(pltpu.make_async_copy(pair_hbm, pair_ref, sems.at[2 * rows]))
    for fetch in fetches:
        fetch.start()
    for fetch in fetches:
        fetch.wait()
    both = slice(rhs, rhs + 2)
    for row in range(rows):
        for column_ref, at in ((first_ref, row * cols), (last_ref, row * cols + cols - 1)):
            column_ref[row, 0:rhs] = v_ref[at]
            column_ref[row, both] = c_ref[at]
    for n, row in enumerate((0, rows - 1)):
        own = slice(row * cols, (row + 1) * cols)
        edge_ref[n, :, 0:rhs] = v_ref[own]
        edge_ref[n, :, both] = c_ref[own]


def use_own(out_ref, parts_ref, high, low, at):
    out_ref[at] += product(dot_nn, parts_ref, at, high, low)


def use_pair(out_ref, parts_ref, items_ref, high, low, n):
    own, other = item_blocks(items_ref[n + 1])
    out_ref[own] += product(dot_nn, parts_ref, other, high, low)
    out_ref[other] += product(dot_nt, parts_ref, own, high, low)


def use_cross(out_ref, parts_ref, items_ref, high, low, n):
    own, other = item_blocks(items_ref[n + 1])
    out_ref[own] += product(dot_nt, parts_ref, other, high, low)


def own_first_kernel(
    pair_ref, v_ref, c_ref, near_ref, cross_ref, out_ref, kept_ref, parts_ref, points_ref, spread_ref
):
    rows, cols = pair_ref.shape[:2]
    lanes = spread_ref.shape[3]

    def one(at):
        store_parts(parts_ref, at, v_ref[at])
        scaled = c_ref[at] * UNIT
        points_ref[at] = scaled
        down = [across_lanes(scaled[axis : axis + 1], lanes) for axis in range(2)]
        rhs = out_ref.shape[1]
        total = [NUGGET * v_ref[at]]

        def use(hi, lo, rows):
            both = dot_nn(parts_ref[at, :, rows], hi)
            total[0] = total[0] + (both[:rhs] + both[rhs:] + dot_nn(parts_ref[at, 0:rhs, rows], lo))

        make_tile(kept_ref, at, *down, points_ref, at, 0.0, 0.0, use)
        out_ref[at] = total[0]
        for axis in range(2):
            spread_ref[at, axis] = down[axis]

    in_turns(0, jnp.int32(rows * cols), one)
    list_items(near_ref, inner_candidates(rows, cols), pair_ref)
    in_rows, in_columns = cross_candidates(rows, cols)
    list_items(cross_ref, in_rows, pair_ref, in_columns)


def inner_first_kernel(items_ref, sum_ref, parts_ref, points_ref, spread_ref, out_ref, kept_ref):
    out_ref[...] = sum_ref[...]

    def make(n):
        code = items_ref[n + 1]
        own, other = item_blocks(code)
        rhs = out_ref.shape[1]
        total = [jnp.zeros(out_ref.shape[1:], jnp.float32)]

        def use(hi, lo, rows):
            both = dot_nn(parts_ref[other, :, rows], hi)
            total[0] = total[0] + (both[:rhs] + both[rhs:] + dot_nn(parts_ref[other, 0:rhs, rows], lo))
            back = dot_nt(parts_ref[own], hi)
            out_ref[other, :, rows] += back[:rhs] + back[rhs:] + dot_nt(parts_ref[own, 0:rhs], lo)

        make_tile(
            kept_ref, n, spread_ref.at[other, 0], spread_ref.at[other, 1], points_ref, own, *item_shifts(code), use
        )
        out_ref[own] += total[0]

    in_turns(0, items_ref[0], make)


def take_round(round_refs, rhs, parts_ref, points_ref=None, start=0):
    for side in round_refs:

        def take(at, carry, side=side, start=start):
            store_parts(parts_ref, start + at, side[at, 0:rhs])
            if points_ref is not None:
                points_ref[start + at] = side[at, rhs : rhs + 2] * UNIT
            return carry

        lax.fori_loop(0, side.shape[0], take, 0)
        start += side.shape[0]


def cross_first_kernel(
    items_ref, sum_ref, north_ref, south_ref, west_ref, east_ref, spread_ref,
    out_ref, kept_ref, parts_ref, points_ref
):
    out_ref[...] = sum_ref[...]
    take_round((north_ref, south_ref, west_ref, east_ref), sum_ref.shape[1], parts_ref, points_ref)

    def make(n):
        code = items_ref[n + 1]
        own, other = item_blocks(code)
        rhs = out_ref.shape[1]

        def use(hi, lo, rows):
            both = dot_nt(parts_ref[other], hi)
            out_ref[own, :, rows] += both[:rhs] + both[rhs:] + dot_nt(parts_ref[other, 0:rhs], lo)

        make_tile(
            kept_ref, n, spread_ref.at[own, 0], spread_ref.at[own, 1], points_ref, other, *item_shifts(code), use
        )

    in_turns(0, items_ref[0], make)


def first_share(count):
    return lax.shift_right_logical(5 * count, 3)


def near_again_kernel(items_ref, v_ref, own_ref, kept_ref, out_ref, parts_ref):
    def one(at, carry):
        store_parts(parts_ref, at, v_ref[at])
        out_ref[at] = NUGGET * v_ref[at]
        return carry

    lax.fori_loop(0, parts_ref.shape[0], one, 0, unroll=2)
    only_use(0, jnp.int32(parts_ref.shape[0]), own_ref, functools.partial(use_own, out_ref, parts_ref))
    use = functools.partial(use_pair, out_ref, parts_ref, items_ref)
    only_use(0, first_share(items_ref[0]), kept_ref, use)


def rest_again_kernel(
    near_ref, cross_ref, sum_ref, parts_ref, near_kept_ref, north_ref, south_ref, cross_kept_ref, out_ref, round_ref
):
    out_ref[...] = sum_ref[...]
    use = functools.partial(use_pair, out_ref, parts_ref, near_ref)
    only_use(first_share(near_ref[0]), near_ref[0], near_kept_ref, use)
    take_round((north_ref, south_ref), sum_ref.shape[1], round_ref)
    in_rows = cross_ref[cross_ref.shape[0] - 1]
    only_use(0, in_rows, cross_kept_ref, functools.partial(use_cross, out_ref, round_ref, cross_ref))


def cross_again_kernel(
    items_ref, sum_ref, west_ref, east_ref, kept_ref, v0_ref, v1_ref, out_ref, moments_ref, parts_ref
):
    out_ref[...] = sum_ref[...]
    start = parts_ref.shape[0] - west_ref.shape[0] - east_ref.shape[0]
    take_round((west_ref, east_ref), sum_ref.shape[1], parts_ref, start=start)
    in_rows = items_ref[items_ref.shape[0] - 1]
    only_use(in_rows, items_ref[0], kept_ref, functools.partial(use_cross, out_ref, parts_ref, items_ref))
    zero = jnp.zeros(out_ref.shape[1:], jnp.float32)

    def gather(at, sums):
        w0, w1, w2 = v0_ref[at], v1_ref[at], out_ref[at]
        terms = (w0 * w0, w0 * w1, w1 * w1, w1 * w2)
        return tuple(s + t for s, t in zip(sums, terms))

    sums = lax.fori_loop(0, out_ref.shape[0], gather, (zero,) * 4)
    lanes = moments_ref.shape[2]
    folded = [sum(s[:, left : left + lanes] for left in range(0, s.shape[1], lanes)) for s in sums]
    stacked = jnp.concatenate(folded, axis=0)
    line = jnp.sum(jnp.transpose(stacked), axis=0, keepdims=True)
    moments_ref[...] = jnp.broadcast_to(line[None], moments_ref.shape)


def final_kernel(moments_ref, v0_ref, v1_ref, v2_ref, solution_ref, residual_ref):
    rhs, points = v0_ref.shape[1:]
    line = moments_ref[0]
    for at in range(1, moments_ref.shape[0]):
        line = line + moments_ref[at]
    table = across_lanes(line, line.shape[1])
    m00, m01, m11, m12 = (table[k * rhs : (k + 1) * rhs] for k in range(4))
    a = m00 / m01
    norm = m00 - 2.0 * a * m01 + a * a * m11
    grow = 1.0 + norm / m00
    step = norm / (grow * (grow * m01 - 2.0 * a * m11) + a * a * m12)
    first = jnp.concatenate([a + step * grow] * (points // line.shape[1]), axis=1)
    second = jnp.concatenate([step * a] * (points // line.shape[1]), axis=1)

    def one(at, carry):
        w0, w1, w2 = v0_ref[at], v1_ref[at], v2_ref[at]
        solution_ref[at] = first * w0 - second * w1
        residual_ref[at] = w0 - first * w1 + second * w2
        return carry

    lax.fori_loop(0, v0_ref.shape[0], one, 0)


def swapped(first, last, axis):
    count = lax.axis_size(axis)
    even = lax.rem(lax.axis_index(axis), 2) == 0
    swap_up = [(i, i ^ 1) for i in range(count) if i ^ 1 < count]
    swap_down = [(i, ((i + 1) ^ 1) - 1) for i in range(count) if 0 <= ((i + 1) ^ 1) - 1 < count]
    got_up = lax.ppermute(jnp.where(even, last, first), axis, swap_up)
    got_down = lax.ppermute(jnp.where(even, first, last), axis, swap_down)
    return jnp.where(even, got_down, got_up), jnp.where(even, got_up, got_down)


def on_device(kernel, outputs, inputs, scratch=(), listed=False, products=0, made=0, where=pltpu.VMEM):
    vmem = pl.BlockSpec(memory_space=pltpu.VMEM)
    smem = pl.BlockSpec(memory_space=pltpu.SMEM)
    source = pl.BlockSpec(memory_space=where)
    return pl.pallas_call(
        kernel,
        out_shape=tuple(outputs),
        in_specs=[smem if listed and x.dtype == jnp.int32 else source for x in inputs],
        out_specs=tuple(smem if out.dtype == jnp.int32 else vmem for out in outputs),
        scratch_shapes=list(scratch),
        compiler_params=pltpu.CompilerParams(vmem_limit_bytes=VMEM_LIMIT),
        cost_estimate=pl.CostEstimate(
            flops=products, transcendentals=made, bytes_accessed=sum(4 * x.size for x in inputs)
        ),
        name=kernel.__name__,
    )(*inputs)


def tiles(count, points):
    return jax.ShapeDtypeStruct((count, 2, points, points), jnp.bfloat16)


def per_device(right_side, coords, pair_list):
    pair_list = jnp.transpose(pair_list, (1, 2, 0))
    rows, cols, rhs, points = right_side.shape
    blocks = rows * cols
    devices = lax.axis_size("region") * lax.axis_size("tile")
    lanes = 128
    f32, bf16, i32 = jnp.float32, jnp.bfloat16, jnp.int32
    array = jax.ShapeDtypeStruct
    halo = 2 * rows + 2 * (cols + 2)
    near_count = len(inner_candidates(rows, cols))
    cross_count = sum(len(part) for part in cross_candidates(rows, cols))
    field = array((blocks, rhs, points), f32)
    column = array((rows, rhs + 2, points), f32)
    parts_round = pltpu.VMEM((halo, 2 * rhs, points), bf16)
    each = 6 * rhs * points * points

    def columns_round(first, last, north, south):
        first = jnp.concatenate([north[:1], first, south[:1]], axis=0)
        last = jnp.concatenate([north[cols - 1 :], last, south[cols - 1 :]], axis=0)
        return swapped(first, last, "tile")

    fetched = (
        column, column, array((2, cols, rhs + 2, points), f32), field, array((blocks, 2, points), f32),
        array(pair_list.shape, i32),
    )
    first, last, edges, w0, stations, pairs = on_device(
        pack_kernel, fetched,
        tuple(pltpu.with_memory_space_constraint(x, pltpu.HBM) for x in (right_side, coords, pair_list)),
        (pltpu.SemaphoreType.DMA((2 * rows + 1,)),), where=pltpu.HBM,
    )
    north, south = swapped(edges[0], edges[1], "region")
    parts_field = array((blocks, 2 * rhs, points), bf16)
    near_items, cross_items, part, own_tiles, parts, own_points, spread = on_device(
        own_first_kernel,
        (array((near_count + 3,), i32), array((cross_count + 3,), i32), field, tiles(blocks, points), parts_field,
         array((blocks, 2, points), f32), array((blocks, 2, points, lanes), f32)),
        (pairs, w0, stations), listed=True, products=blocks * each, made=blocks * 2 * points * points,
    )
    north, south, part = lax.optimization_barrier((north, south, part))
    west, east = columns_round(first, last, north, south)
    part, near_tiles = on_device(
        inner_first_kernel, (field, tiles(near_count + 2, points)), (near_items, part, parts, own_points, spread),
        (), True, near_count * each, near_count * 2 * points * points,
    )
    w1, cross_tiles = on_device(
        cross_first_kernel, (field, tiles(cross_count + 2, points)),
        (cross_items, part, north, south, west, east, spread),
        (parts_round, pltpu.VMEM((halo, 2, points), f32)), True,
        cross_count * each, cross_count * 2 * points * points,
    )
    w1_grid = w1.reshape(right_side.shape)
    north, south = swapped(w1_grid[0], w1_grid[rows - 1], "region")
    part, parts = on_device(
        near_again_kernel, (field, parts_field), (near_items, w1, own_tiles, near_tiles), (), True,
        (blocks + near_count) * each,
    )
    north, south, part = lax.optimization_barrier((north, south, part))
    west, east = columns_round(w1_grid[:, 0], w1_grid[:, cols - 1], north, south)
    (part,) = on_device(
        rest_again_kernel, (field,),
        (near_items, cross_items, part, parts, near_tiles, north, south, cross_tiles), (parts_round,), True,
        near_count * each,
    )
    w2, moments = on_device(
        cross_again_kernel, (field, array((devices, 1, 4 * rhs), f32)),
        (cross_items, part, west, east, cross_tiles, w0, w1), (parts_round,), True, cross_count * each,
    )
    moments = lax.all_to_all(moments, ("region", "tile"), 0, 0)
    solution, residual = on_device(final_kernel, (field, field), (moments, w0, w1, w2))
    return solution.reshape(right_side.shape), residual.reshape(right_side.shape)


def solution(mesh):
    placed = (
        P("region", "tile", None, None),
        P("region", "tile", None, None),
        P(None, "region", "tile"),
    )
    return jax.shard_map(
        per_device,
        mesh=mesh,
        in_specs=placed,
        out_specs=(P("region", "tile", None, None), P("region", "tile", None, None)),
        check_vma=False,
    )
```

```python
import functools

import jax
import jax.numpy as jnp
from jax import lax
from jax.experimental import pallas as pl
from jax.experimental.pallas import tpu as pltpu
from jax.sharding import PartitionSpec as P

LENGTH_SCALE = 0.2
TAPER_RANGE = 0.5
NUGGET = 3.0
OFFSETS = ((0, 1), (1, 0), (1, 1), (1, -1), (0, -1), (-1, 0), (-1, -1), (-1, 1))
UNIT = 1.4426950408889634 / LENGTH_SCALE
EDGE = UNIT * TAPER_RANGE
WEIGHT = 4.0 * 2.0**-EDGE / EDGE**5
CHUNK = 128
VMEM_LIMIT = 10 * 1024 * 1024


def dot_nn(a, b):
    return lax.dot_general(a, b, (((1,), (0,)), ((), ())), preferred_element_type=jnp.float32)


def dot_nt(a, b):
    return lax.dot_general(a, b, (((1,), (1,)), ((), ())), preferred_element_type=jnp.float32)


def split_hi_lo(values):
    hi = values.astype(jnp.bfloat16)
    lo = (values - hi.astype(jnp.float32)).astype(jnp.bfloat16)
    return hi, lo


def across_lanes(row, lanes):
    return jnp.transpose(jnp.broadcast_to(row, (lanes, row.shape[1])))


def tile_rows(rows, down_x, down_y, points_ref, along, shift_a, shift_b):
    points = points_ref.shape[2]
    lanes = down_x.shape[1]
    row_x = points_ref[along, 0:1] - shift_a
    row_y = points_ref[along, 1:2] - shift_b
    halves = []
    for left in range(0, points, lanes):
        cols = slice(left, left + lanes)
        gap_x = down_x[rows] - row_x[:, cols]
        gap_y = down_y[rows] - row_y[:, cols]
        square = jnp.maximum(gap_x * gap_x + gap_y * gap_y, 1e-30)
        rest = jnp.maximum(EDGE - square * lax.rsqrt(square), 0.0)
        rest2 = rest * rest
        halves.append((jnp.exp2(rest) * (rest2 * rest2)) * (1.25 * EDGE - rest))
    return split_hi_lo(jnp.concatenate(halves, axis=1))


def make_tile(keep_ref, slot, down_x, down_y, points_ref, along, shift_a, shift_b, use):
    points = keep_ref.shape[2]
    for start in range(0, points, CHUNK):
        rows = slice(start, start + CHUNK)
        hi, lo = tile_rows(rows, down_x, down_y, points_ref, along, shift_a, shift_b)
        keep_ref[slot, 0, rows] = hi
        keep_ref[slot, 1, rows] = lo
        use(hi, lo, rows)


def product(dot, parts_ref, at, high, low):
    rhs = parts_ref.shape[1] // 2
    both = dot(parts_ref[at], high)
    cross = dot(parts_ref[at, 0:rhs], low)
    return both[:rhs] + both[rhs:] + cross


def store_parts(parts_ref, at, values):
    rhs = values.shape[0]
    hi, lo = split_hi_lo(values * WEIGHT)
    parts_ref[at, 0:rhs] = hi
    parts_ref[at, rhs : 2 * rhs] = lo


def in_turns(first, last, step, log2s=(3, 2, 1, 0)):
    for log2 in log2s:
        turns = lax.shift_right_logical(last - first, log2)

        def one_turn(turn, carry, first=first, log2=log2):
            for n in range(1 << log2):
                step(first + (turn << log2) + n)
            return carry

        lax.fori_loop(0, turns, one_turn, 0)
        first = first + (turns << log2)


def only_use(first, last, kept_ref, use):
    in_turns(first, last, lambda n: use(kept_ref[n, 0], kept_ref[n, 1], n), (4, 3, 2, 1, 0))


def item_code(own, other, shift_a, shift_b):
    return own + 64 * other + 4096 * (shift_a + 1) + 16384 * (shift_b + 1)


NO_ITEM = item_code(0, 0, 2, 2)


def item_blocks_of(code):
    return code % 64, code // 64 % 64


def item_blocks(code):
    return lax.bitwise_and(code, 63), lax.bitwise_and(lax.shift_right_logical(code, 6), 63)


def item_shifts(code):
    shift_a = lax.bitwise_and(lax.shift_right_logical(code, 12), 3) - 1
    shift_b = lax.shift_right_logical(code, 14) - 1
    return shift_a.astype(jnp.float32) * UNIT, shift_b.astype(jnp.float32) * UNIT


def list_items(items_ref, candidates, pair_ref, more=()):
    cols = pair_ref.shape[1]
    count = jnp.int32(0)
    for part in (candidates, more):
        for k, own, code in part:
            items_ref[count + 1] = code
            count = count + jnp.where(pair_ref[own // cols, own % cols, k] > 0, 1, 0)
        if part is candidates:
            items_ref[len(candidates) + len(more) + 2] = count
    items_ref[0] = count
    items_ref[count + 1] = NO_ITEM


def inner_candidates(rows, cols):
    found = []
    for k in range(4):
        shift_a, shift_b = OFFSETS[k]
        for a in range(rows):
            for b in range(cols):
                if 0 <= a + shift_a < rows and 0 <= b + shift_b < cols:
                    own = a * cols + b
                    other = own + shift_a * cols + shift_b
                    found.append((k, own, item_code(own, other, shift_a, shift_b)))
    return found


def cross_candidates(rows, cols):
    places = [(-1, b) for b in range(cols)] + [(rows, b) for b in range(cols)]
    places += [(a, -1) for a in range(-1, rows + 1)] + [(a, cols) for a in range(-1, rows + 1)]
    found = []
    for k in range(8):
        shift_a, shift_b = OFFSETS[k]
        for a in range(rows):
            for b in range(cols):
                place = (a + shift_a, b + shift_b)
                if place in places:
                    own = a * cols + b
                    found.append((k, own, item_code(own, places.index(place), -shift_a, -shift_b)))
    in_rows = [item for item in found if item_blocks_of(item[2])[1] < 2 * cols]
    return in_rows, [item for item in found if item not in in_rows]


def pack_kernel(v_hbm, c_hbm, pair_hbm, first_ref, last_ref, edge_ref, v_ref, c_ref, pair_ref, sems):
    rows, cols, rhs = v_hbm.shape[:3]
    fetches = []
    for row in range(rows):
        own = pl.ds(row * cols, cols)
        fetches.append(pltpu.make_async_copy(v_hbm.at[row], v_ref.at[own], sems.at[2 * row]))
        fetches.append(pltpu.make_async_copy(c_hbm.at[row], c_ref.at[own], sems.at[2 * row + 1]))
    fetches.append(pltpu.make_async_copy(pair_hbm, pair_ref, sems.at[2 * rows]))
    for fetch in fetches:
        fetch.start()
    for fetch in fetches:
        fetch.wait()
    both = slice(rhs, rhs + 2)
    for row in range(rows):
        for column_ref, at in ((first_ref, row * cols), (last_ref, row * cols + cols - 1)):
            column_ref[row, 0:rhs] = v_ref[at]
            column_ref[row, both] = c_ref[at]
    for n, row in enumerate((0, rows - 1)):
        own = slice(row * cols, (row + 1) * cols)
        edge_ref[n, :, 0:rhs] = v_ref[own]
        edge_ref[n, :, both] = c_ref[own]


def use_own(out_ref, parts_ref, high, low, at):
    out_ref[at] += product(dot_nn, parts_ref, at, high, low)


def use_pair(out_ref, parts_ref, items_ref, high, low, n):
    own, other = item_blocks(items_ref[n + 1])
    out_ref[own] += product(dot_nn, parts_ref, other, high, low)
    out_ref[other] += product(dot_nt, parts_ref, own, high, low)


def use_cross(out_ref, parts_ref, items_ref, high, low, n):
    own, other = item_blocks(items_ref[n + 1])
    out_ref[own] += product(dot_nt, parts_ref, other, high, low)


def own_first_kernel(
    pair_ref, v_ref, c_ref, near_ref, cross_ref, out_ref, kept_ref, parts_ref, points_ref, spread_ref
):
    rows, cols = pair_ref.shape[:2]
    lanes = spread_ref.shape[3]

    def one(at):
        store_parts(parts_ref, at, v_ref[at])
        scaled = c_ref[at] * UNIT
        points_ref[at] = scaled
        down = [across_lanes(scaled[axis : axis + 1], lanes) for axis in range(2)]
        rhs = out_ref.shape[1]
        total = [NUGGET * v_ref[at]]

        def use(hi, lo, rows):
            both = dot_nn(parts_ref[at, :, rows], hi)
            total[0] = total[0] + (both[:rhs] + both[rhs:] + dot_nn(parts_ref[at, 0:rhs, rows], lo))

        make_tile(kept_ref, at, *down, points_ref, at, 0.0, 0.0, use)
        out_ref[at] = total[0]
        for axis in range(2):
            spread_ref[at, axis] = down[axis]

    in_turns(0, jnp.int32(rows * cols), one)
    list_items(near_ref, inner_candidates(rows, cols), pair_ref)
    in_rows, in_columns = cross_candidates(rows, cols)
    list_items(cross_ref, in_rows, pair_ref, in_columns)


def inner_first_kernel(items_ref, sum_ref, parts_ref, points_ref, spread_ref, out_ref, kept_ref):
    out_ref[...] = sum_ref[...]

    def make(n):
        code = items_ref[n + 1]
        own, other = item_blocks(code)
        rhs = out_ref.shape[1]
        total = [jnp.zeros(out_ref.shape[1:], jnp.float32)]

        def use(hi, lo, rows):
            both = dot_nn(parts_ref[other, :, rows], hi)
            total[0] = total[0] + (both[:rhs] + both[rhs:] + dot_nn(parts_ref[other, 0:rhs, rows], lo))
            back = dot_nt(parts_ref[own], hi)
            out_ref[other, :, rows] += back[:rhs] + back[rhs:] + dot_nt(parts_ref[own, 0:rhs], lo)

        make_tile(
            kept_ref, n, spread_ref.at[other, 0], spread_ref.at[other, 1], points_ref, own, *item_shifts(code), use
        )
        out_ref[own] += total[0]

    in_turns(0, items_ref[0], make)


def take_round(round_refs, rhs, parts_ref, points_ref=None, start=0):
    for side in round_refs:

        def take(at, carry, side=side, start=start):
            store_parts(parts_ref, start + at, side[at, 0:rhs])
            if points_ref is not None:
                points_ref[start + at] = side[at, rhs : rhs + 2] * UNIT
            return carry

        lax.fori_loop(0, side.shape[0], take, 0)
        start += side.shape[0]


def cross_first_kernel(
    items_ref, sum_ref, north_ref, south_ref, west_ref, east_ref, spread_ref,
    out_ref, kept_ref, parts_ref, points_ref
):
    out_ref[...] = sum_ref[...]
    take_round((north_ref, south_ref, west_ref, east_ref), sum_ref.shape[1], parts_ref, points_ref)

    def make(n):
        code = items_ref[n + 1]
        own, other = item_blocks(code)
        rhs = out_ref.shape[1]

        def use(hi, lo, rows):
            both = dot_nt(parts_ref[other], hi)
            out_ref[own, :, rows] += both[:rhs] + both[rhs:] + dot_nt(parts_ref[other, 0:rhs], lo)

        make_tile(
            kept_ref, n, spread_ref.at[own, 0], spread_ref.at[own, 1], points_ref, other, *item_shifts(code), use
        )

    in_turns(0, items_ref[0], make)


def first_share(count):
    return lax.shift_right_logical(5 * count, 3)


def near_again_kernel(items_ref, v_ref, own_ref, kept_ref, out_ref, parts_ref):
    def one(at, carry):
        store_parts(parts_ref, at, v_ref[at])
        out_ref[at] = NUGGET * v_ref[at]
        return carry

    lax.fori_loop(0, parts_ref.shape[0], one, 0, unroll=2)
    only_use(0, jnp.int32(parts_ref.shape[0]), own_ref, functools.partial(use_own, out_ref, parts_ref))
    use = functools.partial(use_pair, out_ref, parts_ref, items_ref)
    only_use(0, first_share(items_ref[0]), kept_ref, use)


def rest_again_kernel(
    near_ref, cross_ref, sum_ref, parts_ref, near_kept_ref, north_ref, south_ref, cross_kept_ref, v0_ref, v1_ref,
    out_ref, terms_ref, round_ref
):
    out_ref[...] = sum_ref[...]
    use = functools.partial(use_pair, out_ref, parts_ref, near_ref)
    only_use(first_share(near_ref[0]), near_ref[0], near_kept_ref, use)
    take_round((north_ref, south_ref), sum_ref.shape[1], round_ref)
    in_rows = cross_ref[cross_ref.shape[0] - 1]
    only_use(0, in_rows, cross_kept_ref, functools.partial(use_cross, out_ref, round_ref, cross_ref))

    def gather(at, sums):
        w0, w1 = v0_ref[at], v1_ref[at]
        return tuple(s + t for s, t in zip(sums, (w0 * w0, w0 * w1, w1 * w1)))

    zero = jnp.zeros(out_ref.shape[1:], jnp.float32)
    for n, total in enumerate(lax.fori_loop(0, out_ref.shape[0], gather, (zero,) * 3)):
        terms_ref[n] = total


def cross_again_kernel(
    items_ref, sum_ref, west_ref, east_ref, kept_ref, terms_ref, v1_ref, out_ref, moments_ref, parts_ref
):
    out_ref[...] = sum_ref[...]
    start = parts_ref.shape[0] - west_ref.shape[0] - east_ref.shape[0]
    take_round((west_ref, east_ref), sum_ref.shape[1], parts_ref, start=start)
    in_rows = items_ref[items_ref.shape[0] - 1]
    only_use(in_rows, items_ref[0], kept_ref, functools.partial(use_cross, out_ref, parts_ref, items_ref))
    zero = jnp.zeros(out_ref.shape[1:], jnp.float32)
    last = lax.fori_loop(0, out_ref.shape[0], lambda at, total: total + v1_ref[at] * out_ref[at], zero)
    sums = [terms_ref[n] for n in range(3)] + [last]
    lanes = moments_ref.shape[2]
    folded = [sum(s[:, left : left + lanes] for left in range(0, s.shape[1], lanes)) for s in sums]
    stacked = jnp.concatenate(folded, axis=0)
    line = jnp.sum(jnp.transpose(stacked), axis=0, keepdims=True)
    moments_ref[...] = jnp.broadcast_to(line[None], moments_ref.shape)


def final_kernel(moments_ref, v0_ref, v1_ref, v2_ref, solution_ref, residual_ref):
    rhs, points = v0_ref.shape[1:]
    line = moments_ref[0]
    for at in range(1, moments_ref.shape[0]):
        line = line + moments_ref[at]
    table = across_lanes(line, line.shape[1])
    m00, m01, m11, m12 = (table[k * rhs : (k + 1) * rhs] for k in range(4))
    a = m00 / m01
    norm = m00 - 2.0 * a * m01 + a * a * m11
    grow = 1.0 + norm / m00
    step = norm / (grow * (grow * m01 - 2.0 * a * m11) + a * a * m12)
    first = jnp.concatenate([a + step * grow] * (points // line.shape[1]), axis=1)
    second = jnp.concatenate([step * a] * (points // line.shape[1]), axis=1)

    def one(at, carry):
        w0, w1, w2 = v0_ref[at], v1_ref[at], v2_ref[at]
        solution_ref[at] = first * w0 - second * w1
        residual_ref[at] = w0 - first * w1 + second * w2
        return carry

    lax.fori_loop(0, v0_ref.shape[0], one, 0)


def swapped(first, last, axis):
    count = lax.axis_size(axis)
    even = lax.rem(lax.axis_index(axis), 2) == 0
    swap_up = [(i, i ^ 1) for i in range(count) if i ^ 1 < count]
    swap_down = [(i, ((i + 1) ^ 1) - 1) for i in range(count) if 0 <= ((i + 1) ^ 1) - 1 < count]
    got_up = lax.ppermute(jnp.where(even, last, first), axis, swap_up)
    got_down = lax.ppermute(jnp.where(even, first, last), axis, swap_down)
    return jnp.where(even, got_down, got_up), jnp.where(even, got_up, got_down)


def on_device(kernel, outputs, inputs, scratch=(), listed=False, products=0, made=0, where=pltpu.VMEM):
    vmem = pl.BlockSpec(memory_space=pltpu.VMEM)
    smem = pl.BlockSpec(memory_space=pltpu.SMEM)
    source = pl.BlockSpec(memory_space=where)
    return pl.pallas_call(
        kernel,
        out_shape=tuple(outputs),
        in_specs=[smem if listed and x.dtype == jnp.int32 else source for x in inputs],
        out_specs=tuple(smem if out.dtype == jnp.int32 else vmem for out in outputs),
        scratch_shapes=list(scratch),
        compiler_params=pltpu.CompilerParams(vmem_limit_bytes=VMEM_LIMIT),
        cost_estimate=pl.CostEstimate(
            flops=products, transcendentals=made, bytes_accessed=sum(4 * x.size for x in inputs)
        ),
        name=kernel.__name__,
    )(*inputs)


def tiles(count, points):
    return jax.ShapeDtypeStruct((count, 2, points, points), jnp.bfloat16)


def per_device(right_side, coords, pair_list):
    pair_list = jnp.transpose(pair_list, (1, 2, 0))
    rows, cols, rhs, points = right_side.shape
    blocks = rows * cols
    devices = lax.axis_size("region") * lax.axis_size("tile")
    lanes = 128
    f32, bf16, i32 = jnp.float32, jnp.bfloat16, jnp.int32
    array = jax.ShapeDtypeStruct
    halo = 2 * rows + 2 * (cols + 2)
    near_count = len(inner_candidates(rows, cols))
    cross_count = sum(len(part) for part in cross_candidates(rows, cols))
    field = array((blocks, rhs, points), f32)
    column = array((rows, rhs + 2, points), f32)
    parts_round = pltpu.VMEM((halo, 2 * rhs, points), bf16)
    each = 6 * rhs * points * points

    def columns_round(first, last, north, south):
        first = jnp.concatenate([north[:1], first, south[:1]], axis=0)
        last = jnp.concatenate([north[cols - 1 :], last, south[cols - 1 :]], axis=0)
        return swapped(first, last, "tile")

    fetched = (
        column, column, array((2, cols, rhs + 2, points), f32), field, array((blocks, 2, points), f32),
        array(pair_list.shape, i32),
    )
    first, last, edges, w0, stations, pairs = on_device(
        pack_kernel, fetched,
        tuple(pltpu.with_memory_space_constraint(x, pltpu.HBM) for x in (right_side, coords, pair_list)),
        (pltpu.SemaphoreType.DMA((2 * rows + 1,)),), where=pltpu.HBM,
    )
    north, south = swapped(edges[0], edges[1], "region")
    parts_field = array((blocks, 2 * rhs, points), bf16)
    near_items, cross_items, part, own_tiles, parts, own_points, spread = on_device(
        own_first_kernel,
        (array((near_count + 3,), i32), array((cross_count + 3,), i32), field, tiles(blocks, points), parts_field,
         array((blocks, 2, points), f32), array((blocks, 2, points, lanes), f32)),
        (pairs, w0, stations), listed=True, products=blocks * each, made=blocks * 2 * points * points,
    )
    north, south, part = lax.optimization_barrier((north, south, part))
    west, east = columns_round(first, last, north, south)
    part, near_tiles = on_device(
        inner_first_kernel, (field, tiles(near_count + 2, points)), (near_items, part, parts, own_points, spread),
        (), True, near_count * each, near_count * 2 * points * points,
    )
    w1, cross_tiles = on_device(
        cross_first_kernel, (field, tiles(cross_count + 2, points)),
        (cross_items, part, north, south, west, east, spread),
        (parts_round, pltpu.VMEM((halo, 2, points), f32)), True,
        cross_count * each, cross_count * 2 * points * points,
    )
    w1_grid = w1.reshape(right_side.shape)
    north, south = swapped(w1_grid[0], w1_grid[rows - 1], "region")
    part, parts = on_device(
        near_again_kernel, (field, parts_field), (near_items, w1, own_tiles, near_tiles), (), True,
        (blocks + near_count) * each,
    )
    north, south, part = lax.optimization_barrier((north, south, part))
    west, east = columns_round(w1_grid[:, 0], w1_grid[:, cols - 1], north, south)
    part, terms = on_device(
        rest_again_kernel, (field, array((3, rhs, points), f32)),
        (near_items, cross_items, part, parts, near_tiles, north, south, cross_tiles, w0, w1), (parts_round,), True,
        near_count * each,
    )
    w2, moments = on_device(
        cross_again_kernel, (field, array((devices, 1, 4 * rhs), f32)),
        (cross_items, part, west, east, cross_tiles, terms, w1), (parts_round,), True, cross_count * each,
    )
    moments = lax.all_to_all(moments, ("region", "tile"), 0, 0)
    solution, residual = on_device(final_kernel, (field, field), (moments, w0, w1, w2))
    return solution.reshape(right_side.shape), residual.reshape(right_side.shape)


def solution(mesh):
    placed = (
        P("region", "tile", None, None),
        P("region", "tile", None, None),
        P(None, "region", "tile"),
    )
    return jax.shard_map(
        per_device,
        mesh=mesh,
        in_specs=placed,
        out_specs=(P("region", "tile", None, None), P("region", "tile", None, None)),
        check_vma=False,
    )
```

```python
import functools

import jax
import jax.numpy as jnp
from jax import lax
from jax.experimental import pallas as pl
from jax.experimental.pallas import tpu as pltpu
from jax.sharding import PartitionSpec as P

LENGTH_SCALE = 0.2
TAPER_RANGE = 0.5
NUGGET = 3.0
OFFSETS = ((0, 1), (1, 0), (1, 1), (1, -1), (0, -1), (-1, 0), (-1, -1), (-1, 1))
UNIT = 1.4426950408889634 / LENGTH_SCALE
EDGE = UNIT * TAPER_RANGE
WEIGHT = 4.0 * 2.0**-EDGE / EDGE**5
CHUNK = 128
VMEM_LIMIT = 10 * 1024 * 1024


def dot_nn(a, b):
    return lax.dot_general(a, b, (((1,), (0,)), ((), ())), preferred_element_type=jnp.float32)


def dot_nt(a, b):
    return lax.dot_general(a, b, (((1,), (1,)), ((), ())), preferred_element_type=jnp.float32)


def split_hi_lo(values):
    hi = values.astype(jnp.bfloat16)
    lo = (values - hi.astype(jnp.float32)).astype(jnp.bfloat16)
    return hi, lo


def across_lanes(row, lanes):
    return jnp.transpose(jnp.broadcast_to(row, (lanes, row.shape[1])))


def tile_rows(rows, down_x, down_y, points_ref, along, shift_a, shift_b):
    points = points_ref.shape[2]
    lanes = down_x.shape[1]
    row_x = points_ref[along, 0:1] - shift_a
    row_y = points_ref[along, 1:2] - shift_b
    halves = []
    for left in range(0, points, lanes):
        cols = slice(left, left + lanes)
        gap_x = down_x[rows] - row_x[:, cols]
        gap_y = down_y[rows] - row_y[:, cols]
        square = jnp.maximum(gap_x * gap_x + gap_y * gap_y, 1e-30)
        rest = jnp.maximum(EDGE - square * lax.rsqrt(square), 0.0)
        rest2 = rest * rest
        halves.append((jnp.exp2(rest) * (rest2 * rest2)) * (1.25 * EDGE - rest))
    return split_hi_lo(jnp.concatenate(halves, axis=1))


def make_tile(keep_ref, slot, down_x, down_y, points_ref, along, shift_a, shift_b, use):
    points = keep_ref.shape[2]
    for start in range(0, points, CHUNK):
        rows = slice(start, start + CHUNK)
        hi, lo = tile_rows(rows, down_x, down_y, points_ref, along, shift_a, shift_b)
        keep_ref[slot, 0, rows] = hi
        keep_ref[slot, 1, rows] = lo
        use(hi, lo, rows)


def product(dot, parts_ref, at, high, low):
    rhs = parts_ref.shape[1] // 2
    both = dot(parts_ref[at], high)
    cross = dot(parts_ref[at, 0:rhs], low)
    return both[:rhs] + both[rhs:] + cross


def store_parts(parts_ref, at, values):
    rhs = values.shape[0]
    hi, lo = split_hi_lo(values * WEIGHT)
    parts_ref[at, 0:rhs] = hi
    parts_ref[at, rhs : 2 * rhs] = lo


def in_turns(first, last, step, log2s=(3, 2, 1, 0)):
    for log2 in log2s:
        turns = lax.shift_right_logical(last - first, log2)

        def one_turn(turn, carry, first=first, log2=log2):
            for n in range(1 << log2):
                step(first + (turn << log2) + n)
            return carry

        lax.fori_loop(0, turns, one_turn, 0)
        first = first + (turns << log2)


def only_use(first, last, kept_ref, use):
    in_turns(first, last, lambda n: use(kept_ref[n, 0], kept_ref[n, 1], n), (4, 3, 2, 1, 0))


def item_code(own, other, shift_a, shift_b):
    return own + 64 * other + 4096 * (shift_a + 1) + 16384 * (shift_b + 1)


NO_ITEM = item_code(0, 0, 2, 2)


def item_blocks_of(code):
    return code % 64, code // 64 % 64


def item_blocks(code):
    return lax.bitwise_and(code, 63), lax.bitwise_and(lax.shift_right_logical(code, 6), 63)


def item_shifts(code):
    shift_a = lax.bitwise_and(lax.shift_right_logical(code, 12), 3) - 1
    shift_b = lax.shift_right_logical(code, 14) - 1
    return shift_a.astype(jnp.float32) * UNIT, shift_b.astype(jnp.float32) * UNIT


def list_items(items_ref, candidates, pair_ref, more=()):
    cols = pair_ref.shape[1]
    count = jnp.int32(0)
    for part in (candidates, more):
        for k, own, code in part:
            items_ref[count + 1] = code
            count = count + jnp.where(pair_ref[own // cols, own % cols, k] > 0, 1, 0)
        if part is candidates:
            items_ref[len(candidates) + len(more) + 2] = count
    items_ref[0] = count
    items_ref[count + 1] = NO_ITEM


def inner_candidates(rows, cols):
    found = []
    for k in range(4):
        shift_a, shift_b = OFFSETS[k]
        for a in range(rows):
            for b in range(cols):
                if 0 <= a + shift_a < rows and 0 <= b + shift_b < cols:
                    own = a * cols + b
                    other = own + shift_a * cols + shift_b
                    found.append((k, own, item_code(own, other, shift_a, shift_b)))
    return found


def cross_candidates(rows, cols):
    places = [(-1, b) for b in range(cols)] + [(rows, b) for b in range(cols)]
    places += [(a, -1) for a in range(-1, rows + 1)] + [(a, cols) for a in range(-1, rows + 1)]
    found = []
    for k in range(8):
        shift_a, shift_b = OFFSETS[k]
        for a in range(rows):
            for b in range(cols):
                place = (a + shift_a, b + shift_b)
                if place in places:
                    own = a * cols + b
                    found.append((k, own, item_code(own, places.index(place), -shift_a, -shift_b)))
    in_rows = [item for item in found if item_blocks_of(item[2])[1] < 2 * cols]
    return in_rows, [item for item in found if item not in in_rows]


def pack_kernel(v_hbm, c_hbm, pair_hbm, first_ref, last_ref, edge_ref, v_ref, c_ref, pair_ref, sems):
    rows, cols, rhs = v_hbm.shape[:3]
    fetches = []
    for row in range(rows):
        own = pl.ds(row * cols, cols)
        fetches.append(pltpu.make_async_copy(v_hbm.at[row], v_ref.at[own], sems.at[2 * row]))
        fetches.append(pltpu.make_async_copy(c_hbm.at[row], c_ref.at[own], sems.at[2 * row + 1]))
    fetches.append(pltpu.make_async_copy(pair_hbm, pair_ref, sems.at[2 * rows]))
    for fetch in fetches:
        fetch.start()
    for fetch in fetches:
        fetch.wait()
    both = slice(rhs, rhs + 2)
    for row in range(rows):
        for column_ref, at in ((first_ref, row * cols), (last_ref, row * cols + cols - 1)):
            column_ref[row, 0:rhs] = v_ref[at]
            column_ref[row, both] = c_ref[at]
    for n, row in enumerate((0, rows - 1)):
        own = slice(row * cols, (row + 1) * cols)
        edge_ref[n, :, 0:rhs] = v_ref[own]
        edge_ref[n, :, both] = c_ref[own]


def use_own(out_ref, parts_ref, high, low, at):
    out_ref[at] += product(dot_nn, parts_ref, at, high, low)


def use_pair(out_ref, parts_ref, items_ref, high, low, n):
    own, other = item_blocks(items_ref[n + 1])
    out_ref[own] += product(dot_nn, parts_ref, other, high, low)
    out_ref[other] += product(dot_nt, parts_ref, own, high, low)


def use_cross(out_ref, parts_ref, items_ref, high, low, n):
    own, other = item_blocks(items_ref[n + 1])
    out_ref[own] += product(dot_nt, parts_ref, other, high, low)


def own_first_kernel(
    pair_ref, v_ref, c_ref, near_ref, cross_ref, out_ref, kept_ref, parts_ref, points_ref, spread_ref
):
    rows, cols = pair_ref.shape[:2]
    lanes = spread_ref.shape[3]

    def one(at):
        store_parts(parts_ref, at, v_ref[at])
        scaled = c_ref[at] * UNIT
        points_ref[at] = scaled
        down = [across_lanes(scaled[axis : axis + 1], lanes) for axis in range(2)]
        rhs = out_ref.shape[1]
        total = [NUGGET * v_ref[at]]

        def use(hi, lo, rows):
            both = dot_nn(parts_ref[at, :, rows], hi)
            total[0] = total[0] + (both[:rhs] + both[rhs:] + dot_nn(parts_ref[at, 0:rhs, rows], lo))

        make_tile(kept_ref, at, *down, points_ref, at, 0.0, 0.0, use)
        out_ref[at] = total[0]
        for axis in range(2):
            spread_ref[at, axis] = down[axis]

    in_turns(0, jnp.int32(rows * cols), one)
    list_items(near_ref, inner_candidates(rows, cols), pair_ref)
    in_rows, in_columns = cross_candidates(rows, cols)
    list_items(cross_ref, in_rows, pair_ref, in_columns)


def inner_first_kernel(items_ref, sum_ref, parts_ref, points_ref, spread_ref, out_ref, kept_ref):
    out_ref[...] = sum_ref[...]

    def make(n):
        code = items_ref[n + 1]
        own, other = item_blocks(code)
        rhs = out_ref.shape[1]
        total = [jnp.zeros(out_ref.shape[1:], jnp.float32)]

        def use(hi, lo, rows):
            both = dot_nn(parts_ref[other, :, rows], hi)
            total[0] = total[0] + (both[:rhs] + both[rhs:] + dot_nn(parts_ref[other, 0:rhs, rows], lo))
            back = dot_nt(parts_ref[own], hi)
            out_ref[other, :, rows] += back[:rhs] + back[rhs:] + dot_nt(parts_ref[own, 0:rhs], lo)

        make_tile(
            kept_ref, n, spread_ref.at[other, 0], spread_ref.at[other, 1], points_ref, own, *item_shifts(code), use
        )
        out_ref[own] += total[0]

    in_turns(0, items_ref[0], make, (4, 3, 2, 1, 0))


def take_round(round_refs, rhs, parts_ref, points_ref=None, start=0):
    for side in round_refs:

        def take(at, carry, side=side, start=start):
            store_parts(parts_ref, start + at, side[at, 0:rhs])
            if points_ref is not None:
                points_ref[start + at] = side[at, rhs : rhs + 2] * UNIT
            return carry

        lax.fori_loop(0, side.shape[0], take, 0)
        start += side.shape[0]


def cross_first_kernel(
    items_ref, sum_ref, north_ref, south_ref, west_ref, east_ref, spread_ref,
    out_ref, kept_ref, parts_ref, points_ref
):
    out_ref[...] = sum_ref[...]
    take_round((north_ref, south_ref, west_ref, east_ref), sum_ref.shape[1], parts_ref, points_ref)

    def make(n):
        code = items_ref[n + 1]
        own, other = item_blocks(code)
        rhs = out_ref.shape[1]

        def use(hi, lo, rows):
            both = dot_nt(parts_ref[other], hi)
            out_ref[own, :, rows] += both[:rhs] + both[rhs:] + dot_nt(parts_ref[other, 0:rhs], lo)

        make_tile(
            kept_ref, n, spread_ref.at[own, 0], spread_ref.at[own, 1], points_ref, other, *item_shifts(code), use
        )

    in_turns(0, items_ref[0], make)


def first_share(count):
    return lax.shift_right_logical(5 * count, 3)


def near_again_kernel(items_ref, v_ref, own_ref, kept_ref, out_ref, parts_ref):
    def one(at, carry):
        store_parts(parts_ref, at, v_ref[at])
        out_ref[at] = NUGGET * v_ref[at]
        return carry

    lax.fori_loop(0, parts_ref.shape[0], one, 0, unroll=2)
    only_use(0, jnp.int32(parts_ref.shape[0]), own_ref, functools.partial(use_own, out_ref, parts_ref))
    use = functools.partial(use_pair, out_ref, parts_ref, items_ref)
    only_use(0, first_share(items_ref[0]), kept_ref, use)


def rest_again_kernel(
    near_ref, cross_ref, sum_ref, parts_ref, near_kept_ref, north_ref, south_ref, cross_kept_ref, v0_ref, v1_ref,
    out_ref, terms_ref, round_ref
):
    out_ref[...] = sum_ref[...]
    use = functools.partial(use_pair, out_ref, parts_ref, near_ref)
    only_use(first_share(near_ref[0]), near_ref[0], near_kept_ref, use)
    take_round((north_ref, south_ref), sum_ref.shape[1], round_ref)
    in_rows = cross_ref[cross_ref.shape[0] - 1]
    only_use(0, in_rows, cross_kept_ref, functools.partial(use_cross, out_ref, round_ref, cross_ref))

    def gather(at, sums):
        w0, w1 = v0_ref[at], v1_ref[at]
        return tuple(s + t for s, t in zip(sums, (w0 * w0, w0 * w1, w1 * w1)))

    zero = jnp.zeros(out_ref.shape[1:], jnp.float32)
    for n, total in enumerate(lax.fori_loop(0, out_ref.shape[0], gather, (zero,) * 3)):
        terms_ref[n] = total


def cross_again_kernel(
    items_ref, sum_ref, west_ref, east_ref, kept_ref, terms_ref, v1_ref, out_ref, moments_ref, parts_ref
):
    out_ref[...] = sum_ref[...]
    start = parts_ref.shape[0] - west_ref.shape[0] - east_ref.shape[0]
    take_round((west_ref, east_ref), sum_ref.shape[1], parts_ref, start=start)
    in_rows = items_ref[items_ref.shape[0] - 1]
    only_use(in_rows, items_ref[0], kept_ref, functools.partial(use_cross, out_ref, parts_ref, items_ref))
    zero = jnp.zeros(out_ref.shape[1:], jnp.float32)
    last = lax.fori_loop(0, out_ref.shape[0], lambda at, total: total + v1_ref[at] * out_ref[at], zero)
    sums = [terms_ref[n] for n in range(3)] + [last]
    lanes = moments_ref.shape[2]
    folded = [sum(s[:, left : left + lanes] for left in range(0, s.shape[1], lanes)) for s in sums]
    stacked = jnp.concatenate(folded, axis=0)
    line = jnp.sum(jnp.transpose(stacked), axis=0, keepdims=True)
    moments_ref[...] = jnp.broadcast_to(line[None], moments_ref.shape)


def final_kernel(moments_ref, v0_ref, v1_ref, v2_ref, solution_ref, residual_ref):
    rhs, points = v0_ref.shape[1:]
    line = moments_ref[0]
    for at in range(1, moments_ref.shape[0]):
        line = line + moments_ref[at]
    table = across_lanes(line, line.shape[1])
    m00, m01, m11, m12 = (table[k * rhs : (k + 1) * rhs] for k in range(4))
    a = m00 / m01
    norm = m00 - 2.0 * a * m01 + a * a * m11
    grow = 1.0 + norm / m00
    step = norm / (grow * (grow * m01 - 2.0 * a * m11) + a * a * m12)
    first = jnp.concatenate([a + step * grow] * (points // line.shape[1]), axis=1)
    second = jnp.concatenate([step * a] * (points // line.shape[1]), axis=1)

    def one(at, carry):
        w0, w1, w2 = v0_ref[at], v1_ref[at], v2_ref[at]
        solution_ref[at] = first * w0 - second * w1
        residual_ref[at] = w0 - first * w1 + second * w2
        return carry

    lax.fori_loop(0, v0_ref.shape[0], one, 0)


def swapped(first, last, axis):
    count = lax.axis_size(axis)
    even = lax.rem(lax.axis_index(axis), 2) == 0
    swap_up = [(i, i ^ 1) for i in range(count) if i ^ 1 < count]
    swap_down = [(i, ((i + 1) ^ 1) - 1) for i in range(count) if 0 <= ((i + 1) ^ 1) - 1 < count]
    got_up = lax.ppermute(jnp.where(even, last, first), axis, swap_up)
    got_down = lax.ppermute(jnp.where(even, first, last), axis, swap_down)
    return jnp.where(even, got_down, got_up), jnp.where(even, got_up, got_down)


def on_device(kernel, outputs, inputs, scratch=(), listed=False, products=0, made=0, where=pltpu.VMEM):
    vmem = pl.BlockSpec(memory_space=pltpu.VMEM)
    smem = pl.BlockSpec(memory_space=pltpu.SMEM)
    source = pl.BlockSpec(memory_space=where)
    return pl.pallas_call(
        kernel,
        out_shape=tuple(outputs),
        in_specs=[smem if listed and x.dtype == jnp.int32 else source for x in inputs],
        out_specs=tuple(smem if out.dtype == jnp.int32 else vmem for out in outputs),
        scratch_shapes=list(scratch),
        compiler_params=pltpu.CompilerParams(vmem_limit_bytes=VMEM_LIMIT),
        cost_estimate=pl.CostEstimate(
            flops=products, transcendentals=made, bytes_accessed=sum(4 * x.size for x in inputs)
        ),
        name=kernel.__name__,
    )(*inputs)


def tiles(count, points):
    return jax.ShapeDtypeStruct((count, 2, points, points), jnp.bfloat16)


def per_device(right_side, coords, pair_list):
    pair_list = jnp.transpose(pair_list, (1, 2, 0))
    rows, cols, rhs, points = right_side.shape
    blocks = rows * cols
    devices = lax.axis_size("region") * lax.axis_size("tile")
    lanes = 128
    f32, bf16, i32 = jnp.float32, jnp.bfloat16, jnp.int32
    array = jax.ShapeDtypeStruct
    halo = 2 * rows + 2 * (cols + 2)
    near_count = len(inner_candidates(rows, cols))
    cross_count = sum(len(part) for part in cross_candidates(rows, cols))
    field = array((blocks, rhs, points), f32)
    column = array((rows, rhs + 2, points), f32)
    parts_round = pltpu.VMEM((halo, 2 * rhs, points), bf16)
    each = 6 * rhs * points * points

    def columns_round(first, last, north, south):
        first = jnp.concatenate([north[:1], first, south[:1]], axis=0)
        last = jnp.concatenate([north[cols - 1 :], last, south[cols - 1 :]], axis=0)
        return swapped(first, last, "tile")

    fetched = (
        column, column, array((2, cols, rhs + 2, points), f32), field, array((blocks, 2, points), f32),
        array(pair_list.shape, i32),
    )
    first, last, edges, w0, stations, pairs = on_device(
        pack_kernel, fetched,
        tuple(pltpu.with_memory_space_constraint(x, pltpu.HBM) for x in (right_side, coords, pair_list)),
        (pltpu.SemaphoreType.DMA((2 * rows + 1,)),), where=pltpu.HBM,
    )
    north, south = swapped(edges[0], edges[1], "region")
    parts_field = array((blocks, 2 * rhs, points), bf16)
    near_items, cross_items, part, own_tiles, parts, own_points, spread = on_device(
        own_first_kernel,
        (array((near_count + 3,), i32), array((cross_count + 3,), i32), field, tiles(blocks, points), parts_field,
         array((blocks, 2, points), f32), array((blocks, 2, points, lanes), f32)),
        (pairs, w0, stations), listed=True, products=blocks * each, made=blocks * 2 * points * points,
    )
    north, south, part = lax.optimization_barrier((north, south, part))
    west, east = columns_round(first, last, north, south)
    part, near_tiles = on_device(
        inner_first_kernel, (field, tiles(near_count + 2, points)), (near_items, part, parts, own_points, spread),
        (), True, near_count * each, near_count * 2 * points * points,
    )
    w1, cross_tiles = on_device(
        cross_first_kernel, (field, tiles(cross_count + 2, points)),
        (cross_items, part, north, south, west, east, spread),
        (parts_round, pltpu.VMEM((halo, 2, points), f32)), True,
        cross_count * each, cross_count * 2 * points * points,
    )
    w1_grid = w1.reshape(right_side.shape)
    north, south = swapped(w1_grid[0], w1_grid[rows - 1], "region")
    part, parts = on_device(
        near_again_kernel, (field, parts_field), (near_items, w1, own_tiles, near_tiles), (), True,
        (blocks + near_count) * each,
    )
    north, south, part = lax.optimization_barrier((north, south, part))
    west, east = columns_round(w1_grid[:, 0], w1_grid[:, cols - 1], north, south)
    part, terms = on_device(
        rest_again_kernel, (field, array((3, rhs, points), f32)),
        (near_items, cross_items, part, parts, near_tiles, north, south, cross_tiles, w0, w1), (parts_round,), True,
        near_count * each,
    )
    w2, moments = on_device(
        cross_again_kernel, (field, array((devices, 1, 4 * rhs), f32)),
        (cross_items, part, west, east, cross_tiles, terms, w1), (parts_round,), True, cross_count * each,
    )
    moments = lax.all_to_all(moments, ("region", "tile"), 0, 0)
    solution, residual = on_device(final_kernel, (field, field), (moments, w0, w1, w2))
    return solution.reshape(right_side.shape), residual.reshape(right_side.shape)


def solution(mesh):
    placed = (
        P("region", "tile", None, None),
        P("region", "tile", None, None),
        P(None, "region", "tile"),
    )
    return jax.shard_map(
        per_device,
        mesh=mesh,
        in_specs=placed,
        out_specs=(P("region", "tile", None, None), P("region", "tile", None, None)),
        check_vma=False,
    )
```
